32 devices in a mesh: dp: 8 (over z, x), tensor: 4 (over y, core).
Axes of the slice: x: 2, y: 2, z: 4, core: 2. Of those that a mesh axis runs over, the one named last changes fastest.
Arguments:
- residual: float32 [4096, 1024], P(('dp', 'tensor')), may hold values from -6 to 6
- segments: int32 [8, 512], P('dp'), may hold values from 0 to 10, never falling along the last dimension, each value on 1 to 256 neighbouring positions
- norm_gain: float32 [1024], replicated, may hold values from 0.5 to 1.5
- in_gate: bfloat16 [1024, 2048], P('dp', 'tensor'), may hold values from -0.1875 to 0.1875
- in_value: bfloat16 [1024, 2048], P('dp', 'tensor'), may hold values from -0.1875 to 0.1875
- in_step: bfloat16 [1024, 32], P('dp', 'tensor'), may hold values from -0.1875 to 0.1875
- in_state: bfloat16 [1024, 256], P('dp'), may hold values from -0.1875 to 0.1875
- kernel_value: float32 [4, 2048], P(None, 'tensor'), may hold values from -3 to 3
- bias_value: float32 [2048], P('tensor'), may hold values from -1.5 to 1.5
- kernel_state: float32 [4, 256], replicated, may hold values from -3 to 3
- bias_state: float32 [256], replicated, may hold values from -1.5 to 1.5
- step_bias: float32 [32], P('tensor'), may hold values from -5 to -1
- log_decay: float32 [32], P('tensor'), may hold values from -1 to 2.5
- skip_gain: float32 [32], P('tensor'), may hold values from 0.5 to 1.5
- gate_gain: float32 [2048], P('tensor'), may hold values from 0.5 to 1.5
- out_proj: bfloat16 [1024, 2048], P('dp', 'tensor'), may hold values from -0.125 to 0.125
- cotangent: float32 [4096, 1024], P(('dp', 'tensor')), may hold values from -6 to 6
Outputs:
- layer_out: float32 [4096, 1024], P(('dp', 'tensor'))
- grad_input: float32 [4096, 1024], P(('dp', 'tensor'))
- grad_norm_gain: float32 [1024], replicated
- grad_in_gate: float32 [1024, 2048], P('dp', 'tensor')
- grad_in_value: float32 [1024, 2048], P('dp', 'tensor')
- grad_in_step: float32 [1024, 32], P('dp', 'tensor')
- grad_in_state: float32 [1024, 256], P('dp', 'tensor')
- grad_kernel_value: float32 [4, 2048], P(None, 'tensor')
- grad_bias_value: float32 [2048], P('tensor')
- grad_kernel_state: float32 [4, 256], replicated
- grad_bias_state: float32 [256], replicated
- grad_step_bias: float32 [32], P('tensor')
- grad_log_decay: float32 [32], P('tensor')
- grad_skip_gain: float32 [32], P('tensor')
- grad_gate_gain: float32 [2048], P('tensor')
- grad_out_proj: float32 [1024, 2048], P('dp', 'tensor')
The draws below stay inside these ranges and needn't reach their ends.
Inputs may be any that keep to these rules, and one draw needn't show every extreme that they name: `segments`: segment numbers start at 0 in each packed row and never fall along it; one segment of each row holds exactly 256 tokens, none more.
All inputs are finite; a program needn't handle non-finite values.
Results may differ from the reference program's by a relative error of at most 0.0083.
Values may be sent and summed in bfloat16 or wider, within the bound.
A program may use at most 128 MiB of HBM per device.

```python
import math
from functools import partial
import jax
import jax.numpy as jnp
import numpy as np
from jax import lax

D = 1024
HEADS = 32
NSTATE = 128
CONV = 4
BLOCK = 256
SEQ = 512
INNER = 2048
TOKENS = 4096
N_DP = 8


def block_levels(own_key, extent, shards, least, largest):
    factor_of, own = 1.0, jax.random.fold_in(own_key, 6)
    for dim, blocks in shards:
        draws = jnp.exp(jax.random.uniform(jax.random.fold_in(own, dim), (blocks,), jnp.float32, least / len(shards), largest / len(shards)))
        factor_of = factor_of * jnp.repeat(draws, extent[dim] // blocks).reshape([-1 if axis == dim else 1 for axis in range(len(extent))])
    return factor_of


def length_profile(number_of, total, bound, slope):
    weights = [(1 << 20) // math.isqrt(rank ** slope) + 1 for rank in range(2, number_of + 1)]
    surplus, counts = total - bound - (number_of - 1), [1] * (number_of - 1)
    while surplus > 0:
        candidates = [i for i in range(number_of - 1) if counts[i] < bound]
        mass, remaining = sum([weights[i] for i in candidates]), surplus
        for i in candidates:
            addition = min(bound - counts[i], max(1, remaining * weights[i] // mass), surplus)
            counts[i] = counts[i] + addition
            surplus = surplus - addition
    return np.array([bound] + counts)


def ragged(key, amount, total, bound, skew):
    if amount == 2:
        one = jax.random.randint(key, (), max(1, total - bound), min(bound, total - 1) + 1)
        return jnp.stack([one, total - one])
    tallies = jnp.asarray(length_profile(amount, total, bound, skew), jnp.int32)
    twos = (amount - 1) // 2
    source_of, receiver = tallies[1:1 + 2 * twos:2], tallies[2:2 + 2 * twos:2]
    margin = jnp.minimum(source_of - 1, bound - receiver)
    moved = jax.random.randint(jax.random.fold_in(key, 1), (twos,), 0, 1 << 20) % (margin + 1)
    tallies = tallies.at[1:1 + 2 * twos:2].set(source_of - moved).at[2:2 + 2 * twos:2].set(receiver + moved)
    return tallies[jax.random.permutation(jax.random.fold_in(key, 2), amount)]


def bell_draw(own_key, extent, scale, most, shards=(), kind=jnp.bfloat16):
    array = scale * jax.random.normal(own_key, extent, jnp.float32)
    if shards:
        array = array * block_levels(own_key, extent, shards, -0.22, 0.18)
    return jnp.clip(array, -most, most).astype(kind)


def setup_inputs(seed: int = 0) -> dict:
    seeds = jax.random.split(jax.random.key(seed), 18)
    residual = bell_draw(seeds[0], (TOKENS, D), 1.0, 6.0, ((0, 32),), jnp.float32)
    segments = jax.vmap(lambda own: jnp.searchsorted(jnp.cumsum(ragged(own, SEQ // 64 + 3, SEQ, SEQ // 2, 1)), jnp.arange(SEQ), side="right"))(jax.random.split(seeds[1], N_DP)).reshape((N_DP, SEQ)).astype(jnp.int32)
    norm_gain = jnp.clip(1.0 + 0.1 * jax.random.normal(seeds[2], (D,), jnp.float32), 0.5, 1.5)
    in_gate = bell_draw(seeds[3], (D, INNER), D ** -0.5, 0.1875, ((0, 8), (1, 4)))
    in_value = bell_draw(seeds[4], (D, INNER), D ** -0.5, 0.1875, ((0, 8), (1, 4)))
    in_step = bell_draw(seeds[5], (D, HEADS), D ** -0.5, 0.1875, ((0, 8), (1, 4)))
    in_state = bell_draw(seeds[6], (D, 2 * NSTATE), D ** -0.5, 0.1875, ((0, 8),))
    kernel_value = bell_draw(seeds[7], (CONV, INNER), CONV ** -0.5, 3.0, ((1, 4),), jnp.float32)
    bias_value = bell_draw(seeds[8], (INNER,), 0.3, 1.5, ((0, 4),), jnp.float32)
    kernel_state = bell_draw(seeds[9], (CONV, 2 * NSTATE), CONV ** -0.5, 3.0, (), jnp.float32)
    bias_state = bell_draw(seeds[10], (2 * NSTATE,), 0.3, 1.5, (), jnp.float32)
    step_bias = jnp.clip(-5.0 + 4.0 * jax.random.uniform(seeds[11], (HEADS,), jnp.float32) ** block_levels(seeds[11], (HEADS,), ((0, 4),), -0.2, 0.2), -5.0, -1.0)
    log_decay = jnp.clip(-1.0 + 3.5 * jax.random.uniform(seeds[12], (HEADS,), jnp.float32) ** block_levels(seeds[12], (HEADS,), ((0, 4),), -0.2, 0.2), -1.0, 2.5)
    skip_gain = jnp.clip(0.5 + 1.0 * jax.random.uniform(seeds[13], (HEADS,), jnp.float32) ** block_levels(seeds[13], (HEADS,), ((0, 4),), -0.2, 0.2), 0.5, 1.5)
    gate_gain = jnp.clip(1.0 + 0.1 * jax.random.normal(seeds[14], (INNER,), jnp.float32), 0.5, 1.5)
    out_proj = bell_draw(seeds[15], (D, INNER), INNER ** -0.5, 0.125, ((0, 8), (1, 4)))
    cotangent = bell_draw(seeds[16], (TOKENS, D), 1.0, 6.0, ((0, 32),), jnp.float32)
    return {"residual": residual, "segments": segments, "norm_gain": norm_gain, "in_gate": in_gate, "in_value": in_value, "in_step": in_step, "in_state": in_state, "kernel_value": kernel_value, "bias_value": bias_value, "kernel_state": kernel_state, "bias_state": bias_state, "step_bias": step_bias, "log_decay": log_decay, "skip_gain": skip_gain, "gate_gain": gate_gain, "out_proj": out_proj, "cotangent": cotangent}


epsilon = 1e-05
precise = lax.Precision.HIGHEST

def pre_norm(row_block, gain):
    return row_block * lax.rsqrt(lax.optimization_barrier(jnp.mean(row_block * row_block, axis=1, keepdims=True)) + epsilon) * gain

def gated_norm(mixer_out, gate_raw, gain):
    gated_vals = mixer_out * jax.nn.silu(gate_raw)
    return gated_vals * lax.rsqrt(lax.optimization_barrier(jnp.mean(gated_vals * gated_vals, axis=1, keepdims=True)) + epsilon) * gain

def conv_silu(values, kernel, shift_bias, seg_ids):
    taps = kernel.shape[0]
    length = values.shape[0]
    padded = jnp.pad(values, ((taps - 1, 0), (0, 0)))
    seg_pad = jnp.concatenate([jnp.full((taps - 1,), -1, jnp.int32), seg_ids.astype(jnp.int32)])
    summed = jnp.zeros_like(values) + shift_bias
    for offset in range(taps):
        begin_at = taps - 1 - offset
        shifted = padded[begin_at:begin_at + length]
        same_doc = (seg_pad[begin_at:begin_at + length] == seg_ids).astype(values.dtype)
        summed = summed + kernel[offset] * shifted * same_doc[:, None]
    return jax.nn.silu(summed)

def ssd_mixer(values, write_vec, read_vec, step_raw, step_bias, log_decay, skip_gain, seg_ids):
    length, channels = values.shape
    head_count = step_raw.shape[1]
    head_size = channels // head_count
    states = write_vec.shape[1]
    blocks = length // BLOCK
    step_size = jax.nn.softplus(step_raw + step_bias)
    log_keep = -jnp.exp(log_decay) * step_size
    val_blocks = values.reshape(blocks, BLOCK, head_count, head_size)
    write_blocks = write_vec.reshape(blocks, BLOCK, states)
    read_blocks = read_vec.reshape(blocks, BLOCK, states)
    step_blocks = step_size.reshape(blocks, BLOCK, head_count)
    keep_blocks = log_keep.reshape(blocks, BLOCK, head_count)
    seg_blocks = seg_ids.astype(jnp.int32).reshape(blocks, BLOCK)
    carried = jnp.concatenate([jnp.full((1,), -1, jnp.int32), seg_blocks[:-1, -1]])
    row_pos = lax.broadcasted_iota(jnp.int32, (BLOCK, BLOCK), 0)
    col_pos = lax.broadcasted_iota(jnp.int32, (BLOCK, BLOCK), 1)

    def advance(carry_state, block_item):
        val_b, write_b, read_b, step_b, keep_b, seg_b, prior_seg = block_item
        cumulative = jnp.cumsum(keep_b, axis=0).T
        allowed = ((seg_b[:, None] == seg_b[None, :]) & (col_pos <= row_pos))[None]
        spread = cumulative[:, :, None] - cumulative[:, None, :]
        decay_mask = jnp.where(allowed, jnp.exp(jnp.where(allowed, spread, 0.0)), 0.0)
        scores = jnp.dot(read_b, write_b.T, precision=precise)
        mixing = scores[None] * decay_mask * step_b.T[:, None, :]
        inner_part = jnp.einsum('hls,shp->lhp', mixing, val_b, precision=precise)
        keep_prior = (seg_b == prior_seg).astype(values.dtype)
        from_state = jnp.einsum('ln,hpn->lhp', read_b, carry_state, precision=precise)
        carry_scale = jnp.exp(cumulative).T * keep_prior[:, None]
        outer_part = from_state * carry_scale[:, :, None]
        last_seg = seg_b[-1]
        tail_weight = jnp.exp(cumulative[:, -1][None, :] - cumulative.T) * step_b * (seg_b == last_seg).astype(values.dtype)[:, None]
        weighted = val_b * tail_weight[:, :, None]
        fresh_state = jnp.einsum('shp,sn->hpn', weighted, write_b, precision=precise)
        kept_scale = jnp.exp(cumulative[:, -1]) * (last_seg == prior_seg).astype(values.dtype)
        new_state = carry_state * kept_scale[:, None, None] + fresh_state
        return (new_state, inner_part + outer_part)
    initial = jnp.zeros((head_count, head_size, states), values.dtype)
    unused_state, outputs = lax.scan(advance, initial, (val_blocks, write_blocks, read_blocks, step_blocks, keep_blocks, seg_blocks, carried))
    return outputs.reshape(length, channels) + values * jnp.repeat(skip_gain, head_size)[None, :]

def reference(residual, segments, norm_gain, in_gate, in_value, in_step, in_state, kernel_value, bias_value, kernel_state, bias_state, step_bias, log_decay, skip_gain, gate_gain, out_proj, cotangent):
    in_cat = jnp.concatenate([in_gate, in_value, in_step, in_state], axis=1)
    rows_all = residual.reshape(N_DP, SEQ, D)
    cot_all = cotangent.reshape(N_DP, SEQ, D)
    split_one = 2 * INNER
    split_two = 2 * INNER + HEADS

    def one_row(totals, row_item):
        row_block, seg_ids, cot_block = row_item
        normed32, norm_pull = jax.vjp(pre_norm, row_block, norm_gain)
        normed = normed32.astype(jnp.bfloat16)
        projected = jnp.dot(normed, in_cat, preferred_element_type=jnp.float32)
        gate_raw = projected[:, :INNER]
        value_raw = projected[:, INNER:split_one]
        step_raw = projected[:, split_one:split_two]
        state_raw = projected[:, split_two:]
        conv_value, value_pull = jax.vjp(partial(conv_silu, seg_ids=seg_ids), value_raw, kernel_value, bias_value)
        conv_state, state_pull = jax.vjp(partial(conv_silu, seg_ids=seg_ids), state_raw, kernel_state, bias_state)
        mixer_out, mixer_pull = jax.vjp(partial(ssd_mixer, seg_ids=seg_ids), conv_value, conv_state[:, :NSTATE], conv_state[:, NSTATE:], step_raw, step_bias, log_decay, skip_gain)
        gate_out, gate_pull = jax.vjp(gated_norm, mixer_out, gate_raw, gate_gain)
        gate_normed = gate_out.astype(jnp.bfloat16)
        layer_rows = row_block + lax.dot_general(gate_normed, out_proj, (((1,), (1,)), ((), ())), preferred_element_type=jnp.float32)
        cot_half = cot_block.astype(jnp.bfloat16)
        grad_gate_normed = jnp.dot(cot_half, out_proj, preferred_element_type=jnp.float32)
        grad_out = lax.dot_general(cot_half, gate_normed, (((0,), (0,)), ((), ())), preferred_element_type=jnp.float32)
        grad_mixer_out, grad_gate_raw, grad_gate_gain = gate_pull(grad_gate_normed)
        grad_conv_value, grad_write, grad_read, grad_step_raw, grad_step_bias, grad_log_decay, grad_skip = mixer_pull(grad_mixer_out)
        grad_value_raw, grad_kernel_value, grad_bias_value = value_pull(grad_conv_value)
        grad_state_raw, grad_kernel_state, grad_bias_state = state_pull(jnp.concatenate([grad_write, grad_read], axis=1))
        grad_projected = jnp.concatenate([grad_gate_raw, grad_value_raw, grad_step_raw, grad_state_raw], axis=1).astype(jnp.bfloat16)
        grad_normed = lax.dot_general(grad_projected, in_cat, (((1,), (1,)), ((), ())), preferred_element_type=jnp.float32)
        grad_weights = lax.dot_general(normed, grad_projected, (((0,), (0,)), ((), ())), preferred_element_type=jnp.float32)
        grad_rows, grad_norm_part = norm_pull(grad_normed)
        grad_in_rows = cot_block + grad_rows
        updates = (grad_norm_part, grad_weights, grad_kernel_value, grad_bias_value, grad_kernel_state, grad_bias_state, grad_step_bias, grad_log_decay, grad_skip, grad_gate_gain, grad_out)
        totals = jax.tree.map(lambda running, update_term: running + update_term, totals, updates)
        return (totals, (layer_rows, grad_in_rows))
    initial = (jnp.zeros((D,), jnp.float32), jnp.zeros((D, 2 * INNER + HEADS + 2 * NSTATE), jnp.float32), jnp.zeros((CONV, INNER), jnp.float32), jnp.zeros((INNER,), jnp.float32), jnp.zeros((CONV, 2 * NSTATE), jnp.float32), jnp.zeros((2 * NSTATE,), jnp.float32), jnp.zeros((HEADS,), jnp.float32), jnp.zeros((HEADS,), jnp.float32), jnp.zeros((HEADS,), jnp.float32), jnp.zeros((INNER,), jnp.float32), jnp.zeros((D, INNER), jnp.float32))
    totals, outputs = lax.scan(one_row, initial, (rows_all, segments, cot_all))
    layer_out = outputs[0].reshape(TOKENS, D)
    grad_input = outputs[1].reshape(TOKENS, D)
    grad_weights = totals[1]
    return (layer_out, grad_input, totals[0], grad_weights[:, :INNER], grad_weights[:, INNER:split_one], grad_weights[:, split_one:split_two], grad_weights[:, split_two:], totals[2], totals[3], totals[4], totals[5], totals[6], totals[7], totals[8], totals[9], totals[10])
```

```python
from functools import partial
from types import SimpleNamespace

import jax
import jax.numpy as jnp
from jax import lax
from jax.experimental import pallas as pl
from jax.experimental.pallas import tpu as pltpu
from jax.sharding import PartitionSpec as P

epsilon = 1e-05
precise = lax.Precision.HIGHEST
MESH = pl.DeviceIdType.MESH
VM = pl.BlockSpec(memory_space=pltpu.VMEM)
F32 = jnp.float32
BF16 = jnp.bfloat16
LONGEST = 256
LANES = 128
CHUNK = 32
LOG2E = 1.4426950408889634
VMEM_BYTES = 61 * 1024 * 1024


def loop(begin, end, step):
    def body(k, carry):
        step(k)
        return carry

    lax.fori_loop(begin, end, body, 0)


def dot(a, b, ca=1, cb=0, precision=None):
    return lax.dot_general(
        a, b, (((ca,), (cb,)), ((), ())), preferred_element_type=F32, precision=precision
    )


def push(src, dst, ssem, rsem, d, t):
    return pltpu.make_async_remote_copy(
        src_ref=src,
        dst_ref=dst,
        send_sem=ssem,
        recv_sem=rsem,
        device_id=(d, t),
        device_id_type=MESH,
    )


def fold(x):
    return jnp.sum(x.reshape(x.shape[0] // 8, 8, x.shape[1]), axis=0)


def three(x):
    hi = x.astype(BF16)
    rest = x - hi.astype(F32)
    mid = rest.astype(BF16)
    low = (rest - mid.astype(F32)).astype(BF16)
    return hi, mid, low


class Place:
    def __init__(self, n, t_size):
        self.n = n
        self.t_size = t_size
        self.d = lax.axis_index("dp")
        self.t = lax.axis_index("tensor")
        self.hi = self.d // 2
        self.lo = lax.rem(self.d, 2)
        self.line = n // 2
        self.mate = self.d + 1 - 2 * self.lo
        self.has_up = self.hi < self.line - 1
        self.has_down = self.hi > 0
        self.near_low = self.hi < self.line // 2
        self.chips = t_size // 2
        self.y = self.t // 2
        self.core = lax.rem(self.t, 2)
        self.twin = self.t + 1 - 2 * self.core

    def others(self):
        return [lax.rem(self.t + k, self.t_size) for k in range(1, self.t_size)]

    def across(self, core):
        return [
            lax.rem(self.y + k, self.chips) * 2 + core for k in range(1, self.chips)
        ]


class Gather:
    def __init__(self, p, src, buf, sems, mate_first):
        self.p, self.src, self.buf, self.mate_first = p, src, buf, mate_first
        self.sx, self.su, self.sd, self.r = sems

    def own(self, sems, to):
        p = self.p
        return push(self.src, self.buf.at[p.d], sems.at[p.d], self.r.at[p.d], to, p.t)

    def relay(self, q, sems, to):
        return push(
            self.buf.at[q], self.buf.at[q], sems.at[q], self.r.at[q], to, self.p.t
        )

    def arrive(self, q):
        self.relay(q, self.sx, self.p.mate).wait_recv()

    def open(self):
        p = self.p
        if self.mate_first:
            self.own(self.sx, p.mate).start()

        @pl.when(p.has_up)
        def _():
            self.own(self.su, p.d + 2).start()

        @pl.when(p.has_down)
        def _():
            self.own(self.sd, p.d - 2).start()

        if not self.mate_first:
            self.own(self.sx, p.mate).start()

    def open_mate(self):
        p = self.p
        self.arrive(p.mate)

        @pl.when(p.has_up)
        def _():
            self.relay(p.mate, self.su, p.d + 2).start()

        @pl.when(p.has_down)
        def _():
            self.relay(p.mate, self.sd, p.d - 2).start()

    def step(self, k):
        p = self.p
        for below in (True, False):
            far = p.d - 2 * k if below else p.d + 2 * k
            far_mate = p.mate - 2 * k if below else p.mate + 2 * k
            exists = p.hi >= k if below else p.hi + k < p.line
            onward = jnp.logical_and(exists, p.has_up if below else p.has_down)
            sems = self.su if below else self.sd
            to = p.d + 2 if below else p.d - 2
            for q in (far, far_mate) if self.mate_first else (far,):

                @pl.when(exists)
                def _():
                    self.arrive(q)
                    if not self.mate_first:
                        self.relay(q, self.sx, p.mate).start()

                @pl.when(onward)
                def _():
                    self.relay(q, sems, to).start()

    def finish(self):
        p = self.p
        if not self.mate_first:
            loop(0, p.line, lambda k: self.arrive(2 * k + 1 - p.lo))

    def drain(self):
        p = self.p
        if self.mate_first:
            self.own(self.sx, p.mate).wait_send()

        def body(k):
            ours = (2 * k, 2 * k + 1) if self.mate_first else (2 * k + p.lo,)
            if not self.mate_first:
                self.relay(ours[0], self.sx, p.mate).wait_send()

            @pl.when(jnp.logical_and(p.has_up, p.hi >= k))
            def _():
                for q in ours:
                    self.relay(q, self.su, p.mate).wait_send()

            @pl.when(jnp.logical_and(p.has_down, p.hi <= k))
            def _():
                for q in ours:
                    self.relay(q, self.sd, p.mate).wait_send()

        loop(0, p.line, body)


class Reduce:
    def __init__(self, p, w, bufs, sems, line_first):
        self.p, self.w, self.line_first = p, w, line_first
        self.bu, self.ru, self.bd, self.rd, self.bx, self.rx = bufs
        self.su, self.qu, self.sd, self.qd, self.sx, self.qx = sems

    def send_x(self, k):
        p = self.p
        return push(
            self.w.at[2 * k + 1 - p.lo], self.rx.at[k], self.sx.at[k], self.qx.at[k], p.mate, p.t
        )

    def hop(self, up, k, to):
        buf, got, ss, qs = (
            (self.bu, self.ru, self.su, self.qu)
            if up
            else (self.bd, self.rd, self.sd, self.qd)
        )
        return push(buf.at[k], got.at[k], ss.at[k], qs.at[k], to, self.p.t)

    def open(self):
        p = self.p
        if self.line_first:
            return

        def pair(k):
            self.send_x(p.line - 1 - k).start()
            self.send_x(k).start()

        loop(0, p.line // 2, pair)
        if p.line % 2:
            self.send_x(p.line // 2).start()

    def mine(self, k):
        if self.line_first:
            return self.w[pl.ds(2 * k, 2)].astype(F32)
        return self.w[2 * k + self.p.lo].astype(F32) + self.rx[k].astype(F32)

    def chain(self, k, up):
        p = self.p
        has_prev = p.has_down if up else p.has_up
        buf, got = (self.bu, self.ru) if up else (self.bd, self.rd)
        to = p.d + 2 if up else p.d - 2

        @pl.when(k > p.hi if up else k < p.hi)
        def _():
            @pl.when(has_prev)
            def _():
                self.hop(up, k, to).wait_recv()
                buf[k] = (self.mine(k) + got[k].astype(F32)).astype(BF16)

            @pl.when(jnp.logical_not(has_prev))
            def _():
                buf[k] = self.mine(k).astype(BF16)

            self.hop(up, k, to).start()

    def got_x(self, k):
        self.send_x(k).wait_recv()

    def walk(self, k):
        p = self.p
        if not self.line_first:

            @pl.when(2 * k < p.line - 1)
            def _():
                self.got_x(p.line - 1 - k)
                self.got_x(k)

            if p.line % 2:

                @pl.when(2 * k == p.line - 1)
                def _():
                    self.got_x(k)

        @pl.when(p.near_low)
        def _():
            self.chain(p.line - 1 - k, True)
            self.chain(k, False)

        @pl.when(jnp.logical_not(p.near_low))
        def _():
            self.chain(k, False)
            self.chain(p.line - 1 - k, True)

    def settle(self, out):
        p = self.p
        if self.line_first:
            out[...] = self.w[p.d].astype(F32)
            self.bx[...] = self.w[p.mate]
        else:
            if p.line == 1:
                self.got_x(0)
            out[...] = self.mine(p.hi)
        for up, has in ((True, p.has_down), (False, p.has_up)):
            got = self.ru if up else self.rd

            @pl.when(has)
            def _():
                self.hop(up, p.hi, p.d).wait_recv()
                if self.line_first:
                    out[...] = out[...] + got[p.hi, p.lo].astype(F32)
                    self.bx[...] = (
                        self.bx[...].astype(F32) + got[p.hi, 1 - p.lo].astype(F32)
                    ).astype(BF16)
                else:
                    out[...] = out[...] + got[p.hi].astype(F32)

        if self.line_first:
            self.send_last().start()

    def send_last(self):
        p = self.p
        return push(self.bx, self.rx, self.sx.at[0], self.qx.at[0], p.mate, p.t)

    def settle_last(self, out):
        self.send_last().wait()
        out[...] = out[...] + self.rx[...].astype(F32)

    def drain(self):
        p = self.p

        def body(k):
            if not self.line_first:
                self.send_x(k).wait_send()

            @pl.when(k > p.hi)
            def _():
                self.hop(True, k, p.d).wait_send()

            @pl.when(k < p.hi)
            def _():
                self.hop(False, k, p.d).wait_send()

        loop(0, p.line, body)


class Swap:
    def __init__(self, p, src, buf, sems, scatter):
        self.p, self.src, self.buf, self.scatter = p, src, buf, scatter
        self.ss, self.rs = sems

    def send(self, slot, other):
        src = self.src.at[other] if self.scatter else self.src
        return push(src, self.buf.at[slot], self.ss.at[other], self.rs.at[slot], self.p.d, other)

    def open(self):
        for other in self.p.others():
            self.send(self.p.t, other).start()

    def wait(self):
        for other in self.p.others():
            self.send(other, other).wait()

    def own(self):
        return self.src[self.p.t] if self.scatter else self.src[...]

    def total(self):
        self.wait()
        out = self.own().astype(F32)
        for other in self.p.others():
            out = out + self.buf[other].astype(F32)
        return out


class Spread:
    def __init__(self, p, src, buf, sems):
        self.p, self.src, self.buf = p, src, buf
        self.ss, self.s2, self.rs = sems

    def send(self, other):
        p = self.p
        return push(self.src, self.buf.at[p.t], self.ss.at[other], self.rs.at[p.t], p.d, other)

    def relay(self, q):
        p = self.p
        return push(self.buf.at[q], self.buf.at[q], self.s2.at[q], self.rs.at[q], p.d, p.twin)

    def open(self):
        p = self.p
        for other in p.across(p.core):
            self.send(other).start()
        self.send(p.twin).start()

    def pass_on(self):
        p = self.p
        for q in p.across(p.core):
            self.relay(q).wait_recv()
            self.relay(q).start()

    def finish(self):
        p = self.p
        for q in [p.twin] + p.across(1 - p.core):
            self.relay(q).wait_recv()

    def drain(self):
        p = self.p
        for other in p.across(p.core) + [p.twin]:
            self.send(other).wait_send()
        for q in p.across(p.core):
            self.relay(q).wait_send()


class Everyone:
    def __init__(self, p, src, buf, sems):
        self.p, self.src, self.buf = p, src, buf
        self.ss, self.rs = sems

    def send(self, slot, q):
        return push(self.src, self.buf.at[slot], self.ss.at[q], self.rs.at[slot], q, self.p.t)

    def open(self):
        p = self.p
        loop(1, p.n, lambda k: self.send(p.d, lax.rem(p.d + k, p.n)).start())
        self.buf[p.d] = self.src[...]

    def total(self):
        p = self.p

        def body(k):
            q = lax.rem(p.d + k, p.n)
            self.send(q, q).wait()

        loop(1, p.n, body)
        return jnp.sum(self.buf[...], axis=0)


def conv_forward(raw, taps, bias, masks, tokens, emit):
    count, cols = taps.shape

    def chunk(i):
        base = pl.multiple_of(i * CHUNK, CHUNK)
        for j in range(cols // LANES):
            ls = slice(j * LANES, (j + 1) * LANES)
            blk = raw[pl.ds(base, CHUNK + 8), ls]
            pre = bias[:, ls] + taps[0:1, ls] * blk[8:]
            for k in range(1, count):
                pre += taps[k : k + 1, ls] * (
                    blk[8 - k : 8 - k + CHUNK] * masks[k - 1, pl.ds(base, CHUNK), :]
                )
            sig = jax.nn.sigmoid(pre)
            emit(base, j, pre * sig, sig * (1.0 + pre * (1.0 - sig)))

    loop(0, tokens // CHUNK, chunk)


def conv_backward(dpre, raw, taps, masks, sums, tokens, emit):
    count, cols = taps.shape
    sums[...] = jnp.zeros_like(sums)

    def chunk(i):
        base = pl.multiple_of(i * CHUNK, CHUNK)
        for j in range(cols // LANES):
            ls = slice(j * LANES, (j + 1) * LANES)
            d_blk = dpre[pl.ds(base, CHUNK + 8), ls]
            blk = raw[pl.ds(base, CHUNK + 8), ls]
            grad = taps[0:1, ls] * d_blk[:CHUNK]
            sums[count, :, ls] += fold(d_blk[:CHUNK])
            sums[0, :, ls] += fold(d_blk[:CHUNK] * blk[8:])
            for k in range(1, count):
                d_k = d_blk * masks[k - 1, pl.ds(base, CHUNK + 8), :]
                grad += taps[k : k + 1, ls] * d_k[k : k + CHUNK]
                sums[k, :, ls] += fold(d_k[:CHUNK] * blk[8 - k : 8 - k + CHUNK])
            emit(base, j, grad)

    loop(0, tokens // CHUNK, chunk)


def kernel(c, *refs):
    s = SimpleNamespace(**dict(zip(c.names, refs)))
    p = Place(c.n, c.t_size)
    n, t_size, line = c.n, c.t_size, c.n // 2
    tokens, model, width, heads, states, rows = (
        c.tokens,
        c.model,
        c.width,
        c.heads,
        c.states,
        c.rows,
    )
    sw, hw, part = c.sw, c.hw, states // 2
    own_rows = tokens // t_size
    per = LANES // hw
    tiles = width // LANES
    blocks = tokens // LANES
    reach = -(-(LONGEST - 1) // LANES)
    taps = s.kv.shape[0]
    halves = LANES // sw
    inner = width * t_size
    wide = lax.broadcasted_iota(jnp.int32, (1, LANES), 1)
    chunks = tokens // CHUNK

    def band(r):
        return max(0, r - reach), r + 1

    def cut(i):
        return slice(i * LANES, (i + 1) * LANES)

    barrier = pltpu.get_barrier_semaphore()
    for other in p.others():
        pl.semaphore_signal(barrier, inc=1, device_id=(p.d, other), device_id_type=MESH)

    def greet(k):
        to = (lax.rem(p.d + k, n), p.t)
        pl.semaphore_signal(barrier, inc=1, device_id=to, device_id_type=MESH)

    loop(1, n, greet)

    pick = (
        lax.broadcasted_iota(jnp.int32, (states, LANES), 0)
        == lax.broadcasted_iota(jnp.int32, (states, LANES), 1) + p.t * sw
    ) & (lax.broadcasted_iota(jnp.int32, (states, LANES), 1) < sw)
    pick_f = jnp.where(pick, 1.0, 0.0)
    steps = s.step_w[...].astype(F32)
    steps = jnp.concatenate([steps, jnp.zeros((LANES - heads, rows), F32)], axis=0).T
    steps = pltpu.roll(steps, sw, 1)
    s.ws[...] = (dot(s.state_w[...], pick_f.astype(BF16)) + steps).astype(BF16)
    res = s.res[...]
    inv = lax.rsqrt(jnp.mean(res * res, axis=1, keepdims=True) + epsilon)
    s.a_own[...] = (res * inv * s.norm_gain[...]).astype(BF16)

    gS = Gather(p, s.ws, s.gS, (s.gS_x, s.gS_u, s.gS_d, s.gS_r), True)
    gV = Gather(p, s.value_w, s.gV, (s.gV_x, s.gV_u, s.gV_d, s.gV_r), False)
    gG = Gather(p, s.gate_w, s.gG, (s.gG_x, s.gG_u, s.gG_d, s.gG_r), False)
    gO = Gather(p, s.out_w, s.gO, (s.gO_x, s.gO_u, s.gO_d, s.gO_r), False)
    ga = Spread(p, s.a_own, s.ga, (s.ga_s, s.ga_s2, s.ga_r))
    gc = Spread(p, s.c_own, s.gc, (s.gc_s, s.gc_s2, s.gc_r))
    bc = Swap(p, s.bc_own, s.bc_got, (s.bc_s, s.bc_r), False)
    sm = Swap(p, s.sm_own, s.sm_got, (s.sm_s, s.sm_r), False)
    db = Swap(p, s.db_own, s.db_got, (s.db_s, s.db_r), True)
    sl = Swap(p, s.gc, s.ga, (s.l_s, s.l_r), True)
    sg = Swap(p, s.gc, s.g_got, (s.g_s, s.g_r), True)
    tn = Swap(p, s.tn_own, s.tn_got, (s.tn_s, s.tn_r), False)
    ts = Swap(p, s.ts_own, s.ts_got, (s.ts_s, s.ts_r), False)
    en = Everyone(p, s.en_own, s.en_got, (s.en_s, s.en_r))
    ed = Everyone(p, s.ed_own, s.ed_got, (s.ed_s, s.ed_r))

    def reducer(name, w, line_first):
        bufs = [getattr(s, name + b) for b in ("_bu", "_ru", "_bd", "_rd", "_bx", "_rx")]
        sems = [getattr(s, name + b) for b in ("_su", "_qu", "_sd", "_qd", "_sx", "_qx")]
        return Reduce(p, w, bufs, sems, line_first)

    rO = reducer("rO", s.wO, True)
    rG = reducer("rG", s.wG, False)
    rV = reducer("rV", s.gO, False)
    rS = reducer("rS", s.wS, False)

    pl.semaphore_wait(barrier, n + t_size - 2)
    gS.open()
    ga.open()
    gV.open()
    s.gS[p.d] = s.ws[...]
    s.gV[p.d] = s.value_w[...]
    s.gG[p.d] = s.gate_w[...]
    s.gO[p.d] = s.out_w[...]
    s.ga[p.t] = s.a_own[...]
    s.c_own[...] = s.cot[...].astype(BF16)
    s.gc[p.t] = s.c_own[...]
    gS.open_mate()

    seg_row = s.seg[...].astype(F32)
    seg_col = jnp.broadcast_to(seg_row, (LANES, tokens)).T
    position = lax.broadcasted_iota(jnp.int32, (tokens, LANES), 0)
    for k in range(1, taps):
        same = (pltpu.roll(seg_col, k, 0) == seg_col) & (position >= k)
        s.masks[k - 1, :tokens, :] = jnp.where(same, 1.0, 0.0)
        s.masks[k - 1, tokens:, :] = jnp.zeros((8, LANES), F32)
    row_at = lax.broadcasted_iota(jnp.int32, (LANES, LANES), 0)
    col_at = lax.broadcasted_iota(jnp.int32, (LANES, LANES), 1)
    for r in range(blocks):
        for q in range(blocks):
            later = col_at + q * LANES <= row_at + r * LANES
            s.tri[cut(r), cut(q)] = jnp.where(later, 1.0, 0.0).astype(BF16)
            after = col_at + q * LANES >= row_at + r * LANES
            s.upper[cut(r), cut(q)] = jnp.where(after, 1.0, 0.0).astype(BF16)
            if q in range(*band(r)):
                allowed = (seg_col[cut(r)] == seg_row[:, cut(q)]) & later
                s.mask[cut(r), cut(q)] = jnp.where(allowed, 0.0, -1e30)

    def place(ref):
        out = jnp.zeros((1, LANES), F32)
        for h in range(heads):
            out = jnp.where(wide == sw + h, ref[:, h : h + 1], out)
        return out

    is_step = (wide >= sw) & (wide < sw + heads)
    s.ks_own[...] = dot(s.ks[...], pick_f, precision=precise)
    s.bs_own[...] = dot(s.bs[...], pick_f, precision=precise)
    rate = jnp.where(is_step, -jnp.exp(place(s.log_decay)), 0.0)
    step_bias = place(s.step_bias)
    for b in range(tiles):
        out = jnp.zeros((1, LANES), F32)
        for i in range(per):
            out = jnp.where(wide // hw == i, s.skip[:, b * per + i : b * per + i + 1], out)
        s.skips[b] = jnp.broadcast_to(out, (8, LANES))

    def early(k):
        gS.step(k)
        gV.step(k)

    loop(1, min(2, line), early)
    ga.pass_on()
    loop(min(2, line), line, early)
    gG.open()
    ga.finish()

    full = s.ga[...].reshape(tokens, model)
    s.pS[...] = dot(full, s.gS[...].reshape(model, LANES))
    s.rawS[:8, :] = jnp.zeros((8, LANES), F32)
    s.rawS[8:, :] = s.pS[...]
    conv_forward(
        s.rawS, s.ks_own, s.bs_own, s.masks, tokens, lambda base, j, x, dx: set_state(s, base, x, dx)
    )
    pieces = s.xS[...]
    fold_rows = tokens // halves
    packed = jnp.zeros((fold_rows, LANES), F32)
    for i in range(halves):
        piece = pieces[i * fold_rows : (i + 1) * fold_rows]
        if i:
            piece = pltpu.roll(piece, i * sw, 1)
        packed = jnp.where(wide // sw == i, piece, packed)
    s.bc_own[...] = packed.astype(BF16)
    bc.open()
    s.bc_got[p.t] = s.bc_own[...]
    gc.open()

    step_in = s.pS[...] + step_bias
    u = jnp.exp(-jnp.abs(step_in))
    w = 1.0 + u
    soft = jnp.where(w == 1.0, u, jnp.log(w) * u / jnp.where(w == 1.0, 1.0, w - 1.0))
    step_size = jnp.where(is_step, jnp.maximum(step_in, 0.0) + soft, 0.0)
    s.step[...] = step_size
    s.sig_step[...] = jax.nn.sigmoid(step_in)
    keep = rate * step_size
    s.keep[...] = keep
    cum = dot(s.tri[...], jnp.concatenate(three(keep), axis=1))
    cum = (cum[:, :LANES] + cum[:, LANES : 2 * LANES] + cum[:, 2 * LANES :]) * LOG2E
    cum_t = cum.T
    for h in range(heads):
        s.cumr[h] = jnp.broadcast_to(cum_t[sw + h : sw + h + 1], (8, tokens))
        s.cumb[h] = jnp.broadcast_to(cum[:, sw + h : sw + h + 1], (tokens, LANES))
    for b in range(tiles):
        out = jnp.zeros((tokens, LANES), F32)
        for i in range(per):
            h = sw + b * per + i
            out = jnp.where(wide // hw == i, step_size[:, h : h + 1], out)
        s.stepb[b] = out

    gV.finish()
    s.rawV[:8, :] = jnp.zeros((8, width), F32)
    s.rawV[8:, :] = dot(full, s.gV[...].reshape(model, width))
    conv_forward(
        s.rawV, s.kv, s.bv, s.masks, tokens, lambda base, j, x, dx: set_value(s, base, j, x, dx)
    )

    bc.wait()

    def unpack(rank, ref, col):
        got = s.bc_got[rank].astype(F32)
        for i in range(halves):
            shift = (col - i * sw) % LANES
            piece = pltpu.roll(got, shift, 1) if shift else got
            here = slice(i * fold_rows, (i + 1) * fold_rows)
            ref[here, :] = jnp.where((wide >= col) & (wide < col + sw), piece, ref[here, :])

    s.bvec[...] = jnp.zeros_like(s.bvec)
    s.cvec[...] = jnp.zeros_like(s.cvec)
    for rank in range(t_size):
        unpack(rank, s.bvec if rank * sw < part else s.cvec, rank * sw % part)
    s.bh[...] = s.bvec[...].astype(BF16)
    s.ch[...] = s.cvec[...].astype(BF16)
    for r in range(blocks):
        c0, c1 = band(r)
        s.scores[cut(r), c0 * LANES : c1 * LANES] = dot(
            s.ch[cut(r), :], s.bh[c0 * LANES : c1 * LANES, :], 1, 1
        )

    def serve(first, last, b, events):
        count = last - first
        loop(first + count * b // tiles, first + count * (b + 1) // tiles, events)

    def forward(b):
        fed = (s.x[b] * s.stepb[b]).astype(BF16)
        s.fed[b] = fed
        mine = [jnp.where(wide // hw == i, fed, jnp.zeros_like(fed)) for i in range(per)]
        for r in range(blocks):
            c0, c1 = band(r)
            cols = slice(c0 * LANES, c1 * LANES)
            y = jnp.zeros((LANES, LANES), F32)
            for i in range(per):
                h = b * per + i
                col = s.cumb[h, cut(r), :]
                for q in range(c0, c1):
                    row = s.cumr[h, 0:1, cut(q)]
                    decay = jnp.exp2((col - row) + s.mask[cut(r), cut(q)])
                    s.decay[h, r, :, cut(q - c0)] = decay
                    s.mix[h, cut(r), cut(q)] = (s.scores[cut(r), cut(q)] * decay).astype(BF16)
                y = y + dot(s.mix[h, cut(r), cols], mine[i][cols])
            s.core[b, cut(r), :] = y
            s.y[b, cut(r), :] = y + s.skips[b, 0:1, :] * s.x[b, cut(r), :]
        serve(1, line, b, gG.step)

    loop(0, tiles, forward)
    gO.open()
    gG.finish()
    s.gate[:tokens, :] = dot(full, s.gG[...].reshape(model, width))
    gc.pass_on()
    s.aT[...] = s.ga[...].reshape(tokens, model).astype(F32).T.astype(BF16)
    loop(1, line, gO.step)
    gc.finish()
    s.cT[...] = s.gc[...].reshape(tokens, model).astype(F32).T.astype(BF16)
    gO.finish()
    s.ggn[...] = dot(s.gc[...].reshape(tokens, model), s.gO[...].reshape(model, width))

    def sums(i):
        base = pl.multiple_of(i * CHUNK, CHUNK)
        at = pl.ds(base, CHUNK)
        square = jnp.zeros((CHUNK, LANES), F32)
        inner_dot = jnp.zeros((CHUNK, LANES), F32)
        for j in range(tiles):
            gate = s.gate[at, cut(j)]
            gated = s.y[j, at, :] * (gate * jax.nn.sigmoid(gate))
            scaled = s.ggn[at, cut(j)] * s.gate_gain[:, cut(j)]
            square += gated * gated
            inner_dot += scaled * gated
        square = jnp.sum(square, axis=1, keepdims=True)
        inner_dot = jnp.sum(inner_dot, axis=1, keepdims=True)
        s.sums[at, :] = jnp.where(wide == 0, square, jnp.where(wide == 1, inner_dot, 0.0))

    loop(0, chunks, sums)
    s.sm_own[...] = s.sums[...].T[:8]
    ga.drain()
    gc.drain()
    sm.open()
    total = sm.total()
    s.sums[...] = jnp.concatenate([total, jnp.zeros((LANES - 8, tokens), F32)], axis=0).T
    s.gg_sum[...] = jnp.zeros_like(s.gg_sum)

    def gated_norm(i):
        base = pl.multiple_of(i * CHUNK, CHUNK)
        at = pl.ds(base, CHUNK)
        total_sq = s.sums[at, 0:1]
        total_dot = s.sums[at, 1:2]
        inv_rms = lax.rsqrt(total_sq / inner + epsilon)
        coef = inv_rms * inv_rms * inv_rms * (total_dot / inner)
        for j in range(tiles):
            gate = s.gate[at, cut(j)]
            sig = jax.nn.sigmoid(gate)
            act = gate * sig
            mixed = s.y[j, at, :]
            gated = mixed * act
            grad = s.ggn[at, cut(j)]
            gain = s.gate_gain[:, cut(j)]
            unit = gated * inv_rms
            s.gn[at, cut(j)] = (unit * gain).astype(BF16)
            s.gg_sum[:, cut(j)] += fold(grad * unit)
            d_gated = inv_rms * (grad * gain) - gated * coef
            s.y[j, at, :] = d_gated * act
            s.gpG[at, cut(j)] = (d_gated * mixed * (sig + act * (1.0 - sig))).astype(BF16)

    loop(0, chunks, gated_norm)

    def weight_grad(left, right, ref):
        size = max(rows, 256)
        for i in range(model // size):
            out = dot(left[i * size : (i + 1) * size, :], right)
            ref[i * size // rows : (i + 1) * size // rows] = out.astype(BF16).reshape(
                size // rows, rows, out.shape[1]
            )

    weight_grad(s.cT, s.gn[...], s.wO)
    rO.open()

    def o_walk(k):
        rO.walk(k)

    loop(0, min(1, line - 1), o_walk)
    weight_grad(s.aT, s.gpG[...], s.wG)
    rG.open()
    for r in range(t_size):
        s.gc[r] = dot(
            s.gn[r * own_rows : (r + 1) * own_rows, :], s.gO[...].reshape(model, width), 1, 1
        ).astype(BF16)
    sl.open()

    s.dS[...] = jnp.zeros_like(s.dS)
    s.dskip[...] = jnp.zeros_like(s.dskip)

    def backward(b):
        fed = s.fed[b]
        half = s.y[b].astype(BF16)
        mine = [jnp.where(wide // hw == i, half, jnp.zeros_like(half)) for i in range(per)]
        for r in range(blocks):
            c0, c1 = band(r)
            cols = slice(c0 * LANES, c1 * LANES)
            acc = s.dS[cut(r), cols]
            for i in range(per):
                h = b * per + i
                d_mix = dot(mine[i][cut(r)], fed[cols], 1, 1)
                acc = acc + d_mix * s.decay[h, r, :, : (c1 - c0) * LANES]
            s.dS[cut(r), cols] = acc
        for q in range(blocks):
            r1 = min(blocks, q + reach + 1)
            down = slice(q * LANES, r1 * LANES)
            d_fed = jnp.zeros((LANES, LANES), F32)
            for i in range(per):
                d_fed = d_fed + dot(s.mix[b * per + i, down, cut(q)], mine[i][down], 0, 0)
            x = s.x[b, cut(q), :]
            dy = s.y[b, cut(q), :]
            s.core[b, cut(q), :] = (
                half[cut(q)].astype(F32) * s.core[b, cut(q), :] - fed[cut(q)].astype(F32) * d_fed
            )
            s.dskip[b] += fold(dy * x)
            d_x = d_fed * s.stepb[b, cut(q), :] + s.skips[b, 0:1, :] * dy
            s.x[b, cut(q), :] = d_fed * x
            lanes = pl.ds(pl.multiple_of(b * LANES, LANES), LANES)
            s.gate[cut(q), lanes] = d_x * s.dsil[b, cut(q), :]
        serve(min(1, line - 1), line - 1, b, o_walk)

    loop(0, tiles, backward)

    grad_scores = s.dS[...].astype(BF16)
    for r in range(blocks):
        c0, c1 = band(r)
        cols = slice(c0 * LANES, c1 * LANES)
        s.cvec[cut(r), :] = dot(grad_scores[cut(r), cols], s.bh[cols, :])
        r1 = min(blocks, r + reach + 1)
        down = slice(r * LANES, r1 * LANES)
        s.bvec[cut(r), :] = dot(grad_scores[down, cut(r)], s.ch[down, :], 0, 0)
    for rank in range(t_size):
        ref = s.bvec if rank * sw < part else s.cvec
        col = rank * sw % part
        packed = jnp.zeros((fold_rows, LANES), F32)
        for i in range(halves):
            piece = ref[i * fold_rows : (i + 1) * fold_rows, :]
            shift = (i * sw - col) % LANES
            if shift:
                piece = pltpu.roll(piece, shift, 1)
            packed = jnp.where(wide // sw == i, piece, packed)
        s.db_own[rank] = packed.astype(BF16)
    db.open()

    s.gate[tokens:, :] = jnp.zeros((8, width), F32)

    def put_value(base, j, grad):
        s.gpV[pl.ds(base, CHUNK), cut(j)] = grad.astype(BF16)

    conv_backward(s.gate, s.rawV, s.kv, s.masks, s.sumV, tokens, put_value)
    gO.drain()
    weight_grad(s.aT, s.gpV[...], s.gO)
    rV.open()

    head_sum = jnp.zeros((2 * tokens, LANES), F32)
    lane_in = lax.broadcasted_iota(jnp.int32, (LANES, LANES), 0)
    lane_out = lax.broadcasted_iota(jnp.int32, (LANES, LANES), 1)
    skip_sum = jnp.zeros((8, LANES), F32)
    for b in range(tiles):
        to_head = jnp.where(lane_out == sw + b * per + lane_in // hw, 1.0, 0.0)
        both = jnp.concatenate([s.core[b], s.x[b]], axis=0)
        head_sum = head_sum + dot(both, to_head, precision=precise)
        skip_sum = skip_sum + dot(s.dskip[b], to_head, precision=precise)
    d_keep = dot(s.upper[...], jnp.concatenate(three(head_sum[:tokens]), axis=1))
    d_keep = d_keep[:, :LANES] + d_keep[:, LANES : 2 * LANES] + d_keep[:, 2 * LANES :]
    grad_step = (head_sum[tokens:] + d_keep * rate) * s.sig_step[...]
    grad_step = jnp.where(is_step, grad_step, 0.0)
    s.ed_own[taps + 2 : taps + 3, 0:LANES] = jnp.sum(grad_step, axis=0, keepdims=True)
    s.ed_own[taps + 2 : taps + 3, LANES : 2 * LANES] = jnp.sum(
        d_keep * s.keep[...], axis=0, keepdims=True
    )
    s.ed_own[taps + 2 : taps + 3, 2 * LANES : 3 * LANES] = jnp.sum(
        skip_sum, axis=0, keepdims=True
    )

    got = db.total()
    s.dpreS[tokens:, :] = jnp.zeros((8, LANES), F32)
    for i in range(halves):
        piece = pltpu.roll(got, (LANES - i * sw) % LANES, 1) if i else got
        here = slice(i * fold_rows, (i + 1) * fold_rows)
        s.dpreS[here, :] = jnp.where(wide < sw, piece * s.dsilS[here, :], 0.0)

    def put_state(base, j, grad):
        s.gradS[pl.ds(base, CHUNK), :] = grad

    conv_backward(s.dpreS, s.rawS, s.ks_own, s.masks, s.sumS, tokens, put_state)
    s.gpS[...] = jnp.where(wide < sw, s.gradS[...], grad_step).astype(BF16)
    weight_grad(s.aT, s.gpS[...], s.wS)
    rS.open()

    s.o_layer[...] = s.res[...] + sl.total()
    for r in range(t_size):
        here = slice(r * own_rows, (r + 1) * own_rows)
        out = dot(s.gpG[here, :], s.gG[...].reshape(model, width), 1, 1)
        out = out + dot(s.gpV[here, :], s.gV[...].reshape(model, width), 1, 1)
        out = out + dot(s.gpS[here, :], s.gS[...].reshape(model, LANES), 1, 1)
        s.gc[r] = out.astype(BF16)
    sg.open()

    for k in range(taps):
        s.ed_own[k : k + 1, :] = jnp.sum(s.sumV[k], axis=0, keepdims=True)
        s.ed_own[taps + 3 : taps + 4, cut(k)] = jnp.sum(s.sumS[k], axis=0, keepdims=True)
    s.ed_own[taps : taps + 1, :] = jnp.sum(s.sumV[taps], axis=0, keepdims=True)
    s.ed_own[taps + 1 : taps + 2, :] = jnp.sum(s.gg_sum[...], axis=0, keepdims=True)
    s.ed_own[taps + 2 : taps + 3, 3 * LANES : 4 * LANES] = jnp.sum(
        s.sumS[taps], axis=0, keepdims=True
    )
    ed.open()

    loop(0, line - 1, rG.walk)
    rO.settle(s.o_proj)
    rG.settle(s.o_gate)

    loop(0, line - 1, rV.walk)

    g_sum = sg.total()
    res = s.res[...]
    inv = lax.rsqrt(jnp.mean(res * res, axis=1, keepdims=True) + epsilon)
    unit = res * inv
    scaled = g_sum * s.norm_gain[...]
    mean = jnp.mean(scaled * unit, axis=1, keepdims=True)
    s.o_input[...] = s.cot[...] + inv * (scaled - unit * mean)
    s.en_own[...] = jnp.sum(g_sum * unit, axis=0, keepdims=True)
    en.open()

    loop(0, line - 1, rS.walk)
    small = ed.total()
    s.o_small[...] = small
    for k in range(taps):
        s.ts_own[k : k + 1, :] = small[taps + 3 : taps + 4, cut(k)]
    s.ts_own[taps : taps + 1, :] = small[taps + 2 : taps + 3, 3 * LANES : 4 * LANES]
    s.ts_own[taps + 1 :, :] = jnp.zeros((8 - taps - 1, LANES), F32)
    ts.open()
    s.tn_own[...] = en.total()
    tn.open()
    rO.settle_last(s.o_proj)
    rV.settle(s.o_value)
    rS.settle(s.o_state)
    ts.wait()
    s.ts_got[p.t] = s.ts_own[...]
    for rank in range(t_size):
        piece = s.ts_got[rank]
        whole_at = rank * sw // LANES * LANES
        shift = rank * sw % LANES
        if shift:
            piece = pltpu.roll(piece, shift, 1)
        at = slice(whole_at, whole_at + LANES)
        inside = (wide >= shift) & (wide < shift + sw)
        base = jnp.zeros_like(piece) if shift == 0 else s.o_taps[:, at]
        s.o_taps[:, at] = jnp.where(inside, piece, base)
    s.o_norm[...] = tn.total()

    for thing in (gS, gV, gG, rO, rG, rV, rS):
        thing.drain()


def set_state(s, base, x, dx):
    s.xS[pl.ds(base, CHUNK), :] = x
    s.dsilS[pl.ds(base, CHUNK), :] = dx


def set_value(s, base, j, x, dx):
    s.x[j, pl.ds(base, CHUNK), :] = x
    s.dsil[j, pl.ds(base, CHUNK), :] = dx


def finish_kernel(
    sw,
    heads,
    taps,
    layer,
    inp,
    norm,
    gate,
    value,
    state,
    proj,
    small,
    state_taps,
    layer_out,
    input_out,
    norm_out,
    gate_out,
    value_out,
    step_out,
    state_out,
    kv_out,
    bv_out,
    ks_out,
    bs_out,
    sb_out,
    ld_out,
    sk_out,
    gg_out,
    proj_out,
):
    layer_out[...] = layer[...]
    input_out[...] = inp[...]
    norm_out[...] = norm[...]
    gate_out[...] = gate[...]
    value_out[...] = value[...]
    proj_out[...] = proj[...]
    state_out[...] = state[:, :sw]
    step_out[...] = state[...].T[sw : sw + heads]
    kv_out[...] = small[:taps]
    bv_out[...] = small[taps : taps + 1]
    gg_out[...] = small[taps + 1 : taps + 2]
    for i, ref in enumerate((sb_out, ld_out, sk_out)):
        row = small[taps + 2 : taps + 3, i * LANES : (i + 1) * LANES]
        ref[...] = row[:, sw : sw + heads]
    ks_out[...] = state_taps[:taps]
    bs_out[...] = state_taps[taps : taps + 1]


def local(
    n,
    t_size,
    residual,
    segments,
    norm_gain,
    in_gate,
    in_value,
    in_step,
    in_state,
    kernel_value,
    bias_value,
    kernel_state,
    bias_state,
    step_bias,
    log_decay,
    skip_gain,
    gate_gain,
    out_proj,
    cotangent,
):
    tokens = segments.shape[1]
    model = residual.shape[1]
    width = in_gate.shape[1]
    heads = in_step.shape[1]
    states = in_state.shape[1]
    rows = in_gate.shape[0]
    taps = kernel_value.shape[0]
    own_rows = residual.shape[0]
    sw = states // t_size
    hw = width // heads
    tiles = width // LANES
    line = n // 2
    halves = LANES // sw
    vm = pltpu.VMEM
    dma = pltpu.SemaphoreType.DMA
    struct = jax.ShapeDtypeStruct

    args = dict(
        res=residual,
        seg=segments,
        norm_gain=norm_gain[None],
        gate_w=in_gate,
        value_w=in_value,
        step_w=in_step.T,
        state_w=in_state,
        kv=kernel_value,
        bv=bias_value[None],
        ks=kernel_state,
        bs=bias_state[None],
        step_bias=step_bias[None],
        log_decay=log_decay[None],
        skip=skip_gain[None],
        gate_gain=gate_gain[None],
        out_w=out_proj,
        cot=cotangent,
    )
    outs = dict(
        o_layer=struct(residual.shape, F32),
        o_input=struct(residual.shape, F32),
        o_norm=struct((1, model), F32),
        o_gate=struct((rows, width), F32),
        o_value=struct((rows, width), F32),
        o_state=struct((rows, LANES), F32),
        o_proj=struct((rows, width), F32),
        o_small=struct((8, width), F32),
        o_taps=struct((8, states), F32),
    )
    tok_cols = {
        "ggn": width,
        "pS": LANES,
        "xS": LANES,
        "dsilS": LANES,
        "step": LANES,
        "sig_step": LANES,
        "keep": LANES,
        "bvec": LANES,
        "cvec": LANES,
        "sums": LANES,
        "gradS": LANES,
        "scores": tokens,
        "mask": tokens,
        "dS": tokens,
    }
    half_cols = {
        "bh": LANES,
        "ch": LANES,
        "tri": tokens,
        "upper": tokens,
        "gn": width,
        "gpG": width,
        "gpV": width,
        "gpS": LANES,
    }
    scratch = {k: vm((tokens, cols), F32) for k, cols in tok_cols.items()}
    scratch |= {k: vm((tokens, cols), BF16) for k, cols in half_cols.items()}
    scratch |= {
        k: vm((tiles, tokens, LANES), F32)
        for k in ("x", "dsil", "y", "core", "stepb")
    }
    small_rows = 8
    scratch |= dict(
        fed=vm((tiles, tokens, LANES), BF16),
        cumb=vm((heads, tokens, LANES), F32),
        cumr=vm((heads, 8, tokens), F32),
        decay=vm((heads, tokens // LANES, LANES, (-(-(LONGEST - 1) // LANES) + 1) * LANES), F32),
        mix=vm((heads, tokens, tokens), BF16),
        ws=vm((rows, LANES), BF16),
        a_own=vm((own_rows, model), BF16),
        c_own=vm((own_rows, model), BF16),
        ga=vm((t_size, own_rows, model), BF16),
        gc=vm((t_size, own_rows, model), BF16),
        aT=vm((model, tokens), BF16),
        cT=vm((model, tokens), BF16),
        gS=vm((n, rows, LANES), BF16),
        gV=vm((n, rows, width), BF16),
        gG=vm((n, rows, width), BF16),
        gO=vm((n, rows, width), BF16),
        wS=vm((n, rows, LANES), BF16),
        wG=vm((n, rows, width), BF16),
        wO=vm((n, rows, width), BF16),
        masks=vm((taps - 1, tokens + 8, LANES), F32),
        ks_own=vm((taps, LANES), F32),
        bs_own=vm((1, LANES), F32),
        skips=vm((tiles, 8, LANES), F32),
        dskip=vm((tiles, 8, LANES), F32),
        rawS=vm((tokens + 8, LANES), F32),
        rawV=vm((tokens + 8, width), F32),
        gate=vm((tokens + 8, width), F32),
        dpreS=vm((tokens + 8, LANES), F32),
        sumV=vm((taps + 1, 8, width), F32),
        sumS=vm((taps + 1, 8, LANES), F32),
        gg_sum=vm((8, width), F32),
        bc_own=vm((tokens // halves, LANES), BF16),
        bc_got=vm((t_size, tokens // halves, LANES), BF16),
        db_own=vm((t_size, tokens // halves, LANES), BF16),
        db_got=vm((t_size, tokens // halves, LANES), BF16),
        sm_own=vm((8, tokens), F32),
        sm_got=vm((t_size, 8, tokens), F32),
        g_got=vm((t_size, own_rows, model), BF16),
        tn_own=vm((1, model), F32),
        tn_got=vm((t_size, 1, model), F32),
        ts_own=vm((8, LANES), F32),
        ts_got=vm((t_size, 8, LANES), F32),
        en_own=vm((1, model), F32),
        en_got=vm((n, 1, model), F32),
        ed_own=vm((small_rows, width), F32),
        ed_got=vm((n, small_rows, width), F32),
    )
    for g in ("gS", "gV", "gG", "gO"):
        for k in "xudr":
            scratch[g + "_" + k] = dma((n,))
    for g in ("ga", "gc"):
        for k in ("s", "s2", "r"):
            scratch[g + "_" + k] = dma((t_size,))
    for g in ("bc", "sm", "db", "l", "g", "tn", "ts"):
        for k in "sr":
            scratch[g + "_" + k] = dma((t_size,))
    for g in ("en", "ed"):
        for k in "sr":
            scratch[g + "_" + k] = dma((n,))
    for g in ("rO", "rG", "rV", "rS"):
        cols = LANES if g == "rS" else width
        first = g == "rO"
        hop = (line, 2, rows, cols) if first else (line, rows, cols)
        for k in ("_bu", "_ru", "_bd", "_rd"):
            scratch[g + k] = vm(hop, BF16)
        scratch[g + "_bx"] = vm((rows, cols) if first else (16, LANES), BF16)
        scratch[g + "_rx"] = vm((rows, cols) if first else (line, rows, cols), BF16)
        for k in ("_su", "_qu", "_sd", "_qd", "_sx", "_qx"):
            scratch[g + k] = dma((line,))

    names = list(args) + list(outs) + list(scratch)
    conf = SimpleNamespace(
        names=names,
        n=n,
        t_size=t_size,
        tokens=tokens,
        model=model,
        width=width,
        heads=heads,
        states=states,
        rows=rows,
        sw=sw,
        hw=hw,
    )
    results = pl.pallas_call(
        partial(kernel, conf),
        out_shape=tuple(outs.values()),
        in_specs=[VM] * len(args),
        out_specs=(VM,) * len(outs),
        scratch_shapes=list(scratch.values()),
        compiler_params=pltpu.CompilerParams(
            collective_id=0, has_side_effects=True, vmem_limit_bytes=VMEM_BYTES
        ),
    )(*args.values())
    finals = (
        struct(residual.shape, F32),
        struct(residual.shape, F32),
        struct((1, model), F32),
        struct((rows, width), F32),
        struct((rows, width), F32),
        struct((heads, rows), F32),
        struct((rows, sw), F32),
        struct((taps, width), F32),
        struct((1, width), F32),
        struct((taps, states), F32),
        struct((1, states), F32),
        struct((1, heads), F32),
        struct((1, heads), F32),
        struct((1, heads), F32),
        struct((1, width), F32),
        struct((rows, width), F32),
    )
    out = pl.pallas_call(
        partial(finish_kernel, sw, heads, taps),
        out_shape=finals,
        in_specs=[VM] * len(results),
        out_specs=(VM,) * len(finals),
    )(*results)
    out = list(out)
    out[5] = out[5].T
    for i in (2, 8, 10, 11, 12, 13, 14):
        out[i] = out[i][0]
    return tuple(out)


def solution(mesh):
    in_specs = (
        P(("dp", "tensor"), None),
        P("dp", None),
        P(),
        P("dp", "tensor"),
        P("dp", "tensor"),
        P("dp", "tensor"),
        P("dp", None),
        P(None, "tensor"),
        P("tensor"),
        P(),
        P(),
        P("tensor"),
        P("tensor"),
        P("tensor"),
        P("tensor"),
        P("dp", "tensor"),
        P(("dp", "tensor"), None),
    )
    out_specs = (
        P(("dp", "tensor"), None),
        P(("dp", "tensor"), None),
        P(),
        P("dp", "tensor"),
        P("dp", "tensor"),
        P("dp", "tensor"),
        P("dp", "tensor"),
        P(None, "tensor"),
        P("tensor"),
        P(),
        P(),
        P("tensor"),
        P("tensor"),
        P("tensor"),
        P("tensor"),
        P("dp", "tensor"),
    )
    body = partial(local, mesh.shape["dp"], mesh.shape["tensor"])
    return jax.shard_map(body, mesh=mesh, in_specs=in_specs, out_specs=out_specs, check_vma=False)
```

```python
from functools import partial
from types import SimpleNamespace

import jax
import jax.numpy as jnp
from jax import lax
from jax.experimental import pallas as pl
from jax.experimental.pallas import tpu as pltpu
from jax.sharding import PartitionSpec as P

epsilon = 1e-05
precise = lax.Precision.HIGHEST
MESH = pl.DeviceIdType.MESH
VM = pl.BlockSpec(memory_space=pltpu.VMEM)
F32 = jnp.float32
BF16 = jnp.bfloat16
LONGEST = 256
LANES = 128
CHUNK = 32
AHEAD = 2
LOG2E = 1.4426950408889634
VMEM_BYTES = 61 * 1024 * 1024


def loop(begin, end, step):
    def body(k, carry):
        step(k)
        return carry

    lax.fori_loop(begin, end, body, 0)


def dot(a, b, ca=1, cb=0, precision=None):
    return lax.dot_general(
        a, b, (((ca,), (cb,)), ((), ())), preferred_element_type=F32, precision=precision
    )


def push(src, dst, ssem, rsem, d, t):
    return pltpu.make_async_remote_copy(
        src_ref=src,
        dst_ref=dst,
        send_sem=ssem,
        recv_sem=rsem,
        device_id=(d, t),
        device_id_type=MESH,
    )


def fold(x):
    return jnp.sum(x.reshape(x.shape[0] // 8, 8, x.shape[1]), axis=0)


def three(x):
    hi = x.astype(BF16)
    rest = x - hi.astype(F32)
    mid = rest.astype(BF16)
    low = (rest - mid.astype(F32)).astype(BF16)
    return hi, mid, low


class Place:
    def __init__(self, n, t_size):
        self.n = n
        self.t_size = t_size
        self.d = lax.axis_index("dp")
        self.t = lax.axis_index("tensor")
        self.hi = self.d // 2
        self.lo = lax.rem(self.d, 2)
        self.line = n // 2
        self.mate = self.d + 1 - 2 * self.lo
        self.has_up = self.hi < self.line - 1
        self.has_down = self.hi > 0
        self.near_low = self.hi < self.line // 2
        self.chips = t_size // 2
        self.y = self.t // 2
        self.core = lax.rem(self.t, 2)
        self.twin = self.t + 1 - 2 * self.core

    def others(self):
        return [lax.rem(self.t + k, self.t_size) for k in range(1, self.t_size)]

    def across(self, core):
        return [
            lax.rem(self.y + k, self.chips) * 2 + core for k in range(1, self.chips)
        ]


class Gather:
    def __init__(self, p, src, buf, sems, piece, pieces):
        size = src.shape[0] // pieces
        self.here = pl.ds(piece * size, size)
        self.p, self.src, self.buf = p, src.at[self.here], buf
        self.sx, self.su, self.sd, self.r = [sem.at[piece] for sem in sems]

    def into(self, q):
        return self.buf.at[q, self.here]

    def along(self, k, up):
        p = self.p
        sem = self.su if up else self.sd
        to = p.d + 2 * k if up else p.d - 2 * k
        return push(self.src, self.into(p.d), sem.at[k], self.r.at[p.d], to, p.t)

    def own(self):
        p = self.p
        return push(self.src, self.into(p.d), self.sx.at[p.d], self.r.at[p.d], p.mate, p.t)

    def relay(self, q):
        p = self.p
        return push(self.into(q), self.into(q), self.sx.at[q], self.r.at[q], p.mate, p.t)

    def arrive(self, q):
        self.relay(q).wait_recv()

    def both(self, k, up, down):
        p = self.p

        @pl.when(p.hi + k < p.line)
        def _():
            up()

        @pl.when(p.hi >= k)
        def _():
            down()

    def open(self):
        p = self.p
        loop(
            1,
            p.line,
            lambda k: self.both(
                k, self.along(k, True).start, self.along(k, False).start
            ),
        )
        self.own().start()

    def step(self, k):
        p = self.p

        def took(q):
            self.arrive(q)
            self.relay(q).start()

        self.both(k, lambda: took(p.d + 2 * k), lambda: took(p.d - 2 * k))

    def finish(self):
        p = self.p
        loop(0, p.line, lambda k: self.arrive(2 * k + 1 - p.lo))

    def drain(self):
        p = self.p
        loop(0, p.line, lambda k: self.relay(2 * k + p.lo).wait_send())
        loop(
            1,
            p.line,
            lambda k: self.both(
                k, self.along(k, True).wait_send, self.along(k, False).wait_send
            ),
        )


class Chain(Gather):
    def onward(self, q, up):
        p = self.p
        sem = self.su if up else self.sd
        to = p.d + 2 if up else p.d - 2
        return push(self.into(q), self.into(q), sem.at[q], self.r.at[q], to, p.t)

    def open(self):
        p = self.p

        @pl.when(p.has_up)
        def _():
            push(self.src, self.into(p.d), self.su.at[p.d], self.r.at[p.d], p.d + 2, p.t).start()

        @pl.when(p.has_down)
        def _():
            push(self.src, self.into(p.d), self.sd.at[p.d], self.r.at[p.d], p.d - 2, p.t).start()

        self.own().start()

    def step(self, k):
        p = self.p

        def took(q, up):
            self.arrive(q)

            @pl.when(p.has_up if up else p.has_down)
            def _():
                self.onward(q, up).start()

            self.relay(q).start()

        self.both(k, lambda: took(p.d + 2 * k, False), lambda: took(p.d - 2 * k, True))

    def drain(self):
        p = self.p

        def body(k):
            q = 2 * k + p.lo
            self.relay(q).wait_send()

            @pl.when(jnp.logical_and(p.has_up, p.hi >= k))
            def _():
                self.onward(q, True).wait_send()

            @pl.when(jnp.logical_and(p.has_down, p.hi <= k))
            def _():
                self.onward(q, False).wait_send()

        loop(0, p.line, body)


class Reduce:
    def __init__(self, p, w, bufs, sems, piece, pieces):
        size = w.shape[1] // pieces
        self.p, self.here = p, pl.ds(piece * size, size)
        self.w, self.rx, self.buf, self.got = [ref.at[:, self.here] for ref in [w] + bufs]
        self.sx, self.qx, self.ss, self.qs = [sem.at[piece] for sem in sems]

    def after(self, j):
        return lax.rem(self.p.hi + j, self.p.line)

    def send_x(self, k):
        p = self.p
        return push(
            self.w.at[2 * k + 1 - p.lo], self.rx.at[k], self.sx.at[k], self.qx.at[k], p.mate, p.t
        )

    def send(self, k, slot):
        p = self.p
        to = 2 * k + p.lo
        return push(
            self.buf.at[k], self.got.at[slot], self.ss.at[k], self.qs.at[slot], to, p.t
        )

    def open(self):
        loop(1, min(AHEAD, self.p.line) + 1, lambda j: self.send_x(self.after(j)).start())

    def mine(self, k):
        return self.w[2 * k + self.p.lo].astype(F32) + self.rx[k].astype(F32)

    def turn(self, j):
        k = self.after(j)
        self.send_x(k).wait_recv()

        @pl.when(j + AHEAD <= self.p.line)
        def _():
            self.send_x(self.after(j + AHEAD)).start()

        self.buf[k] = self.mine(k).astype(BF16)
        self.send(k, self.p.hi).start()

    def settle(self, out):
        p = self.p
        self.send_x(p.hi).wait_recv()
        out[self.here, :] = self.mine(p.hi)

        def add(j):
            k = self.after(j)
            self.send(k, k).wait_recv()
            out[self.here, :] = out[self.here, :] + self.got[k].astype(F32)

        loop(1, p.line, add)

    def drain(self):
        p = self.p

        def body(j):
            self.send_x(self.after(j)).wait_send()
            self.send(self.after(j), p.hi).wait_send()

        loop(1, p.line, body)
        self.send_x(p.hi).wait_send()


class Swap:
    def __init__(self, p, src, buf, sems, scatter):
        self.p, self.src, self.buf, self.scatter = p, src, buf, scatter
        self.ss, self.rs = sems

    def send(self, slot, other):
        src = self.src.at[other] if self.scatter else self.src
        return push(src, self.buf.at[slot], self.ss.at[other], self.rs.at[slot], self.p.d, other)

    def open(self):
        for other in self.p.others():
            self.send(self.p.t, other).start()

    def wait(self):
        for other in self.p.others():
            self.send(other, other).wait()

    def own(self):
        return self.src[self.p.t] if self.scatter else self.src[...]

    def total(self):
        self.wait()
        out = self.own().astype(F32)
        for other in self.p.others():
            out = out + self.buf[other].astype(F32)
        return out


class Spread:
    def __init__(self, p, src, buf, sems):
        self.p, self.src, self.buf = p, src, buf
        self.ss, self.s2, self.rs = sems

    def send(self, other):
        p = self.p
        return push(self.src, self.buf.at[p.t], self.ss.at[other], self.rs.at[p.t], p.d, other)

    def relay(self, q):
        p = self.p
        return push(self.buf.at[q], self.buf.at[q], self.s2.at[q], self.rs.at[q], p.d, p.twin)

    def open(self):
        p = self.p
        for other in p.across(p.core):
            self.send(other).start()
        self.send(p.twin).start()

    def pass_on(self):
        p = self.p
        for q in p.across(p.core):
            self.relay(q).wait_recv()
            self.relay(q).start()

    def finish(self):
        p = self.p
        for q in [p.twin] + p.across(1 - p.core):
            self.relay(q).wait_recv()

    def drain(self):
        p = self.p
        for other in p.across(p.core) + [p.twin]:
            self.send(other).wait_send()
        for q in p.across(p.core):
            self.relay(q).wait_send()


class Everyone:
    def __init__(self, p, src, buf, sems):
        self.p, self.src, self.buf = p, src, buf
        self.ss, self.rs = sems

    def send(self, slot, q):
        return push(self.src, self.buf.at[slot], self.ss.at[q], self.rs.at[slot], q, self.p.t)

    def open(self):
        p = self.p
        loop(1, p.n, lambda k: self.send(p.d, lax.rem(p.d + k, p.n)).start())
        self.buf[p.d] = self.src[...]

    def total(self):
        p = self.p

        def body(k):
            q = lax.rem(p.d + k, p.n)
            self.send(q, q).wait()

        loop(1, p.n, body)
        return jnp.sum(self.buf[...], axis=0)


def conv_forward(raw, taps, bias, masks, tokens, emit):
    count, cols = taps.shape

    def chunk(i):
        base = pl.multiple_of(i * CHUNK, CHUNK)
        for j in range(cols // LANES):
            ls = slice(j * LANES, (j + 1) * LANES)
            blk = raw[pl.ds(base, CHUNK + 8), ls]
            pre = bias[:, ls] + taps[0:1, ls] * blk[8:]
            for k in range(1, count):
                pre += taps[k : k + 1, ls] * (
                    blk[8 - k : 8 - k + CHUNK] * masks[k - 1, pl.ds(base, CHUNK), :]
                )
            sig = jax.nn.sigmoid(pre)
            emit(base, j, pre * sig, sig * (1.0 + pre * (1.0 - sig)))

    loop(0, tokens // CHUNK, chunk)


def conv_backward(dpre, raw, taps, masks, sums, tokens, emit):
    count, cols = taps.shape
    sums[...] = jnp.zeros_like(sums)

    def chunk(i):
        base = pl.multiple_of(i * CHUNK, CHUNK)
        for j in range(cols // LANES):
            ls = slice(j * LANES, (j + 1) * LANES)
            d_blk = dpre[pl.ds(base, CHUNK + 8), ls]
            blk = raw[pl.ds(base, CHUNK + 8), ls]
            grad = taps[0:1, ls] * d_blk[:CHUNK]
            sums[count, :, ls] += fold(d_blk[:CHUNK])
            sums[0, :, ls] += fold(d_blk[:CHUNK] * blk[8:])
            for k in range(1, count):
                d_k = d_blk * masks[k - 1, pl.ds(base, CHUNK + 8), :]
                grad += taps[k : k + 1, ls] * d_k[k : k + CHUNK]
                sums[k, :, ls] += fold(d_k[:CHUNK] * blk[8 - k : 8 - k + CHUNK])
            emit(base, j, grad)

    loop(0, tokens // CHUNK, chunk)


def kernel(c, *refs):
    s = SimpleNamespace(**dict(zip(c.names, refs)))
    p = Place(c.n, c.t_size)
    n, t_size, line = c.n, c.t_size, c.n // 2
    tokens, model, width, heads, states, rows = (
        c.tokens,
        c.model,
        c.width,
        c.heads,
        c.states,
        c.rows,
    )
    sw, hw, part = c.sw, c.hw, states // 2
    own_rows = tokens // t_size
    per = LANES // hw
    tiles = width // LANES
    blocks = tokens // LANES
    reach = -(-(LONGEST - 1) // LANES)
    taps = s.kv.shape[0]
    halves = LANES // sw
    inner = width * t_size
    wide = lax.broadcasted_iota(jnp.int32, (1, LANES), 1)
    chunks = tokens // CHUNK

    def band(r):
        return max(0, r - reach), r + 1

    def cut(i):
        return slice(i * LANES, (i + 1) * LANES)

    barrier = pltpu.get_barrier_semaphore()
    for other in p.others():
        pl.semaphore_signal(barrier, inc=1, device_id=(p.d, other), device_id_type=MESH)

    def greet(k):
        to = (lax.rem(p.d + k, n), p.t)
        pl.semaphore_signal(barrier, inc=1, device_id=to, device_id_type=MESH)

    loop(1, n, greet)

    pick = (
        lax.broadcasted_iota(jnp.int32, (states, LANES), 0)
        == lax.broadcasted_iota(jnp.int32, (states, LANES), 1) + p.t * sw
    ) & (lax.broadcasted_iota(jnp.int32, (states, LANES), 1) < sw)
    pick_f = jnp.where(pick, 1.0, 0.0)
    steps = s.step_w[...].astype(F32)
    steps = jnp.concatenate([steps, jnp.zeros((LANES - heads, rows), F32)], axis=0).T
    steps = pltpu.roll(steps, sw, 1)
    s.ws[...] = (dot(s.state_w[...], pick_f.astype(BF16)) + steps).astype(BF16)
    res = s.res[...]
    inv = lax.rsqrt(jnp.mean(res * res, axis=1, keepdims=True) + epsilon)
    s.a_own[...] = (res * inv * s.norm_gain[...]).astype(BF16)

    def gather(kind, name, src):
        sems = [getattr(s, name + b) for b in ("_x", "_u", "_d", "_r")]
        return kind(p, src, getattr(s, name), sems, 0, 1)

    gS = gather(Gather, "gS", s.ws)
    gV = gather(Chain, "gV", s.value_w)
    gG = gather(Chain, "gG", s.gate_w)
    gO = gather(Chain, "gO", s.out_w)
    queue = [gS, gV, gG, gO]

    def ahead(i):
        if i < len(queue):
            queue[i].open()

    def follow(i):
        loop(1, min(2, line), queue[i].step)
        ahead(i + 2)

    def rest(i):
        loop(min(2, line), line, queue[i].step)

    ga = Spread(p, s.a_own, s.ga, (s.ga_s, s.ga_s2, s.ga_r))
    gc = Spread(p, s.c_own, s.gc, (s.gc_s, s.gc_s2, s.gc_r))
    bc = Swap(p, s.bc_own, s.bc_got, (s.bc_s, s.bc_r), False)
    sm = Swap(p, s.sm_own, s.sm_got, (s.sm_s, s.sm_r), False)
    sn = Swap(p, s.sn_own, s.sn_got, (s.sn_s, s.sn_r), False)
    db = Swap(p, s.db_own, s.db_got, (s.db_s, s.db_r), True)
    sl = Swap(p, s.gc, s.ga, (s.l_s, s.l_r), True)
    sg = Swap(p, s.gc, s.g_got, (s.g_s, s.g_r), True)
    tn = Swap(p, s.tn_own, s.tn_got, (s.tn_s, s.tn_r), False)
    ts = Swap(p, s.ts_own, s.ts_got, (s.ts_s, s.ts_r), False)
    en = Everyone(p, s.en_own, s.en_got, (s.en_s, s.en_r))
    ed = Everyone(p, s.ed_own, s.ed_got, (s.ed_s, s.ed_r))

    def reducer(name, w):
        bufs = [getattr(s, name + b) for b in ("_rx", "_buf", "_got")]
        sems = [getattr(s, name + b) for b in ("_sx", "_qx", "_ss", "_qs")]
        return [Reduce(p, w, bufs, sems, i, c.pieces) for i in range(c.pieces)]

    rO = reducer("rO", s.wO)
    rG = reducer("rG", s.wG)
    rV = reducer("rV", s.gO)
    rS = reducer("rS", s.wS)

    pl.semaphore_wait(barrier, n + t_size - 2)
    ahead(0)
    ga.open()
    ahead(1)
    s.gS[p.d] = s.ws[...]
    s.gV[p.d] = s.value_w[...]
    s.gG[p.d] = s.gate_w[...]
    s.gO[p.d] = s.out_w[...]
    s.ga[p.t] = s.a_own[...]
    s.c_own[...] = s.cot[...].astype(BF16)
    s.gc[p.t] = s.c_own[...]

    seg_row = s.seg[...].astype(F32)
    seg_col = jnp.broadcast_to(seg_row, (LANES, tokens)).T
    position = lax.broadcasted_iota(jnp.int32, (tokens, LANES), 0)
    for k in range(1, taps):
        same = (pltpu.roll(seg_col, k, 0) == seg_col) & (position >= k)
        s.masks[k - 1, :tokens, :] = jnp.where(same, 1.0, 0.0)
        s.masks[k - 1, tokens:, :] = jnp.zeros((8, LANES), F32)
    row_at = lax.broadcasted_iota(jnp.int32, (LANES, LANES), 0)
    col_at = lax.broadcasted_iota(jnp.int32, (LANES, LANES), 1)
    for r in range(blocks):
        for q in range(blocks):
            later = col_at + q * LANES <= row_at + r * LANES
            s.tri[cut(r), cut(q)] = jnp.where(later, 1.0, 0.0).astype(BF16)
            after = col_at + q * LANES >= row_at + r * LANES
            s.upper[cut(r), cut(q)] = jnp.where(after, 1.0, 0.0).astype(BF16)
            if q in range(*band(r)):
                allowed = (seg_col[cut(r)] == seg_row[:, cut(q)]) & later
                s.mask[cut(r), cut(q)] = jnp.where(allowed, 0.0, -1e30)

    def place(ref):
        out = jnp.zeros((1, LANES), F32)
        for h in range(heads):
            out = jnp.where(wide == sw + h, ref[:, h : h + 1], out)
        return out

    is_step = (wide >= sw) & (wide < sw + heads)
    s.ks_own[...] = dot(s.ks[...], pick_f, precision=precise)
    s.bs_own[...] = dot(s.bs[...], pick_f, precision=precise)
    rate = jnp.where(is_step, -jnp.exp(place(s.log_decay)), 0.0)
    step_bias = place(s.step_bias)
    for b in range(tiles):
        out = jnp.zeros((1, LANES), F32)
        for i in range(per):
            out = jnp.where(wide // hw == i, s.skip[:, b * per + i : b * per + i + 1], out)
        s.skips[b] = jnp.broadcast_to(out, (8, LANES))

    follow(0)
    rest(0)
    ga.pass_on()
    follow(1)
    rest(1)
    gS.finish()
    ga.finish()

    def full():
        return s.ga[...].reshape(tokens, model)

    s.pS[...] = dot(full(), s.gS[...].reshape(model, LANES))
    s.rawS[:8, :] = jnp.zeros((8, LANES), F32)
    s.rawS[8:, :] = s.pS[...]
    conv_forward(
        s.rawS, s.ks_own, s.bs_own, s.masks, tokens, lambda base, j, x, dx: set_state(s, base, x, dx)
    )
    pieces = s.xS[...]
    fold_rows = tokens // halves
    packed = jnp.zeros((fold_rows, LANES), F32)
    for i in range(halves):
        piece = pieces[i * fold_rows : (i + 1) * fold_rows]
        if i:
            piece = pltpu.roll(piece, i * sw, 1)
        packed = jnp.where(wide // sw == i, piece, packed)
    s.bc_own[...] = packed.astype(BF16)
    bc.open()
    s.bc_got[p.t] = s.bc_own[...]
    gc.open()

    step_in = s.pS[...] + step_bias
    u = jnp.exp(-jnp.abs(step_in))
    w = 1.0 + u
    soft = jnp.where(w == 1.0, u, jnp.log(w) * u / jnp.where(w == 1.0, 1.0, w - 1.0))
    step_size = jnp.where(is_step, jnp.maximum(step_in, 0.0) + soft, 0.0)
    s.step[...] = step_size
    s.sig_step[...] = jax.nn.sigmoid(step_in)
    keep = rate * step_size
    s.keep[...] = keep
    cum = dot(s.tri[...], jnp.concatenate(three(keep), axis=1))
    cum = (cum[:, :LANES] + cum[:, LANES : 2 * LANES] + cum[:, 2 * LANES :]) * LOG2E
    cum_t = cum.T
    for h in range(heads):
        s.cumr[h] = jnp.broadcast_to(cum_t[sw + h : sw + h + 1], (8, tokens))
        s.cumb[h] = jnp.broadcast_to(cum[:, sw + h : sw + h + 1], (tokens, LANES))
    for b in range(tiles):
        out = jnp.zeros((tokens, LANES), F32)
        for i in range(per):
            h = sw + b * per + i
            out = jnp.where(wide // hw == i, step_size[:, h : h + 1], out)
        s.stepb[b] = out

    gV.finish()
    s.rawV[:8, :] = jnp.zeros((8, width), F32)
    s.rawV[8:, :] = dot(full(), s.gV[...].reshape(model, width))
    conv_forward(
        s.rawV, s.kv, s.bv, s.masks, tokens, lambda base, j, x, dx: set_value(s, base, j, x, dx)
    )

    bc.wait()

    def unpack(rank, ref, col):
        got = s.bc_got[rank].astype(F32)
        for i in range(halves):
            shift = (col - i * sw) % LANES
            piece = pltpu.roll(got, shift, 1) if shift else got
            here = slice(i * fold_rows, (i + 1) * fold_rows)
            ref[here, :] = jnp.where((wide >= col) & (wide < col + sw), piece, ref[here, :])

    s.bvec[...] = jnp.zeros_like(s.bvec)
    s.cvec[...] = jnp.zeros_like(s.cvec)
    for rank in range(t_size):
        unpack(rank, s.bvec if rank * sw < part else s.cvec, rank * sw % part)
    s.bh[...] = s.bvec[...].astype(BF16)
    s.ch[...] = s.cvec[...].astype(BF16)
    for r in range(blocks):
        c0, c1 = band(r)
        s.scores[cut(r), c0 * LANES : c1 * LANES] = dot(
            s.ch[cut(r), :], s.bh[c0 * LANES : c1 * LANES, :], 1, 1
        )

    def serve(first, last, b, events):
        count = last - first
        loop(first + count * b // tiles, first + count * (b + 1) // tiles, events)

    def forward(b):
        fed = (s.x[b] * s.stepb[b]).astype(BF16)
        s.fed[b] = fed
        mine = [jnp.where(wide // hw == i, fed, jnp.zeros_like(fed)) for i in range(per)]
        for r in range(blocks):
            c0, c1 = band(r)
            cols = slice(c0 * LANES, c1 * LANES)
            y = jnp.zeros((LANES, LANES), F32)
            for i in range(per):
                h = b * per + i
                col = s.cumb[h, cut(r), :]
                for q in range(c0, c1):
                    row = s.cumr[h, 0:1, cut(q)]
                    decay = jnp.exp2((col - row) + s.mask[cut(r), cut(q)])
                    s.decay[h, r, :, cut(q - c0)] = decay
                    s.mix[h, cut(r), cut(q)] = (s.scores[cut(r), cut(q)] * decay).astype(BF16)
                y = y + dot(s.mix[h, cut(r), cols], mine[i][cols])
            s.core[b, cut(r), :] = y
            s.y[b, cut(r), :] = y + s.skips[b, 0:1, :] * s.x[b, cut(r), :]

    follow(2)
    loop(0, tiles, forward)
    rest(2)
    gG.finish()
    s.gate[:tokens, :] = dot(full(), s.gG[...].reshape(model, width))
    follow(3)
    gc.pass_on()

    def squares(i):
        base = pl.multiple_of(i * CHUNK, CHUNK)
        at = pl.ds(base, CHUNK)
        square = jnp.zeros((CHUNK, LANES), F32)
        for j in range(tiles):
            gate = s.gate[at, cut(j)]
            gated = s.y[j, at, :] * (gate * jax.nn.sigmoid(gate))
            s.gated[at, cut(j)] = gated
            square += gated * gated
        s.sums[at, :] = jnp.broadcast_to(jnp.sum(square, axis=1, keepdims=True), square.shape)

    loop(0, chunks, squares)
    s.sm_own[...] = s.sums[...].T[:8]
    ga.drain()
    sm.open()
    s.aT[...] = s.ga[...].reshape(tokens, model).astype(F32).T.astype(BF16)
    rest(3)
    gc.finish()
    s.cT[...] = s.gc[...].reshape(tokens, model).astype(F32).T.astype(BF16)

    def columns(total):
        return jnp.broadcast_to(total[0:1], (LANES, tokens)).T

    s.inv_rms[...] = lax.rsqrt(columns(sm.total()) / inner + epsilon)

    def norm(i):
        base = pl.multiple_of(i * CHUNK, CHUNK)
        at = pl.ds(base, CHUNK)
        inv_rms = s.inv_rms[at, :]
        for j in range(tiles):
            unit = s.gated[at, cut(j)] * inv_rms
            s.gn[at, cut(j)] = (unit * s.gate_gain[:, cut(j)]).astype(BF16)

    loop(0, chunks, norm)

    def turns(group, begin, end):
        for r in group:
            loop(begin, end, r.turn)

    def weight_grad(left, right, ref):
        size = max(rows, 256)
        for i in range(model // size):
            out = dot(left[i * size : (i + 1) * size, :], right)
            ref[i * size // rows : (i + 1) * size // rows] = out.astype(BF16).reshape(
                size // rows, rows, out.shape[1]
            )

    weight_grad(s.cT, s.gn[...], s.wO)
    for r in rO:
        r.open()
    gO.finish()
    s.ggn[...] = dot(s.gc[...].reshape(tokens, model), s.gO[...].reshape(model, width))

    def inners(i):
        base = pl.multiple_of(i * CHUNK, CHUNK)
        at = pl.ds(base, CHUNK)
        inner_dot = jnp.zeros((CHUNK, LANES), F32)
        for j in range(tiles):
            scaled = s.ggn[at, cut(j)] * s.gate_gain[:, cut(j)]
            inner_dot += scaled * s.gated[at, cut(j)]
        s.sums[at, :] = jnp.broadcast_to(
            jnp.sum(inner_dot, axis=1, keepdims=True), inner_dot.shape
        )

    loop(0, chunks, inners)
    s.sn_own[...] = s.sums[...].T[:8]
    gc.drain()
    sn.open()
    s.gg_sum[...] = jnp.zeros_like(s.gg_sum)
    for r in range(t_size):
        s.gc[r] = dot(
            s.gn[r * own_rows : (r + 1) * own_rows, :], s.gO[...].reshape(model, width), 1, 1
        ).astype(BF16)
    s.sums[...] = columns(sn.total())
    sl.open()

    def gated_norm(i):
        base = pl.multiple_of(i * CHUNK, CHUNK)
        at = pl.ds(base, CHUNK)
        inv_rms = s.inv_rms[at, :]
        coef = inv_rms * inv_rms * inv_rms * (s.sums[at, :] / inner)
        for j in range(tiles):
            gate = s.gate[at, cut(j)]
            sig = jax.nn.sigmoid(gate)
            act = gate * sig
            gated = s.gated[at, cut(j)]
            grad = s.ggn[at, cut(j)]
            s.gg_sum[:, cut(j)] += fold(grad * (gated * inv_rms))
            d_gated = inv_rms * (grad * s.gate_gain[:, cut(j)]) - gated * coef
            mixed = s.y[j, at, :]
            s.y[j, at, :] = d_gated * act
            s.gpG[at, cut(j)] = (d_gated * mixed * (sig + act * (1.0 - sig))).astype(BF16)

    loop(0, chunks, gated_norm)

    weight_grad(s.aT, s.gpG[...], s.wG)
    for r in rG:
        r.open()
    turns(rO, 1, min(2, line))

    s.dS[...] = jnp.zeros_like(s.dS)
    s.dskip[...] = jnp.zeros_like(s.dskip)

    def o_turn(j):
        for r in rO:
            r.turn(j)

    def backward(b):
        fed = s.fed[b]
        half = s.y[b].astype(BF16)
        mine = [jnp.where(wide // hw == i, half, jnp.zeros_like(half)) for i in range(per)]
        for r in range(blocks):
            c0, c1 = band(r)
            cols = slice(c0 * LANES, c1 * LANES)
            acc = s.dS[cut(r), cols]
            for i in range(per):
                h = b * per + i
                d_mix = dot(mine[i][cut(r)], fed[cols], 1, 1)
                acc = acc + d_mix * s.decay[h, r, :, : (c1 - c0) * LANES]
            s.dS[cut(r), cols] = acc
        for q in range(blocks):
            r1 = min(blocks, q + reach + 1)
            down = slice(q * LANES, r1 * LANES)
            d_fed = jnp.zeros((LANES, LANES), F32)
            for i in range(per):
                d_fed = d_fed + dot(s.mix[b * per + i, down, cut(q)], mine[i][down], 0, 0)
            x = s.x[b, cut(q), :]
            dy = s.y[b, cut(q), :]
            s.core[b, cut(q), :] = (
                half[cut(q)].astype(F32) * s.core[b, cut(q), :] - fed[cut(q)].astype(F32) * d_fed
            )
            s.dskip[b] += fold(dy * x)
            d_x = d_fed * s.stepb[b, cut(q), :] + s.skips[b, 0:1, :] * dy
            s.x[b, cut(q), :] = d_fed * x
            lanes = pl.ds(pl.multiple_of(b * LANES, LANES), LANES)
            s.gate[cut(q), lanes] = d_x * s.dsil[b, cut(q), :]
        serve(min(2, line), line, b, o_turn)

    loop(0, tiles, backward)

    grad_scores = s.dS[...].astype(BF16)
    for r in range(blocks):
        c0, c1 = band(r)
        cols = slice(c0 * LANES, c1 * LANES)
        s.cvec[cut(r), :] = dot(grad_scores[cut(r), cols], s.bh[cols, :])
        r1 = min(blocks, r + reach + 1)
        down = slice(r * LANES, r1 * LANES)
        s.bvec[cut(r), :] = dot(grad_scores[down, cut(r)], s.ch[down, :], 0, 0)
    for rank in range(t_size):
        ref = s.bvec if rank * sw < part else s.cvec
        col = rank * sw % part
        packed = jnp.zeros((fold_rows, LANES), F32)
        for i in range(halves):
            piece = ref[i * fold_rows : (i + 1) * fold_rows, :]
            shift = (i * sw - col) % LANES
            if shift:
                piece = pltpu.roll(piece, shift, 1)
            packed = jnp.where(wide // sw == i, piece, packed)
        s.db_own[rank] = packed.astype(BF16)
    db.open()

    s.gate[tokens:, :] = jnp.zeros((8, width), F32)

    def put_value(base, j, grad):
        s.gpV[pl.ds(base, CHUNK), cut(j)] = grad.astype(BF16)

    conv_backward(s.gate, s.rawV, s.kv, s.masks, s.sumV, tokens, put_value)
    gO.drain()
    weight_grad(s.aT, s.gpV[...], s.gO)
    for r in rV:
        r.open()
    turns(rG, 1, min(2, line))

    head_sum = jnp.zeros((2 * tokens, LANES), F32)
    lane_in = lax.broadcasted_iota(jnp.int32, (LANES, LANES), 0)
    lane_out = lax.broadcasted_iota(jnp.int32, (LANES, LANES), 1)
    skip_sum = jnp.zeros((8, LANES), F32)
    for b in range(tiles):
        to_head = jnp.where(lane_out == sw + b * per + lane_in // hw, 1.0, 0.0)
        both = jnp.concatenate([s.core[b], s.x[b]], axis=0)
        head_sum = head_sum + dot(both, to_head, precision=precise)
        skip_sum = skip_sum + dot(s.dskip[b], to_head, precision=precise)
    d_keep = dot(s.upper[...], jnp.concatenate(three(head_sum[:tokens]), axis=1))
    d_keep = d_keep[:, :LANES] + d_keep[:, LANES : 2 * LANES] + d_keep[:, 2 * LANES :]
    grad_step = (head_sum[tokens:] + d_keep * rate) * s.sig_step[...]
    grad_step = jnp.where(is_step, grad_step, 0.0)
    s.ed_own[taps + 2 : taps + 3, 0:LANES] = jnp.sum(grad_step, axis=0, keepdims=True)
    s.ed_own[taps + 2 : taps + 3, LANES : 2 * LANES] = jnp.sum(
        d_keep * s.keep[...], axis=0, keepdims=True
    )
    s.ed_own[taps + 2 : taps + 3, 2 * LANES : 3 * LANES] = jnp.sum(
        skip_sum, axis=0, keepdims=True
    )

    turns(rG, min(2, line), min(3, line))
    got = db.total()
    s.dpreS[tokens:, :] = jnp.zeros((8, LANES), F32)
    for i in range(halves):
        piece = pltpu.roll(got, (LANES - i * sw) % LANES, 1) if i else got
        here = slice(i * fold_rows, (i + 1) * fold_rows)
        s.dpreS[here, :] = jnp.where(wide < sw, piece * s.dsilS[here, :], 0.0)

    def put_state(base, j, grad):
        s.gradS[pl.ds(base, CHUNK), :] = grad

    conv_backward(s.dpreS, s.rawS, s.ks_own, s.masks, s.sumS, tokens, put_state)
    s.gpS[...] = jnp.where(wide < sw, s.gradS[...], grad_step).astype(BF16)
    weight_grad(s.aT, s.gpS[...], s.wS)
    for r in rS:
        r.open()
    turns(rG, min(3, line), line)

    s.o_layer[...] = s.res[...] + sl.total()
    for r in range(t_size):
        here = slice(r * own_rows, (r + 1) * own_rows)
        out = dot(s.gpG[here, :], s.gG[...].reshape(model, width), 1, 1)
        out = out + dot(s.gpV[here, :], s.gV[...].reshape(model, width), 1, 1)
        out = out + dot(s.gpS[here, :], s.gS[...].reshape(model, LANES), 1, 1)
        s.gc[r] = out.astype(BF16)
    sg.open()

    for k in range(taps):
        s.ed_own[k : k + 1, :] = jnp.sum(s.sumV[k], axis=0, keepdims=True)
        s.ed_own[taps + 3 : taps + 4, cut(k)] = jnp.sum(s.sumS[k], axis=0, keepdims=True)
    s.ed_own[taps : taps + 1, :] = jnp.sum(s.sumV[taps], axis=0, keepdims=True)
    s.ed_own[taps + 1 : taps + 2, :] = jnp.sum(s.gg_sum[...], axis=0, keepdims=True)
    s.ed_own[taps + 2 : taps + 3, 3 * LANES : 4 * LANES] = jnp.sum(
        s.sumS[taps], axis=0, keepdims=True
    )
    ed.open()

    turns(rV, 1, line)
    for r in rO:
        r.settle(s.o_proj)
    for r in rG:
        r.settle(s.o_gate)

    g_sum = sg.total()
    res = s.res[...]
    inv = lax.rsqrt(jnp.mean(res * res, axis=1, keepdims=True) + epsilon)
    unit = res * inv
    scaled = g_sum * s.norm_gain[...]
    mean = jnp.mean(scaled * unit, axis=1, keepdims=True)
    s.o_input[...] = s.cot[...] + inv * (scaled - unit * mean)
    s.en_own[...] = jnp.sum(g_sum * unit, axis=0, keepdims=True)
    en.open()

    turns(rS, 1, line)
    small = ed.total()
    s.o_small[...] = small
    for k in range(taps):
        s.ts_own[k : k + 1, :] = small[taps + 3 : taps + 4, cut(k)]
    s.ts_own[taps : taps + 1, :] = small[taps + 2 : taps + 3, 3 * LANES : 4 * LANES]
    s.ts_own[taps + 1 :, :] = jnp.zeros((8 - taps - 1, LANES), F32)
    ts.open()
    s.tn_own[...] = en.total()
    tn.open()
    for r in rV:
        r.settle(s.o_value)
    for r in rS:
        r.settle(s.o_state)
    ts.wait()
    s.ts_got[p.t] = s.ts_own[...]
    for rank in range(t_size):
        piece = s.ts_got[rank]
        whole_at = rank * sw // LANES * LANES
        shift = rank * sw % LANES
        if shift:
            piece = pltpu.roll(piece, shift, 1)
        at = slice(whole_at, whole_at + LANES)
        inside = (wide >= shift) & (wide < shift + sw)
        base = jnp.zeros_like(piece) if shift == 0 else s.o_taps[:, at]
        s.o_taps[:, at] = jnp.where(inside, piece, base)
    s.o_norm[...] = tn.total()

    for thing in [gS, gV, gG] + rO + rG + rV + rS:
        thing.drain()


def set_state(s, base, x, dx):
    s.xS[pl.ds(base, CHUNK), :] = x
    s.dsilS[pl.ds(base, CHUNK), :] = dx


def set_value(s, base, j, x, dx):
    s.x[j, pl.ds(base, CHUNK), :] = x
    s.dsil[j, pl.ds(base, CHUNK), :] = dx


def finish_kernel(
    sw,
    heads,
    taps,
    layer,
    inp,
    norm,
    gate,
    value,
    state,
    proj,
    small,
    state_taps,
    layer_out,
    input_out,
    norm_out,
    gate_out,
    value_out,
    step_out,
    state_out,
    kv_out,
    bv_out,
    ks_out,
    bs_out,
    sb_out,
    ld_out,
    sk_out,
    gg_out,
    proj_out,
):
    layer_out[...] = layer[...]
    input_out[...] = inp[...]
    norm_out[...] = norm[...]
    gate_out[...] = gate[...]
    value_out[...] = value[...]
    proj_out[...] = proj[...]
    turned = state[...].T
    state_out[...] = turned[:sw]
    step_out[...] = turned[sw : sw + heads]
    kv_out[...] = small[:taps]
    bv_out[...] = small[taps : taps + 1]
    gg_out[...] = small[taps + 1 : taps + 2]
    for i, ref in enumerate((sb_out, ld_out, sk_out)):
        row = small[taps + 2 : taps + 3, i * LANES : (i + 1) * LANES]
        ref[...] = row[:, sw : sw + heads]
    ks_out[...] = state_taps[:taps]
    bs_out[...] = state_taps[taps : taps + 1]


def local(
    n,
    t_size,
    residual,
    segments,
    norm_gain,
    in_gate,
    in_value,
    in_step,
    in_state,
    kernel_value,
    bias_value,
    kernel_state,
    bias_state,
    step_bias,
    log_decay,
    skip_gain,
    gate_gain,
    out_proj,
    cotangent,
):
    tokens = segments.shape[1]
    model = residual.shape[1]
    width = in_gate.shape[1]
    heads = in_step.shape[1]
    states = in_state.shape[1]
    rows = in_gate.shape[0]
    taps = kernel_value.shape[0]
    own_rows = residual.shape[0]
    sw = states // t_size
    hw = width // heads
    tiles = width // LANES
    line = n // 2
    halves = LANES // sw
    vm = pltpu.VMEM
    dma = pltpu.SemaphoreType.DMA
    struct = jax.ShapeDtypeStruct

    args = dict(
        res=residual,
        seg=segments,
        norm_gain=norm_gain[None],
        gate_w=in_gate,
        value_w=in_value,
        step_w=in_step.T,
        state_w=in_state,
        kv=kernel_value,
        bv=bias_value[None],
        ks=kernel_state,
        bs=bias_state[None],
        step_bias=step_bias[None],
        log_decay=log_decay[None],
        skip=skip_gain[None],
        gate_gain=gate_gain[None],
        out_w=out_proj,
        cot=cotangent,
    )
    outs = dict(
        o_layer=struct(residual.shape, F32),
        o_input=struct(residual.shape, F32),
        o_norm=struct((1, model), F32),
        o_gate=struct((rows, width), F32),
        o_value=struct((rows, width), F32),
        o_state=struct((rows, LANES), F32),
        o_proj=struct((rows, width), F32),
        o_small=struct((8, width), F32),
        o_taps=struct((8, states), F32),
    )
    tok_cols = {
        "ggn": width,
        "pS": LANES,
        "xS": LANES,
        "dsilS": LANES,
        "step": LANES,
        "sig_step": LANES,
        "keep": LANES,
        "bvec": LANES,
        "cvec": LANES,
        "sums": LANES,
        "gradS": LANES,
        "scores": tokens,
        "mask": tokens,
        "dS": tokens,
    }
    half_cols = {
        "bh": LANES,
        "ch": LANES,
        "tri": tokens,
        "upper": tokens,
        "gn": width,
        "gpG": width,
        "gpV": width,
        "gpS": LANES,
    }
    scratch = {k: vm((tokens, cols), F32) for k, cols in tok_cols.items()}
    scratch |= {k: vm((tokens, cols), BF16) for k, cols in half_cols.items()}
    scratch |= {
        k: vm((tiles, tokens, LANES), F32)
        for k in ("x", "dsil", "y", "core", "stepb")
    }
    small_rows = 8
    pieces = 2 if rows % 32 == 0 else 1
    scratch |= dict(
        fed=vm((tiles, tokens, LANES), BF16),
        cumb=vm((heads, tokens, LANES), F32),
        cumr=vm((heads, 8, tokens), F32),
        decay=vm((heads, tokens // LANES, LANES, (-(-(LONGEST - 1) // LANES) + 1) * LANES), F32),
        mix=vm((heads, tokens, tokens), BF16),
        ws=vm((rows, LANES), BF16),
        a_own=vm((own_rows, model), BF16),
        c_own=vm((own_rows, model), BF16),
        ga=vm((t_size, own_rows, model), BF16),
        gc=vm((t_size, own_rows, model), BF16),
        aT=vm((model, tokens), BF16),
        cT=vm((model, tokens), BF16),
        gS=vm((n, rows, LANES), BF16),
        gV=vm((n, rows, width), BF16),
        gG=vm((n, rows, width), BF16),
        gO=vm((n, rows, width), BF16),
        wS=vm((n, rows, LANES), BF16),
        wG=vm((n, rows, width), BF16),
        wO=vm((n, rows, width), BF16),
        masks=vm((taps - 1, tokens + 8, LANES), F32),
        ks_own=vm((taps, LANES), F32),
        bs_own=vm((1, LANES), F32),
        skips=vm((tiles, 8, LANES), F32),
        dskip=vm((tiles, 8, LANES), F32),
        rawS=vm((tokens + 8, LANES), F32),
        rawV=vm((tokens + 8, width), F32),
        gate=vm((tokens + 8, width), F32),
        dpreS=vm((tokens + 8, LANES), F32),
        sumV=vm((taps + 1, 8, width), F32),
        sumS=vm((taps + 1, 8, LANES), F32),
        gg_sum=vm((8, width), F32),
        bc_own=vm((tokens // halves, LANES), BF16),
        bc_got=vm((t_size, tokens // halves, LANES), BF16),
        db_own=vm((t_size, tokens // halves, LANES), BF16),
        db_got=vm((t_size, tokens // halves, LANES), BF16),
        gated=vm((tokens, width), F32),
        inv_rms=vm((tokens, LANES), F32),
        sn_own=vm((8, tokens), F32),
        sn_got=vm((t_size, 8, tokens), F32),
        sm_own=vm((8, tokens), F32),
        sm_got=vm((t_size, 8, tokens), F32),
        g_got=vm((t_size, own_rows, model), BF16),
        tn_own=vm((1, model), F32),
        tn_got=vm((t_size, 1, model), F32),
        ts_own=vm((8, LANES), F32),
        ts_got=vm((t_size, 8, LANES), F32),
        en_own=vm((1, model), F32),
        en_got=vm((n, 1, model), F32),
        ed_own=vm((small_rows, width), F32),
        ed_got=vm((n, small_rows, width), F32),
    )
    for g in ("gS", "gV", "gG", "gO"):
        for k in "xudr":
            scratch[g + "_" + k] = dma((1, n))
    for g in ("ga", "gc"):
        for k in ("s", "s2", "r"):
            scratch[g + "_" + k] = dma((t_size,))
    for g in ("bc", "sm", "sn", "db", "l", "g", "tn", "ts"):
        for k in "sr":
            scratch[g + "_" + k] = dma((t_size,))
    for g in ("en", "ed"):
        for k in "sr":
            scratch[g + "_" + k] = dma((n,))
    for g in ("rO", "rG", "rV", "rS"):
        cols = LANES if g == "rS" else width
        for k in ("_rx", "_buf", "_got"):
            scratch[g + k] = vm((line, rows, cols), BF16)
        for k in ("_sx", "_qx", "_ss", "_qs"):
            scratch[g + k] = dma((pieces, line))

    names = list(args) + list(outs) + list(scratch)
    conf = SimpleNamespace(
        names=names,
        n=n,
        t_size=t_size,
        tokens=tokens,
        model=model,
        width=width,
        heads=heads,
        states=states,
        rows=rows,
        sw=sw,
        hw=hw,
        pieces=pieces,
    )
    results = pl.pallas_call(
        partial(kernel, conf),
        out_shape=tuple(outs.values()),
        in_specs=[VM] * len(args),
        out_specs=(VM,) * len(outs),
        scratch_shapes=list(scratch.values()),
        compiler_params=pltpu.CompilerParams(
            collective_id=0, has_side_effects=True, vmem_limit_bytes=VMEM_BYTES
        ),
    )(*args.values())
    finals = (
        struct(residual.shape, F32),
        struct(residual.shape, F32),
        struct((1, model), F32),
        struct((rows, width), F32),
        struct((rows, width), F32),
        struct((heads, rows), F32),
        struct((sw, rows), F32),
        struct((taps, width), F32),
        struct((1, width), F32),
        struct((taps, states), F32),
        struct((1, states), F32),
        struct((1, heads), F32),
        struct((1, heads), F32),
        struct((1, heads), F32),
        struct((1, width), F32),
        struct((rows, width), F32),
    )
    out = pl.pallas_call(
        partial(finish_kernel, sw, heads, taps),
        out_shape=finals,
        in_specs=[VM] * len(results),
        out_specs=(VM,) * len(finals),
    )(*results)
    out = list(out)
    out[5], out[6] = out[5].T, out[6].T
    for i in (2, 8, 10, 11, 12, 13, 14):
        out[i] = out[i][0]
    return tuple(out)


def solution(mesh):
    in_specs = (
        P(("dp", "tensor"), None),
        P("dp", None),
        P(),
        P("dp", "tensor"),
        P("dp", "tensor"),
        P("dp", "tensor"),
        P("dp", None),
        P(None, "tensor"),
        P("tensor"),
        P(),
        P(),
        P("tensor"),
        P("tensor"),
        P("tensor"),
        P("tensor"),
        P("dp", "tensor"),
        P(("dp", "tensor"), None),
    )
    out_specs = (
        P(("dp", "tensor"), None),
        P(("dp", "tensor"), None),
        P(),
        P("dp", "tensor"),
        P("dp", "tensor"),
        P("dp", "tensor"),
        P("dp", "tensor"),
        P(None, "tensor"),
        P("tensor"),
        P(),
        P(),
        P("tensor"),
        P("tensor"),
        P("tensor"),
        P("tensor"),
        P("dp", "tensor"),
    )
    body = partial(local, mesh.shape["dp"], mesh.shape["tensor"])
    return jax.shard_map(body, mesh=mesh, in_specs=in_specs, out_specs=out_specs, check_vma=False)
```

```python
from functools import partial
from types import SimpleNamespace

import jax
import jax.numpy as jnp
from jax import lax
from jax.experimental import pallas as pl
from jax.experimental.pallas import tpu as pltpu
from jax.sharding import PartitionSpec as P

epsilon = 1e-05
precise = lax.Precision.HIGHEST
MESH = pl.DeviceIdType.MESH
VM = pl.BlockSpec(memory_space=pltpu.VMEM)
F32 = jnp.float32
BF16 = jnp.bfloat16
LONGEST = 256
LANES = 128
CHUNK = 32
LOG2E = 1.4426950408889634
VMEM_BYTES = 61 * 1024 * 1024


def loop(begin, end, step):
    def body(k, carry):
        step(k)
        return carry

    lax.fori_loop(begin, end, body, 0)


def dot(a, b, ca=1, cb=0, precision=None):
    return lax.dot_general(
        a, b, (((ca,), (cb,)), ((), ())), preferred_element_type=F32, precision=precision
    )


def push(src, dst, ssem, rsem, d, t):
    return pltpu.make_async_remote_copy(
        src_ref=src,
        dst_ref=dst,
        send_sem=ssem,
        recv_sem=rsem,
        device_id=(d, t),
        device_id_type=MESH,
    )


def fold(x):
    return jnp.sum(x.reshape(x.shape[0] // 8, 8, x.shape[1]), axis=0)


def three(x):
    hi = x.astype(BF16)
    rest = x - hi.astype(F32)
    mid = rest.astype(BF16)
    low = (rest - mid.astype(F32)).astype(BF16)
    return hi, mid, low


class Place:
    def __init__(self, n, t_size):
        self.n = n
        self.t_size = t_size
        self.d = lax.axis_index("dp")
        self.t = lax.axis_index("tensor")
        self.hi = self.d // 2
        self.lo = lax.rem(self.d, 2)
        self.line = n // 2
        self.mate = self.d + 1 - 2 * self.lo
        self.has_up = self.hi < self.line - 1
        self.has_down = self.hi > 0
        self.near_low = self.hi < self.line // 2
        self.chips = t_size // 2
        self.y = self.t // 2
        self.core = lax.rem(self.t, 2)
        self.twin = self.t + 1 - 2 * self.core

    def others(self):
        return [lax.rem(self.t + k, self.t_size) for k in range(1, self.t_size)]

    def across(self, core):
        return [
            lax.rem(self.y + k, self.chips) * 2 + core for k in range(1, self.chips)
        ]


class Gather:
    def __init__(self, p, src, buf, sems, piece, pieces):
        size = src.shape[0] // pieces
        self.here = pl.ds(piece * size, size)
        self.p, self.src, self.buf = p, src.at[self.here], buf
        self.sx, self.su, self.sd, self.r = [sem.at[piece] for sem in sems]

    def into(self, q):
        return self.buf.at[q, self.here]

    def along(self, k, up):
        p = self.p
        sem = self.su if up else self.sd
        to = p.d + 2 * k if up else p.d - 2 * k
        return push(self.src, self.into(p.d), sem.at[k], self.r.at[p.d], to, p.t)

    def own(self):
        p = self.p
        return push(self.src, self.into(p.d), self.sx.at[p.d], self.r.at[p.d], p.mate, p.t)

    def relay(self, q):
        p = self.p
        return push(self.into(q), self.into(q), self.sx.at[q], self.r.at[q], p.mate, p.t)

    def arrive(self, q):
        self.relay(q).wait_recv()

    def both(self, k, up, down):
        p = self.p

        @pl.when(p.hi + k < p.line)
        def _():
            up()

        @pl.when(p.hi >= k)
        def _():
            down()

    def open(self):
        p = self.p
        loop(
            1,
            p.line,
            lambda k: self.both(
                k, self.along(k, True).start, self.along(k, False).start
            ),
        )
        self.own().start()

    def step(self, k):
        p = self.p

        def took(q):
            self.arrive(q)
            self.relay(q).start()

        self.both(k, lambda: took(p.d + 2 * k), lambda: took(p.d - 2 * k))

    def finish(self):
        p = self.p
        loop(0, p.line, lambda k: self.arrive(2 * k + 1 - p.lo))

    def drain(self):
        p = self.p
        loop(0, p.line, lambda k: self.relay(2 * k + p.lo).wait_send())
        loop(
            1,
            p.line,
            lambda k: self.both(
                k, self.along(k, True).wait_send, self.along(k, False).wait_send
            ),
        )


class Chain(Gather):
    def onward(self, q, up):
        p = self.p
        sem = self.su if up else self.sd
        to = p.d + 2 if up else p.d - 2
        return push(self.into(q), self.into(q), sem.at[q], self.r.at[q], to, p.t)

    def open(self):
        p = self.p

        @pl.when(p.has_up)
        def _():
            push(self.src, self.into(p.d), self.su.at[p.d], self.r.at[p.d], p.d + 2, p.t).start()

        @pl.when(p.has_down)
        def _():
            push(self.src, self.into(p.d), self.sd.at[p.d], self.r.at[p.d], p.d - 2, p.t).start()

        self.own().start()

    def step(self, k):
        p = self.p

        def took(q, up):
            self.arrive(q)

            @pl.when(p.has_up if up else p.has_down)
            def _():
                self.onward(q, up).start()

            self.relay(q).start()

        self.both(k, lambda: took(p.d + 2 * k, False), lambda: took(p.d - 2 * k, True))

    def drain(self):
        p = self.p

        def body(k):
            q = 2 * k + p.lo
            self.relay(q).wait_send()

            @pl.when(jnp.logical_and(p.has_up, p.hi >= k))
            def _():
                self.onward(q, True).wait_send()

            @pl.when(jnp.logical_and(p.has_down, p.hi <= k))
            def _():
                self.onward(q, False).wait_send()

        loop(0, p.line, body)


class Reduce:
    def __init__(self, p, w, bufs, sems, piece, pieces):
        size = w.shape[1] // pieces
        self.p, self.here = p, pl.ds(piece * size, size)
        self.w, self.rx, self.buf, self.got = [ref.at[:, self.here] for ref in [w] + bufs]
        self.sx, self.qx, self.ss, self.qs = [sem.at[piece] for sem in sems]

    def after(self, j):
        return lax.rem(self.p.hi + j, self.p.line)

    def send_x(self, k):
        p = self.p
        return push(
            self.w.at[2 * k + 1 - p.lo], self.rx.at[k], self.sx.at[k], self.qx.at[k], p.mate, p.t
        )

    def send(self, k, slot):
        p = self.p
        to = 2 * k + p.lo
        return push(
            self.buf.at[k], self.got.at[slot], self.ss.at[k], self.qs.at[slot], to, p.t
        )

    def open(self):
        loop(1, self.p.line + 1, lambda j: self.send_x(self.after(j)).start())

    def mine(self, k):
        return self.w[2 * k + self.p.lo].astype(F32) + self.rx[k].astype(F32)

    def turn(self, j):
        k = self.after(j)
        self.send_x(k).wait_recv()

        self.buf[k] = self.mine(k).astype(BF16)
        self.send(k, self.p.hi).start()

    def settle(self, out):
        p = self.p
        self.send_x(p.hi).wait_recv()
        out[self.here, :] = self.mine(p.hi)

        def add(j):
            k = self.after(j)
            self.send(k, k).wait_recv()
            out[self.here, :] = out[self.here, :] + self.got[k].astype(F32)

        loop(1, p.line, add)

    def drain(self):
        p = self.p

        def body(j):
            self.send_x(self.after(j)).wait_send()
            self.send(self.after(j), p.hi).wait_send()

        loop(1, p.line, body)
        self.send_x(p.hi).wait_send()


class Swap:
    def __init__(self, p, src, buf, sems, scatter):
        self.p, self.src, self.buf, self.scatter = p, src, buf, scatter
        self.ss, self.rs = sems

    def send(self, slot, other):
        src = self.src.at[other] if self.scatter else self.src
        return push(src, self.buf.at[slot], self.ss.at[other], self.rs.at[slot], self.p.d, other)

    def open(self):
        for other in self.p.others():
            self.send(self.p.t, other).start()

    def wait(self):
        for other in self.p.others():
            self.send(other, other).wait()

    def own(self):
        return self.src[self.p.t] if self.scatter else self.src[...]

    def total(self):
        self.wait()
        out = self.own().astype(F32)
        for other in self.p.others():
            out = out + self.buf[other].astype(F32)
        return out


class Spread:
    def __init__(self, p, src, buf, sems):
        self.p, self.src, self.buf = p, src, buf
        self.ss, self.s2, self.rs = sems

    def send(self, other):
        p = self.p
        return push(self.src, self.buf.at[p.t], self.ss.at[other], self.rs.at[p.t], p.d, other)

    def relay(self, q):
        p = self.p
        return push(self.buf.at[q], self.buf.at[q], self.s2.at[q], self.rs.at[q], p.d, p.twin)

    def open(self):
        p = self.p
        for other in p.across(p.core):
            self.send(other).start()
        self.send(p.twin).start()

    def pass_on(self):
        p = self.p
        for q in p.across(p.core):
            self.relay(q).wait_recv()
            self.relay(q).start()

    def finish(self):
        p = self.p
        for q in [p.twin] + p.across(1 - p.core):
            self.relay(q).wait_recv()

    def drain(self):
        p = self.p
        for other in p.across(p.core) + [p.twin]:
            self.send(other).wait_send()
        for q in p.across(p.core):
            self.relay(q).wait_send()


class Halve:
    def __init__(self, p, bufs, sems):
        self.p = p
        self.out_t, self.got_t, self.out_y, self.got_y, self.mine = bufs
        self.st, self.qt, self.sy, self.qy = sems

    def to_twin(self, k):
        return push(
            self.out_t.at[k], self.got_t.at[k], self.st.at[k], self.qt.at[k], self.p.d, self.p.twin
        )

    def to_chip(self, k):
        p = self.p
        to = lax.rem(p.y + k, p.chips) * 2 + p.core
        return push(self.out_y.at[k], self.got_y.at[k], self.sy.at[k], self.qy.at[k], p.d, to)

    def put(self, k, value):
        size = value.shape[0] // 2
        first, second = value[:size], value[size:]
        even = self.p.core == 0
        self.mine[k] = jnp.where(even, first, second)
        self.out_t[k] = jnp.where(even, second, first).astype(BF16)
        self.to_twin(k).start()

    def pass_on(self):
        for k in range(1, self.p.chips):
            self.to_twin(k).wait_recv()
            self.out_y[k] = (self.mine[k] + self.got_t[k].astype(F32)).astype(BF16)
            self.to_chip(k).start()

    def total(self):
        self.to_twin(0).wait_recv()
        out = self.mine[0] + self.got_t[0].astype(F32)
        for k in range(1, self.p.chips):
            self.to_chip(k).wait_recv()
            out = out + self.got_y[k].astype(F32)
        return out

    def drain(self):
        for k in range(self.p.chips):
            self.to_twin(k).wait_send()
            if k:
                self.to_chip(k).wait_send()


class Everyone:
    def __init__(self, p, src, buf, sems):
        self.p, self.src, self.buf = p, src, buf
        self.ss, self.rs = sems

    def send(self, slot, q):
        return push(self.src, self.buf.at[slot], self.ss.at[q], self.rs.at[slot], q, self.p.t)

    def open(self):
        p = self.p
        loop(1, p.n, lambda k: self.send(p.d, lax.rem(p.d + k, p.n)).start())
        self.buf[p.d] = self.src[...]

    def total(self):
        p = self.p

        def body(k):
            q = lax.rem(p.d + k, p.n)
            self.send(q, q).wait()

        loop(1, p.n, body)
        return jnp.sum(self.buf[...], axis=0)


def conv_forward(raw, taps, bias, masks, tokens, emit):
    count, cols = taps.shape

    def chunk(i):
        base = pl.multiple_of(i * CHUNK, CHUNK)
        for j in range(cols // LANES):
            ls = slice(j * LANES, (j + 1) * LANES)
            blk = raw[pl.ds(base, CHUNK + 8), ls]
            pre = bias[:, ls] + taps[0:1, ls] * blk[8:]
            for k in range(1, count):
                pre += taps[k : k + 1, ls] * (
                    blk[8 - k : 8 - k + CHUNK] * masks[k - 1, pl.ds(base, CHUNK), :]
                )
            sig = jax.nn.sigmoid(pre)
            emit(base, j, pre * sig, sig * (1.0 + pre * (1.0 - sig)))

    loop(0, tokens // CHUNK, chunk)


def conv_backward(dpre, raw, taps, masks, sums, tokens, emit):
    count, cols = taps.shape
    sums[...] = jnp.zeros_like(sums)

    def chunk(i):
        base = pl.multiple_of(i * CHUNK, CHUNK)
        for j in range(cols // LANES):
            ls = slice(j * LANES, (j + 1) * LANES)
            d_blk = dpre[pl.ds(base, CHUNK + 8), ls]
            blk = raw[pl.ds(base, CHUNK + 8), ls]
            grad = taps[0:1, ls] * d_blk[:CHUNK]
            sums[count, :, ls] += fold(d_blk[:CHUNK])
            sums[0, :, ls] += fold(d_blk[:CHUNK] * blk[8:])
            for k in range(1, count):
                d_k = d_blk * masks[k - 1, pl.ds(base, CHUNK + 8), :]
                grad += taps[k : k + 1, ls] * d_k[k : k + CHUNK]
                sums[k, :, ls] += fold(d_k[:CHUNK] * blk[8 - k : 8 - k + CHUNK])
            emit(base, j, grad)

    loop(0, tokens // CHUNK, chunk)


def kernel(c, *refs):
    s = SimpleNamespace(**dict(zip(c.names, refs)))
    p = Place(c.n, c.t_size)
    n, t_size, line = c.n, c.t_size, c.n // 2
    tokens, model, width, heads, states, rows = (
        c.tokens,
        c.model,
        c.width,
        c.heads,
        c.states,
        c.rows,
    )
    sw, hw, part = c.sw, c.hw, states // 2
    own_rows = tokens // t_size
    per = LANES // hw
    tiles = width // LANES
    blocks = tokens // LANES
    reach = -(-(LONGEST - 1) // LANES)
    taps = s.kv.shape[0]
    halves = LANES // sw
    inner = width * t_size
    wide = lax.broadcasted_iota(jnp.int32, (1, LANES), 1)
    chunks = tokens // CHUNK

    def band(r):
        return max(0, r - reach), r + 1

    def cut(i):
        return slice(i * LANES, (i + 1) * LANES)

    barrier = pltpu.get_barrier_semaphore()
    for other in p.others():
        pl.semaphore_signal(barrier, inc=1, device_id=(p.d, other), device_id_type=MESH)

    def greet(k):
        to = (lax.rem(p.d + k, n), p.t)
        pl.semaphore_signal(barrier, inc=1, device_id=to, device_id_type=MESH)

    loop(1, n, greet)

    pick = (
        lax.broadcasted_iota(jnp.int32, (states, LANES), 0)
        == lax.broadcasted_iota(jnp.int32, (states, LANES), 1) + p.t * sw
    ) & (lax.broadcasted_iota(jnp.int32, (states, LANES), 1) < sw)
    pick_f = jnp.where(pick, 1.0, 0.0)
    steps = s.step_w[...].astype(F32)
    steps = jnp.concatenate([steps, jnp.zeros((LANES - heads, rows), F32)], axis=0).T
    steps = pltpu.roll(steps, sw, 1)
    s.ws[...] = (dot(s.state_w[...], pick_f.astype(BF16)) + steps).astype(BF16)
    res = s.res[...]
    inv = lax.rsqrt(jnp.mean(res * res, axis=1, keepdims=True) + epsilon)
    s.a_own[...] = (res * inv * s.norm_gain[...]).astype(BF16)

    def gather(kind, name, src):
        sems = [getattr(s, name + b) for b in ("_x", "_u", "_d", "_r")]
        return kind(p, src, getattr(s, name), sems, 0, 1)

    gS = gather(Gather, "gS", s.ws)
    gV = gather(Chain, "gV", s.value_w)
    gG = gather(Chain, "gG", s.gate_w)
    gO = gather(Chain, "gO", s.out_w)
    queue = [gS, gV, gG, gO]

    def ahead(i):
        if i < len(queue):
            queue[i].open()

    def follow(i):
        loop(1, min(2, line), queue[i].step)
        ahead(i + 2)

    def rest(i):
        loop(min(2, line), line, queue[i].step)

    ga = Spread(p, s.a_own, s.ga, (s.ga_s, s.ga_s2, s.ga_r))
    gc = Spread(p, s.c_own, s.gc, (s.gc_s, s.gc_s2, s.gc_r))
    bc = Swap(p, s.bc_own, s.bc_got, (s.bc_s, s.bc_r), False)
    sm = Swap(p, s.sm_own, s.sm_got, (s.sm_s, s.sm_r), False)
    sn = Swap(p, s.sn_own, s.sn_got, (s.sn_s, s.sn_r), False)
    db = Swap(p, s.db_own, s.db_got, (s.db_s, s.db_r), True)
    sl = Swap(p, s.gc, s.l_got, (s.l_s, s.l_r), True)
    sg = Halve(
        p, (s.g_out, s.g_in, s.g_out2, s.g_in2, s.g_mine), (s.g_st, s.g_qt, s.g_sy, s.g_qy)
    )
    tn = Swap(p, s.tn_own, s.tn_got, (s.tn_s, s.tn_r), False)
    ts = Swap(p, s.ts_own, s.ts_got, (s.ts_s, s.ts_r), False)
    en = Everyone(p, s.en_own, s.en_got, (s.en_s, s.en_r))
    ed = Everyone(p, s.ed_own, s.ed_got, (s.ed_s, s.ed_r))

    def reducer(name, w):
        bufs = [getattr(s, name + b) for b in ("_rx", "_buf", "_got")]
        sems = [getattr(s, name + b) for b in ("_sx", "_qx", "_ss", "_qs")]
        return [Reduce(p, w, bufs, sems, i, c.pieces) for i in range(c.pieces)]

    rO = reducer("rO", s.wO)
    rG = reducer("rG", s.wG)
    rV = reducer("rV", s.gO)
    rS = reducer("rS", s.wS)

    pl.semaphore_wait(barrier, n + t_size - 2)
    ahead(0)
    ga.open()
    ahead(1)
    s.gS[p.d] = s.ws[...]
    s.gV[p.d] = s.value_w[...]
    s.gG[p.d] = s.gate_w[...]
    s.gO[p.d] = s.out_w[...]
    s.ga[p.t] = s.a_own[...]
    s.c_own[...] = s.cot[...].astype(BF16)
    s.gc[p.t] = s.c_own[...]

    seg_row = s.seg[...].astype(F32)
    seg_col = jnp.broadcast_to(seg_row, (LANES, tokens)).T
    position = lax.broadcasted_iota(jnp.int32, (tokens, LANES), 0)
    for k in range(1, taps):
        same = (pltpu.roll(seg_col, k, 0) == seg_col) & (position >= k)
        s.masks[k - 1, :tokens, :] = jnp.where(same, 1.0, 0.0)
        s.masks[k - 1, tokens:, :] = jnp.zeros((8, LANES), F32)
    row_at = lax.broadcasted_iota(jnp.int32, (LANES, LANES), 0)
    col_at = lax.broadcasted_iota(jnp.int32, (LANES, LANES), 1)
    for r in range(blocks):
        for q in range(blocks):
            later = col_at + q * LANES <= row_at + r * LANES
            s.tri[cut(r), cut(q)] = jnp.where(later, 1.0, 0.0).astype(BF16)
            after = col_at + q * LANES >= row_at + r * LANES
            s.upper[cut(r), cut(q)] = jnp.where(after, 1.0, 0.0).astype(BF16)
            if q in range(*band(r)):
                allowed = (seg_col[cut(r)] == seg_row[:, cut(q)]) & later
                s.mask[cut(r), cut(q)] = jnp.where(allowed, 0.0, -1e30)

    def place(ref):
        out = jnp.zeros((1, LANES), F32)
        for h in range(heads):
            out = jnp.where(wide == sw + h, ref[:, h : h + 1], out)
        return out

    is_step = (wide >= sw) & (wide < sw + heads)
    s.ks_own[...] = dot(s.ks[...], pick_f, precision=precise)
    s.bs_own[...] = dot(s.bs[...], pick_f, precision=precise)
    rate = jnp.where(is_step, -jnp.exp(place(s.log_decay)), 0.0)
    step_bias = place(s.step_bias)
    for b in range(tiles):
        out = jnp.zeros((1, LANES), F32)
        for i in range(per):
            out = jnp.where(wide // hw == i, s.skip[:, b * per + i : b * per + i + 1], out)
        s.skips[b] = jnp.broadcast_to(out, (8, LANES))

    follow(0)
    rest(0)
    ga.pass_on()
    follow(1)
    rest(1)
    gS.finish()
    ga.finish()

    def full():
        return s.ga[...].reshape(tokens, model)

    s.pS[...] = dot(full(), s.gS[...].reshape(model, LANES))
    s.rawS[:8, :] = jnp.zeros((8, LANES), F32)
    s.rawS[8:, :] = s.pS[...]
    conv_forward(
        s.rawS, s.ks_own, s.bs_own, s.masks, tokens, lambda base, j, x, dx: set_state(s, base, x, dx)
    )
    pieces = s.xS[...]
    fold_rows = tokens // halves
    packed = jnp.zeros((fold_rows, LANES), F32)
    for i in range(halves):
        piece = pieces[i * fold_rows : (i + 1) * fold_rows]
        if i:
            piece = pltpu.roll(piece, i * sw, 1)
        packed = jnp.where(wide // sw == i, piece, packed)
    s.bc_own[...] = packed.astype(BF16)
    bc.open()
    s.bc_got[p.t] = s.bc_own[...]
    gc.open()

    step_in = s.pS[...] + step_bias
    u = jnp.exp(-jnp.abs(step_in))
    w = 1.0 + u
    soft = jnp.where(w == 1.0, u, jnp.log(w) * u / jnp.where(w == 1.0, 1.0, w - 1.0))
    step_size = jnp.where(is_step, jnp.maximum(step_in, 0.0) + soft, 0.0)
    s.step[...] = step_size
    s.sig_step[...] = jax.nn.sigmoid(step_in)
    keep = rate * step_size
    s.keep[...] = keep
    cum = dot(s.tri[...], jnp.concatenate(three(keep), axis=1))
    cum = (cum[:, :LANES] + cum[:, LANES : 2 * LANES] + cum[:, 2 * LANES :]) * LOG2E
    cum_t = cum.T
    for h in range(heads):
        s.cumr[h] = jnp.broadcast_to(cum_t[sw + h : sw + h + 1], (8, tokens))
        s.cumb[h] = jnp.broadcast_to(cum[:, sw + h : sw + h + 1], (tokens, LANES))
    for b in range(tiles):
        out = jnp.zeros((tokens, LANES), F32)
        for i in range(per):
            h = sw + b * per + i
            out = jnp.where(wide // hw == i, step_size[:, h : h + 1], out)
        s.stepb[b] = out

    gV.finish()
    s.rawV[:8, :] = jnp.zeros((8, width), F32)
    s.rawV[8:, :] = dot(full(), s.gV[...].reshape(model, width))
    conv_forward(
        s.rawV, s.kv, s.bv, s.masks, tokens, lambda base, j, x, dx: set_value(s, base, j, x, dx)
    )

    bc.wait()

    def unpack(rank, ref, col):
        got = s.bc_got[rank].astype(F32)
        for i in range(halves):
            shift = (col - i * sw) % LANES
            piece = pltpu.roll(got, shift, 1) if shift else got
            here = slice(i * fold_rows, (i + 1) * fold_rows)
            ref[here, :] = jnp.where((wide >= col) & (wide < col + sw), piece, ref[here, :])

    s.bvec[...] = jnp.zeros_like(s.bvec)
    s.cvec[...] = jnp.zeros_like(s.cvec)
    for rank in range(t_size):
        unpack(rank, s.bvec if rank * sw < part else s.cvec, rank * sw % part)
    s.bh[...] = s.bvec[...].astype(BF16)
    s.ch[...] = s.cvec[...].astype(BF16)
    for r in range(blocks):
        c0, c1 = band(r)
        s.scores[cut(r), c0 * LANES : c1 * LANES] = dot(
            s.ch[cut(r), :], s.bh[c0 * LANES : c1 * LANES, :], 1, 1
        )

    def serve(first, last, b, events):
        count = last - first
        loop(first + count * b // tiles, first + count * (b + 1) // tiles, events)

    def forward(b):
        fed = (s.x[b] * s.stepb[b]).astype(BF16)
        s.fed[b] = fed
        mine = [jnp.where(wide // hw == i, fed, jnp.zeros_like(fed)) for i in range(per)]
        for r in range(blocks):
            c0, c1 = band(r)
            cols = slice(c0 * LANES, c1 * LANES)
            y = jnp.zeros((LANES, LANES), F32)
            for i in range(per):
                h = b * per + i
                col = s.cumb[h, cut(r), :]
                for q in range(c0, c1):
                    row = s.cumr[h, 0:1, cut(q)]
                    decay = jnp.exp2((col - row) + s.mask[cut(r), cut(q)])
                    s.decay[h, r, :, cut(q - c0)] = decay
                    s.mix[h, cut(r), cut(q)] = (s.scores[cut(r), cut(q)] * decay).astype(BF16)
                y = y + dot(s.mix[h, cut(r), cols], mine[i][cols])
            s.core[b, cut(r), :] = y
            s.y[b, cut(r), :] = y + s.skips[b, 0:1, :] * s.x[b, cut(r), :]

    follow(2)
    loop(0, tiles, forward)
    rest(2)
    gG.finish()
    s.gate[:tokens, :] = dot(full(), s.gG[...].reshape(model, width))
    follow(3)
    gc.pass_on()

    def squares(i):
        base = pl.multiple_of(i * CHUNK, CHUNK)
        at = pl.ds(base, CHUNK)
        square = jnp.zeros((CHUNK, LANES), F32)
        for j in range(tiles):
            gate = s.gate[at, cut(j)]
            gated = s.y[j, at, :] * (gate * jax.nn.sigmoid(gate))
            s.gated[at, cut(j)] = gated
            square += gated * gated
        s.sums[at, :] = jnp.broadcast_to(jnp.sum(square, axis=1, keepdims=True), square.shape)

    loop(0, chunks, squares)
    s.sm_own[...] = s.sums[...].T[:8]
    ga.drain()
    sm.open()
    s.aT[...] = s.ga[...].reshape(tokens, model).astype(F32).T.astype(BF16)
    rest(3)
    gc.finish()
    s.cT[...] = s.gc[...].reshape(tokens, model).astype(F32).T.astype(BF16)

    def columns(total):
        return jnp.broadcast_to(total[0:1], (LANES, tokens)).T

    s.inv_rms[...] = lax.rsqrt(columns(sm.total()) / inner + epsilon)

    def norm(i):
        base = pl.multiple_of(i * CHUNK, CHUNK)
        at = pl.ds(base, CHUNK)
        inv_rms = s.inv_rms[at, :]
        for j in range(tiles):
            unit = s.gated[at, cut(j)] * inv_rms
            s.gn[at, cut(j)] = (unit * s.gate_gain[:, cut(j)]).astype(BF16)

    loop(0, chunks, norm)

    def turns(group, begin, end):
        for r in group:
            loop(begin, end, r.turn)

    def weight_grad(left, right, ref):
        size = max(rows, 256)
        for i in range(model // size):
            out = dot(left[i * size : (i + 1) * size, :], right)
            ref[i * size // rows : (i + 1) * size // rows] = out.astype(BF16).reshape(
                size // rows, rows, out.shape[1]
            )

    weight_grad(s.cT, s.gn[...], s.wO)
    for r in rO:
        r.open()
    gO.finish()
    s.ggn[...] = dot(s.gc[...].reshape(tokens, model), s.gO[...].reshape(model, width))

    def inners(i):
        base = pl.multiple_of(i * CHUNK, CHUNK)
        at = pl.ds(base, CHUNK)
        inner_dot = jnp.zeros((CHUNK, LANES), F32)
        for j in range(tiles):
            scaled = s.ggn[at, cut(j)] * s.gate_gain[:, cut(j)]
            inner_dot += scaled * s.gated[at, cut(j)]
        s.sums[at, :] = jnp.broadcast_to(
            jnp.sum(inner_dot, axis=1, keepdims=True), inner_dot.shape
        )

    loop(0, chunks, inners)
    s.sn_own[...] = s.sums[...].T[:8]
    gc.drain()
    sn.open()
    s.gg_sum[...] = jnp.zeros_like(s.gg_sum)
    for r in range(t_size):
        s.gc[r] = dot(
            s.gn[r * own_rows : (r + 1) * own_rows, :], s.gO[...].reshape(model, width), 1, 1
        ).astype(BF16)
    s.sums[...] = columns(sn.total())
    sl.open()

    def gated_norm(i):
        base = pl.multiple_of(i * CHUNK, CHUNK)
        at = pl.ds(base, CHUNK)
        inv_rms = s.inv_rms[at, :]
        coef = inv_rms * inv_rms * inv_rms * (s.sums[at, :] / inner)
        for j in range(tiles):
            gate = s.gate[at, cut(j)]
            sig = jax.nn.sigmoid(gate)
            act = gate * sig
            gated = s.gated[at, cut(j)]
            grad = s.ggn[at, cut(j)]
            s.gg_sum[:, cut(j)] += fold(grad * (gated * inv_rms))
            d_gated = inv_rms * (grad * s.gate_gain[:, cut(j)]) - gated * coef
            mixed = s.y[j, at, :]
            s.y[j, at, :] = d_gated * act
            s.gpG[at, cut(j)] = (d_gated * mixed * (sig + act * (1.0 - sig))).astype(BF16)

    turns(rO, 1, 2)
    loop(0, chunks, gated_norm)

    weight_grad(s.aT, s.gpG[...], s.wG)
    for r in rG:
        r.open()
    turns(rO, 2, min(3, line))

    s.dS[...] = jnp.zeros_like(s.dS)
    s.dskip[...] = jnp.zeros_like(s.dskip)

    def o_turn(j):
        for r in rO:
            r.turn(j)

    def backward(b):
        fed = s.fed[b]
        half = s.y[b].astype(BF16)
        mine = [jnp.where(wide // hw == i, half, jnp.zeros_like(half)) for i in range(per)]
        for r in range(blocks):
            c0, c1 = band(r)
            cols = slice(c0 * LANES, c1 * LANES)
            acc = s.dS[cut(r), cols]
            for i in range(per):
                h = b * per + i
                d_mix = dot(mine[i][cut(r)], fed[cols], 1, 1)
                acc = acc + d_mix * s.decay[h, r, :, : (c1 - c0) * LANES]
            s.dS[cut(r), cols] = acc
        for q in range(blocks):
            r1 = min(blocks, q + reach + 1)
            down = slice(q * LANES, r1 * LANES)
            d_fed = jnp.zeros((LANES, LANES), F32)
            for i in range(per):
                d_fed = d_fed + dot(s.mix[b * per + i, down, cut(q)], mine[i][down], 0, 0)
            x = s.x[b, cut(q), :]
            dy = s.y[b, cut(q), :]
            s.core[b, cut(q), :] = (
                half[cut(q)].astype(F32) * s.core[b, cut(q), :] - fed[cut(q)].astype(F32) * d_fed
            )
            s.dskip[b] += fold(dy * x)
            d_x = d_fed * s.stepb[b, cut(q), :] + s.skips[b, 0:1, :] * dy
            s.x[b, cut(q), :] = d_fed * x
            lanes = pl.ds(pl.multiple_of(b * LANES, LANES), LANES)
            s.gate[cut(q), lanes] = d_x * s.dsil[b, cut(q), :]
        serve(min(3, line), line, b, o_turn)

    loop(0, tiles, backward)

    grad_scores = s.dS[...].astype(BF16)
    for r in range(blocks):
        c0, c1 = band(r)
        cols = slice(c0 * LANES, c1 * LANES)
        s.cvec[cut(r), :] = dot(grad_scores[cut(r), cols], s.bh[cols, :])
        r1 = min(blocks, r + reach + 1)
        down = slice(r * LANES, r1 * LANES)
        s.bvec[cut(r), :] = dot(grad_scores[down, cut(r)], s.ch[down, :], 0, 0)
    for rank in range(t_size):
        ref = s.bvec if rank * sw < part else s.cvec
        col = rank * sw % part
        packed = jnp.zeros((fold_rows, LANES), F32)
        for i in range(halves):
            piece = ref[i * fold_rows : (i + 1) * fold_rows, :]
            shift = (i * sw - col) % LANES
            if shift:
                piece = pltpu.roll(piece, shift, 1)
            packed = jnp.where(wide // sw == i, piece, packed)
        s.db_own[rank] = packed.astype(BF16)
    db.open()

    s.gate[tokens:, :] = jnp.zeros((8, width), F32)

    def put_value(base, j, grad):
        s.gpV[pl.ds(base, CHUNK), cut(j)] = grad.astype(BF16)

    conv_backward(s.gate, s.rawV, s.kv, s.masks, s.sumV, tokens, put_value)
    gO.drain()
    weight_grad(s.aT, s.gpV[...], s.gO)
    for r in rV:
        r.open()
    turns(rG, 1, line)

    head_sum = jnp.zeros((2 * tokens, LANES), F32)
    lane_in = lax.broadcasted_iota(jnp.int32, (LANES, LANES), 0)
    lane_out = lax.broadcasted_iota(jnp.int32, (LANES, LANES), 1)
    skip_sum = jnp.zeros((8, LANES), F32)
    for b in range(tiles):
        to_head = jnp.where(lane_out == sw + b * per + lane_in // hw, 1.0, 0.0)
        both = jnp.concatenate([s.core[b], s.x[b]], axis=0)
        head_sum = head_sum + dot(both, to_head, precision=precise)
        skip_sum = skip_sum + dot(s.dskip[b], to_head, precision=precise)
    d_keep = dot(s.upper[...], jnp.concatenate(three(head_sum[:tokens]), axis=1))
    d_keep = d_keep[:, :LANES] + d_keep[:, LANES : 2 * LANES] + d_keep[:, 2 * LANES :]
    grad_step = (head_sum[tokens:] + d_keep * rate) * s.sig_step[...]
    grad_step = jnp.where(is_step, grad_step, 0.0)
    s.ed_own[taps + 2 : taps + 3, 0:LANES] = jnp.sum(grad_step, axis=0, keepdims=True)
    s.ed_own[taps + 2 : taps + 3, LANES : 2 * LANES] = jnp.sum(
        d_keep * s.keep[...], axis=0, keepdims=True
    )
    s.ed_own[taps + 2 : taps + 3, 2 * LANES : 3 * LANES] = jnp.sum(
        skip_sum, axis=0, keepdims=True
    )

    got = db.total()
    s.dpreS[tokens:, :] = jnp.zeros((8, LANES), F32)
    for i in range(halves):
        piece = pltpu.roll(got, (LANES - i * sw) % LANES, 1) if i else got
        here = slice(i * fold_rows, (i + 1) * fold_rows)
        s.dpreS[here, :] = jnp.where(wide < sw, piece * s.dsilS[here, :], 0.0)

    def put_state(base, j, grad):
        s.gradS[pl.ds(base, CHUNK), :] = grad

    conv_backward(s.dpreS, s.rawS, s.ks_own, s.masks, s.sumS, tokens, put_state)
    s.gpS[...] = jnp.where(wide < sw, s.gradS[...], grad_step).astype(BF16)
    weight_grad(s.aT, s.gpS[...], s.wS)
    for r in rS:
        r.open()

    s.o_layer[...] = s.res[...] + sl.total()
    s.norm_sum[...] = jnp.zeros_like(s.norm_sum)
    for k in [*range(1, p.chips), 0]:
        chip = lax.rem(p.y + k, p.chips)
        here = pl.ds(pl.multiple_of(chip * 2 * own_rows, 2 * own_rows), 2 * own_rows)
        out = dot(s.gpG[here, :], s.gG[...].reshape(model, width), 1, 1)
        out = out + dot(s.gpV[here, :], s.gV[...].reshape(model, width), 1, 1)
        out = out + dot(s.gpS[here, :], s.gS[...].reshape(model, LANES), 1, 1)
        sg.put(k, out)
        rows_in = s.ga[pl.ds(chip * 2, 2)].reshape(2 * own_rows, model).astype(F32)
        s.norm_sum[...] += fold(out * rows_in)
    sg.pass_on()
    s.en_own[...] = jnp.sum(s.norm_sum[...], axis=0, keepdims=True) / s.norm_gain[...]
    en.open()

    for k in range(taps):
        s.ed_own[k : k + 1, :] = jnp.sum(s.sumV[k], axis=0, keepdims=True)
        s.ed_own[taps + 3 : taps + 4, cut(k)] = jnp.sum(s.sumS[k], axis=0, keepdims=True)
    s.ed_own[taps : taps + 1, :] = jnp.sum(s.sumV[taps], axis=0, keepdims=True)
    s.ed_own[taps + 1 : taps + 2, :] = jnp.sum(s.gg_sum[...], axis=0, keepdims=True)
    s.ed_own[taps + 2 : taps + 3, 3 * LANES : 4 * LANES] = jnp.sum(
        s.sumS[taps], axis=0, keepdims=True
    )
    ed.open()

    turns(rV, 1, line)
    turns(rS, 1, line)
    s.tn_own[...] = en.total()
    tn.open()
    small = ed.total()
    s.o_small[...] = small
    for k in range(taps):
        s.ts_own[k : k + 1, :] = small[taps + 3 : taps + 4, cut(k)]
    s.ts_own[taps : taps + 1, :] = small[taps + 2 : taps + 3, 3 * LANES : 4 * LANES]
    s.ts_own[taps + 1 :, :] = jnp.zeros((8 - taps - 1, LANES), F32)
    ts.open()
    for r in rO:
        r.settle(s.o_proj)
    for r in rG:
        r.settle(s.o_gate)

    g_sum = sg.total()
    res = s.res[...]
    inv = lax.rsqrt(jnp.mean(res * res, axis=1, keepdims=True) + epsilon)
    unit = res * inv
    scaled = g_sum * s.norm_gain[...]
    mean = jnp.mean(scaled * unit, axis=1, keepdims=True)
    s.o_input[...] = s.cot[...] + inv * (scaled - unit * mean)

    ts.wait()
    s.ts_got[p.t] = s.ts_own[...]
    for rank in range(t_size):
        piece = s.ts_got[rank]
        whole_at = rank * sw // LANES * LANES
        shift = rank * sw % LANES
        if shift:
            piece = pltpu.roll(piece, shift, 1)
        at = slice(whole_at, whole_at + LANES)
        inside = (wide >= shift) & (wide < shift + sw)
        base = jnp.zeros_like(piece) if shift == 0 else s.o_taps[:, at]
        s.o_taps[:, at] = jnp.where(inside, piece, base)
    s.o_norm[...] = tn.total()
    for r in rV:
        r.settle(s.o_value)
    for r in rS:
        r.settle(s.o_state)

    sg.drain()
    for thing in [gS, gV, gG] + rO + rG + rV + rS:
        thing.drain()


def set_state(s, base, x, dx):
    s.xS[pl.ds(base, CHUNK), :] = x
    s.dsilS[pl.ds(base, CHUNK), :] = dx


def set_value(s, base, j, x, dx):
    s.x[j, pl.ds(base, CHUNK), :] = x
    s.dsil[j, pl.ds(base, CHUNK), :] = dx


def finish_kernel(
    sw,
    heads,
    taps,
    layer,
    inp,
    norm,
    gate,
    value,
    state,
    proj,
    small,
    state_taps,
    layer_out,
    input_out,
    norm_out,
    gate_out,
    value_out,
    step_out,
    state_out,
    kv_out,
    bv_out,
    ks_out,
    bs_out,
    sb_out,
    ld_out,
    sk_out,
    gg_out,
    proj_out,
):
    layer_out[...] = layer[...]
    input_out[...] = inp[...]
    norm_out[...] = norm[...]
    gate_out[...] = gate[...]
    value_out[...] = value[...]
    proj_out[...] = proj[...]
    turned = state[...].T
    state_out[...] = turned[:sw]
    step_out[...] = turned[sw : sw + heads]
    kv_out[...] = small[:taps]
    bv_out[...] = small[taps : taps + 1]
    gg_out[...] = small[taps + 1 : taps + 2]
    for i, ref in enumerate((sb_out, ld_out, sk_out)):
        row = small[taps + 2 : taps + 3, i * LANES : (i + 1) * LANES]
        ref[...] = row[:, sw : sw + heads]
    ks_out[...] = state_taps[:taps]
    bs_out[...] = state_taps[taps : taps + 1]


def local(
    n,
    t_size,
    residual,
    segments,
    norm_gain,
    in_gate,
    in_value,
    in_step,
    in_state,
    kernel_value,
    bias_value,
    kernel_state,
    bias_state,
    step_bias,
    log_decay,
    skip_gain,
    gate_gain,
    out_proj,
    cotangent,
):
    tokens = segments.shape[1]
    model = residual.shape[1]
    width = in_gate.shape[1]
    heads = in_step.shape[1]
    states = in_state.shape[1]
    rows = in_gate.shape[0]
    taps = kernel_value.shape[0]
    own_rows = residual.shape[0]
    sw = states // t_size
    hw = width // heads
    tiles = width // LANES
    line = n // 2
    halves = LANES // sw
    vm = pltpu.VMEM
    dma = pltpu.SemaphoreType.DMA
    struct = jax.ShapeDtypeStruct

    args = dict(
        res=residual,
        seg=segments,
        norm_gain=norm_gain[None],
        gate_w=in_gate,
        value_w=in_value,
        step_w=in_step.T,
        state_w=in_state,
        kv=kernel_value,
        bv=bias_value[None],
        ks=kernel_state,
        bs=bias_state[None],
        step_bias=step_bias[None],
        log_decay=log_decay[None],
        skip=skip_gain[None],
        gate_gain=gate_gain[None],
        out_w=out_proj,
        cot=cotangent,
    )
    outs = dict(
        o_layer=struct(residual.shape, F32),
        o_input=struct(residual.shape, F32),
        o_norm=struct((1, model), F32),
        o_gate=struct((rows, width), F32),
        o_value=struct((rows, width), F32),
        o_state=struct((rows, LANES), F32),
        o_proj=struct((rows, width), F32),
        o_small=struct((8, width), F32),
        o_taps=struct((8, states), F32),
    )
    tok_cols = {
        "ggn": width,
        "pS": LANES,
        "xS": LANES,
        "dsilS": LANES,
        "step": LANES,
        "sig_step": LANES,
        "keep": LANES,
        "bvec": LANES,
        "cvec": LANES,
        "sums": LANES,
        "gradS": LANES,
        "scores": tokens,
        "mask": tokens,
        "dS": tokens,
    }
    half_cols = {
        "bh": LANES,
        "ch": LANES,
        "tri": tokens,
        "upper": tokens,
        "gn": width,
        "gpG": width,
        "gpV": width,
        "gpS": LANES,
    }
    scratch = {k: vm((tokens, cols), F32) for k, cols in tok_cols.items()}
    scratch |= {k: vm((tokens, cols), BF16) for k, cols in half_cols.items()}
    scratch |= {
        k: vm((tiles, tokens, LANES), F32)
        for k in ("x", "dsil", "y", "core", "stepb")
    }
    small_rows = 8
    pieces = 1
    scratch |= dict(
        fed=vm((tiles, tokens, LANES), BF16),
        cumb=vm((heads, tokens, LANES), F32),
        cumr=vm((heads, 8, tokens), F32),
        decay=vm((heads, tokens // LANES, LANES, (-(-(LONGEST - 1) // LANES) + 1) * LANES), F32),
        mix=vm((heads, tokens, tokens), BF16),
        ws=vm((rows, LANES), BF16),
        a_own=vm((own_rows, model), BF16),
        c_own=vm((own_rows, model), BF16),
        ga=vm((t_size, own_rows, model), BF16),
        gc=vm((t_size, own_rows, model), BF16),
        aT=vm((model, tokens), BF16),
        cT=vm((model, tokens), BF16),
        gS=vm((n, rows, LANES), BF16),
        gV=vm((n, rows, width), BF16),
        gG=vm((n, rows, width), BF16),
        gO=vm((n, rows, width), BF16),
        wS=vm((n, rows, LANES), BF16),
        wG=vm((n, rows, width), BF16),
        wO=vm((n, rows, width), BF16),
        masks=vm((taps - 1, tokens + 8, LANES), F32),
        ks_own=vm((taps, LANES), F32),
        bs_own=vm((1, LANES), F32),
        skips=vm((tiles, 8, LANES), F32),
        dskip=vm((tiles, 8, LANES), F32),
        rawS=vm((tokens + 8, LANES), F32),
        rawV=vm((tokens + 8, width), F32),
        gate=vm((tokens + 8, width), F32),
        dpreS=vm((tokens + 8, LANES), F32),
        sumV=vm((taps + 1, 8, width), F32),
        sumS=vm((taps + 1, 8, LANES), F32),
        gg_sum=vm((8, width), F32),
        bc_own=vm((tokens // halves, LANES), BF16),
        bc_got=vm((t_size, tokens // halves, LANES), BF16),
        db_own=vm((t_size, tokens // halves, LANES), BF16),
        db_got=vm((t_size, tokens // halves, LANES), BF16),
        gated=vm((tokens, width), F32),
        inv_rms=vm((tokens, LANES), F32),
        sn_own=vm((8, tokens), F32),
        sn_got=vm((t_size, 8, tokens), F32),
        sm_own=vm((8, tokens), F32),
        sm_got=vm((t_size, 8, tokens), F32),
        l_got=vm((t_size, own_rows, model), BF16),
        norm_sum=vm((8, model), F32),
        g_out=vm((t_size // 2, own_rows, model), BF16),
        g_in=vm((t_size // 2, own_rows, model), BF16),
        g_out2=vm((t_size // 2, own_rows, model), BF16),
        g_in2=vm((t_size // 2, own_rows, model), BF16),
        g_mine=vm((t_size // 2, own_rows, model), F32),
        tn_own=vm((1, model), F32),
        tn_got=vm((t_size, 1, model), F32),
        ts_own=vm((8, LANES), F32),
        ts_got=vm((t_size, 8, LANES), F32),
        en_own=vm((1, model), F32),
        en_got=vm((n, 1, model), F32),
        ed_own=vm((small_rows, width), F32),
        ed_got=vm((n, small_rows, width), F32),
    )
    for g in ("gS", "gV", "gG", "gO"):
        for k in "xudr":
            scratch[g + "_" + k] = dma((1, n))
    for g in ("ga", "gc"):
        for k in ("s", "s2", "r"):
            scratch[g + "_" + k] = dma((t_size,))
    for g in ("bc", "sm", "sn", "db", "l", "tn", "ts"):
        for k in "sr":
            scratch[g + "_" + k] = dma((t_size,))
    for k in ("g_st", "g_qt", "g_sy", "g_qy"):
        scratch[k] = dma((t_size // 2,))
    for g in ("en", "ed"):
        for k in "sr":
            scratch[g + "_" + k] = dma((n,))
    for g in ("rO", "rG", "rV", "rS"):
        cols = LANES if g == "rS" else width
        for k in ("_rx", "_buf", "_got"):
            scratch[g + k] = vm((line, rows, cols), BF16)
        for k in ("_sx", "_qx", "_ss", "_qs"):
            scratch[g + k] = dma((pieces, line))

    names = list(args) + list(outs) + list(scratch)
    conf = SimpleNamespace(
        names=names,
        n=n,
        t_size=t_size,
        tokens=tokens,
        model=model,
        width=width,
        heads=heads,
        states=states,
        rows=rows,
        sw=sw,
        hw=hw,
        pieces=pieces,
    )
    results = pl.pallas_call(
        partial(kernel, conf),
        out_shape=tuple(outs.values()),
        in_specs=[VM] * len(args),
        out_specs=(VM,) * len(outs),
        scratch_shapes=list(scratch.values()),
        compiler_params=pltpu.CompilerParams(
            collective_id=0, has_side_effects=True, vmem_limit_bytes=VMEM_BYTES
        ),
    )(*args.values())
    finals = (
        struct(residual.shape, F32),
        struct(residual.shape, F32),
        struct((1, model), F32),
        struct((rows, width), F32),
        struct((rows, width), F32),
        struct((heads, rows), F32),
        struct((sw, rows), F32),
        struct((taps, width), F32),
        struct((1, width), F32),
        struct((taps, states), F32),
        struct((1, states), F32),
        struct((1, heads), F32),
        struct((1, heads), F32),
        struct((1, heads), F32),
        struct((1, width), F32),
        struct((rows, width), F32),
    )
    out = pl.pallas_call(
        partial(finish_kernel, sw, heads, taps),
        out_shape=finals,
        in_specs=[VM] * len(results),
        out_specs=(VM,) * len(finals),
    )(*results)
    out = list(out)
    out[5], out[6] = out[5].T, out[6].T
    for i in (2, 8, 10, 11, 12, 13, 14):
        out[i] = out[i][0]
    return tuple(out)


def solution(mesh):
    in_specs = (
        P(("dp", "tensor"), None),
        P("dp", None),
        P(),
        P("dp", "tensor"),
        P("dp", "tensor"),
        P("dp", "tensor"),
        P("dp", None),
        P(None, "tensor"),
        P("tensor"),
        P(),
        P(),
        P("tensor"),
        P("tensor"),
        P("tensor"),
        P("tensor"),
        P("dp", "tensor"),
        P(("dp", "tensor"), None),
    )
    out_specs = (
        P(("dp", "tensor"), None),
        P(("dp", "tensor"), None),
        P(),
        P("dp", "tensor"),
        P("dp", "tensor"),
        P("dp", "tensor"),
        P("dp", "tensor"),
        P(None, "tensor"),
        P("tensor"),
        P(),
        P(),
        P("tensor"),
        P("tensor"),
        P("tensor"),
        P("tensor"),
        P("dp", "tensor"),
    )
    body = partial(local, mesh.shape["dp"], mesh.shape["tensor"])
    return jax.shard_map(body, mesh=mesh, in_specs=in_specs, out_specs=out_specs, check_vma=False)
```

```python
from functools import partial
from types import SimpleNamespace

import jax
import jax.numpy as jnp
from jax import lax
from jax.experimental import pallas as pl
from jax.experimental.pallas import tpu as pltpu
from jax.sharding import PartitionSpec as P

epsilon = 1e-05
precise = lax.Precision.HIGHEST
MESH = pl.DeviceIdType.MESH
VM = pl.BlockSpec(memory_space=pltpu.VMEM)
F32 = jnp.float32
BF16 = jnp.bfloat16
LONGEST = 256
LANES = 128
CHUNK = 32
LOG2E = 1.4426950408889634
VMEM_BYTES = 61 * 1024 * 1024


def loop(begin, end, step):
    def body(k, carry):
        step(k)
        return carry

    lax.fori_loop(begin, end, body, 0)


def dot(a, b, ca=1, cb=0, precision=None):
    return lax.dot_general(
        a, b, (((ca,), (cb,)), ((), ())), preferred_element_type=F32, precision=precision
    )


def push(src, dst, ssem, rsem, d, t):
    return pltpu.make_async_remote_copy(
        src_ref=src,
        dst_ref=dst,
        send_sem=ssem,
        recv_sem=rsem,
        device_id=(d, t),
        device_id_type=MESH,
    )


def fold(x):
    return jnp.sum(x.reshape(x.shape[0] // 8, 8, x.shape[1]), axis=0)


def three(x):
    hi = x.astype(BF16)
    rest = x - hi.astype(F32)
    mid = rest.astype(BF16)
    low = (rest - mid.astype(F32)).astype(BF16)
    return hi, mid, low


class Place:
    def __init__(self, n, t_size):
        self.n = n
        self.t_size = t_size
        self.d = lax.axis_index("dp")
        self.t = lax.axis_index("tensor")
        self.hi = self.d // 2
        self.lo = lax.rem(self.d, 2)
        self.line = n // 2
        self.mate = self.d + 1 - 2 * self.lo
        self.has_up = self.hi < self.line - 1
        self.has_down = self.hi > 0
        self.near_low = self.hi < self.line // 2
        self.chips = t_size // 2
        self.y = self.t // 2
        self.core = lax.rem(self.t, 2)
        self.twin = self.t + 1 - 2 * self.core

    def others(self):
        return [lax.rem(self.t + k, self.t_size) for k in range(1, self.t_size)]

    def across(self, core):
        return [
            lax.rem(self.y + k, self.chips) * 2 + core for k in range(1, self.chips)
        ]


class Gather:
    def __init__(self, p, src, buf, sems, piece, pieces):
        size = src.shape[0] // pieces
        self.here = pl.ds(piece * size, size)
        self.p, self.src, self.buf = p, src.at[self.here], buf
        self.sx, self.su, self.sd, self.r = [sem.at[piece] for sem in sems]

    def into(self, q):
        return self.buf.at[q, self.here]

    def along(self, k, up):
        p = self.p
        sem = self.su if up else self.sd
        to = p.d + 2 * k if up else p.d - 2 * k
        return push(self.src, self.into(p.d), sem.at[k], self.r.at[p.d], to, p.t)

    def own(self):
        p = self.p
        return push(self.src, self.into(p.d), self.sx.at[p.d], self.r.at[p.d], p.mate, p.t)

    def relay(self, q):
        p = self.p
        return push(self.into(q), self.into(q), self.sx.at[q], self.r.at[q], p.mate, p.t)

    def arrive(self, q):
        self.relay(q).wait_recv()

    def both(self, k, up, down):
        p = self.p

        @pl.when(p.hi + k < p.line)
        def _():
            up()

        @pl.when(p.hi >= k)
        def _():
            down()

    def open(self):
        p = self.p
        loop(
            1,
            p.line,
            lambda k: self.both(
                k, self.along(k, True).start, self.along(k, False).start
            ),
        )
        self.own().start()

    def step(self, k):
        p = self.p

        def took(q):
            self.arrive(q)
            self.relay(q).start()

        self.both(k, lambda: took(p.d + 2 * k), lambda: took(p.d - 2 * k))

    def finish(self):
        p = self.p
        loop(0, p.line, lambda k: self.arrive(2 * k + 1 - p.lo))

    def drain(self):
        p = self.p
        loop(0, p.line, lambda k: self.relay(2 * k + p.lo).wait_send())
        loop(
            1,
            p.line,
            lambda k: self.both(
                k, self.along(k, True).wait_send, self.along(k, False).wait_send
            ),
        )


class Chain(Gather):
    def onward(self, q, up):
        p = self.p
        sem = self.su if up else self.sd
        to = p.d + 2 if up else p.d - 2
        return push(self.into(q), self.into(q), sem.at[q], self.r.at[q], to, p.t)

    def open(self):
        p = self.p

        @pl.when(p.has_up)
        def _():
            push(self.src, self.into(p.d), self.su.at[p.d], self.r.at[p.d], p.d + 2, p.t).start()

        @pl.when(p.has_down)
        def _():
            push(self.src, self.into(p.d), self.sd.at[p.d], self.r.at[p.d], p.d - 2, p.t).start()

        self.own().start()

    def step(self, k):
        p = self.p

        def took(q, up):
            self.arrive(q)

            @pl.when(p.has_up if up else p.has_down)
            def _():
                self.onward(q, up).start()

            self.relay(q).start()

        self.both(k, lambda: took(p.d + 2 * k, False), lambda: took(p.d - 2 * k, True))

    def drain(self):
        p = self.p

        def body(k):
            q = 2 * k + p.lo
            self.relay(q).wait_send()

            @pl.when(jnp.logical_and(p.has_up, p.hi >= k))
            def _():
                self.onward(q, True).wait_send()

            @pl.when(jnp.logical_and(p.has_down, p.hi <= k))
            def _():
                self.onward(q, False).wait_send()

        loop(0, p.line, body)


class Reduce:
    def __init__(self, p, w, bufs, sems, piece, pieces):
        size = w.shape[1] // pieces
        self.p, self.here = p, pl.ds(piece * size, size)
        self.w, self.rx, self.buf, self.got = [ref.at[:, self.here] for ref in [w] + bufs]
        self.sx, self.qx, self.ss, self.qs = [sem.at[piece] for sem in sems]

    def after(self, j):
        return lax.rem(self.p.hi + j, self.p.line)

    def send_x(self, k):
        p = self.p
        return push(
            self.w.at[2 * k + 1 - p.lo], self.rx.at[k], self.sx.at[k], self.qx.at[k], p.mate, p.t
        )

    def send(self, k, slot):
        p = self.p
        to = 2 * k + p.lo
        return push(
            self.buf.at[k], self.got.at[slot], self.ss.at[k], self.qs.at[slot], to, p.t
        )

    def open(self):
        loop(1, self.p.line + 1, lambda j: self.send_x(self.after(j)).start())

    def mine(self, k):
        return self.w[2 * k + self.p.lo].astype(F32) + self.rx[k].astype(F32)

    def turn(self, j):
        k = self.after(j)
        self.send_x(k).wait_recv()

        self.buf[k] = self.mine(k).astype(BF16)
        self.send(k, self.p.hi).start()

    def settle(self, out):
        p = self.p
        self.send_x(p.hi).wait_recv()
        out[self.here, :] = self.mine(p.hi)

        def add(j):
            k = self.after(j)
            self.send(k, k).wait_recv()
            out[self.here, :] = out[self.here, :] + self.got[k].astype(F32)

        loop(1, p.line, add)

    def drain(self):
        p = self.p

        def body(j):
            self.send_x(self.after(j)).wait_send()
            self.send(self.after(j), p.hi).wait_send()

        loop(1, p.line, body)
        self.send_x(p.hi).wait_send()


class Swap:
    def __init__(self, p, src, buf, sems, scatter):
        self.p, self.src, self.buf, self.scatter = p, src, buf, scatter
        self.ss, self.rs = sems

    def send(self, slot, other):
        src = self.src.at[other] if self.scatter else self.src
        return push(src, self.buf.at[slot], self.ss.at[other], self.rs.at[slot], self.p.d, other)

    def open(self):
        for other in self.p.others():
            self.send(self.p.t, other).start()

    def wait(self):
        for other in self.p.others():
            self.send(other, other).wait()

    def own(self):
        return self.src[self.p.t] if self.scatter else self.src[...]

    def total(self):
        self.wait()
        out = self.own().astype(F32)
        for other in self.p.others():
            out = out + self.buf[other].astype(F32)
        return out


class Spread:
    def __init__(self, p, src, buf, sems):
        self.p, self.src, self.buf = p, src, buf
        self.ss, self.s2, self.rs = sems

    def send(self, other):
        p = self.p
        return push(self.src, self.buf.at[p.t], self.ss.at[other], self.rs.at[p.t], p.d, other)

    def relay(self, q):
        p = self.p
        return push(self.buf.at[q], self.buf.at[q], self.s2.at[q], self.rs.at[q], p.d, p.twin)

    def open(self):
        p = self.p
        for other in p.across(p.core):
            self.send(other).start()
        self.send(p.twin).start()

    def pass_on(self):
        p = self.p
        for q in p.across(p.core):
            self.relay(q).wait_recv()
            self.relay(q).start()

    def finish(self):
        p = self.p
        for q in [p.twin] + p.across(1 - p.core):
            self.relay(q).wait_recv()

    def drain(self):
        p = self.p
        for other in p.across(p.core) + [p.twin]:
            self.send(other).wait_send()
        for q in p.across(p.core):
            self.relay(q).wait_send()


class Halve:
    def __init__(self, p, bufs, sems):
        self.p = p
        self.out_t, self.got_t, self.out_y, self.got_y, self.mine = bufs
        self.st, self.qt, self.sy, self.qy = sems

    def to_twin(self, k):
        return push(
            self.out_t.at[k], self.got_t.at[k], self.st.at[k], self.qt.at[k], self.p.d, self.p.twin
        )

    def to_chip(self, k):
        p = self.p
        to = lax.rem(p.y + k, p.chips) * 2 + p.core
        return push(self.out_y.at[k], self.got_y.at[k], self.sy.at[k], self.qy.at[k], p.d, to)

    def put(self, k, value):
        size = value.shape[0] // 2
        first, second = value[:size], value[size:]
        even = self.p.core == 0
        self.mine[k] = jnp.where(even, first, second)
        self.out_t[k] = jnp.where(even, second, first).astype(BF16)
        self.to_twin(k).start()

    def pass_on(self):
        for k in range(1, self.p.chips):
            self.to_twin(k).wait_recv()
            self.out_y[k] = (self.mine[k] + self.got_t[k].astype(F32)).astype(BF16)
            self.to_chip(k).start()

    def total(self):
        self.to_twin(0).wait_recv()
        out = self.mine[0] + self.got_t[0].astype(F32)
        for k in range(1, self.p.chips):
            self.to_chip(k).wait_recv()
            out = out + self.got_y[k].astype(F32)
        return out

    def drain(self):
        for k in range(self.p.chips):
            self.to_twin(k).wait_send()
            if k:
                self.to_chip(k).wait_send()


class Everyone:
    def __init__(self, p, src, buf, sems):
        self.p, self.src, self.buf = p, src, buf
        self.ss, self.rs = sems

    def send(self, slot, q):
        return push(self.src, self.buf.at[slot], self.ss.at[q], self.rs.at[slot], q, self.p.t)

    def open(self):
        p = self.p
        loop(1, p.n, lambda k: self.send(p.d, lax.rem(p.d + k, p.n)).start())
        self.buf[p.d] = self.src[...]

    def total(self):
        p = self.p

        def body(k):
            q = lax.rem(p.d + k, p.n)
            self.send(q, q).wait()

        loop(1, p.n, body)
        return jnp.sum(self.buf[...], axis=0)


def conv_forward(raw, taps, bias, masks, tokens, emit):
    count, cols = taps.shape

    def chunk(i):
        base = pl.multiple_of(i * CHUNK, CHUNK)
        for j in range(cols // LANES):
            ls = slice(j * LANES, (j + 1) * LANES)
            blk = raw[pl.ds(base, CHUNK + 8), ls]
            pre = bias[:, ls] + taps[0:1, ls] * blk[8:]
            for k in range(1, count):
                pre += taps[k : k + 1, ls] * (
                    blk[8 - k : 8 - k + CHUNK] * masks[k - 1, pl.ds(base, CHUNK), :]
                )
            sig = jax.nn.sigmoid(pre)
            emit(base, j, pre * sig, sig * (1.0 + pre * (1.0 - sig)))

    loop(0, tokens // CHUNK, chunk)


def conv_backward(dpre, raw, taps, masks, sums, tokens, emit):
    count, cols = taps.shape
    sums[...] = jnp.zeros_like(sums)

    def chunk(i):
        base = pl.multiple_of(i * CHUNK, CHUNK)
        for j in range(cols // LANES):
            ls = slice(j * LANES, (j + 1) * LANES)
            d_blk = dpre[pl.ds(base, CHUNK + 8), ls]
            blk = raw[pl.ds(base, CHUNK + 8), ls]
            grad = taps[0:1, ls] * d_blk[:CHUNK]
            sums[count, :, ls] += fold(d_blk[:CHUNK])
            sums[0, :, ls] += fold(d_blk[:CHUNK] * blk[8:])
            for k in range(1, count):
                d_k = d_blk * masks[k - 1, pl.ds(base, CHUNK + 8), :]
                grad += taps[k : k + 1, ls] * d_k[k : k + CHUNK]
                sums[k, :, ls] += fold(d_k[:CHUNK] * blk[8 - k : 8 - k + CHUNK])
            emit(base, j, grad)

    loop(0, tokens // CHUNK, chunk)


def kernel(c, *refs):
    s = SimpleNamespace(**dict(zip(c.names, refs)))
    p = Place(c.n, c.t_size)
    n, t_size, line = c.n, c.t_size, c.n // 2
    tokens, model, width, heads, states, rows = (
        c.tokens,
        c.model,
        c.width,
        c.heads,
        c.states,
        c.rows,
    )
    sw, hw, part = c.sw, c.hw, states // 2
    own_rows = tokens // t_size
    per = LANES // hw
    tiles = width // LANES
    blocks = tokens // LANES
    reach = -(-(LONGEST - 1) // LANES)
    taps = s.kv.shape[0]
    halves = LANES // sw
    inner = width * t_size
    wide = lax.broadcasted_iota(jnp.int32, (1, LANES), 1)
    chunks = tokens // CHUNK

    def band(r):
        return max(0, r - reach), r + 1

    def cut(i):
        return slice(i * LANES, (i + 1) * LANES)

    barrier = pltpu.get_barrier_semaphore()
    for other in p.others():
        pl.semaphore_signal(barrier, inc=1, device_id=(p.d, other), device_id_type=MESH)

    def greet(k):
        to = (lax.rem(p.d + k, n), p.t)
        pl.semaphore_signal(barrier, inc=1, device_id=to, device_id_type=MESH)

    loop(1, n, greet)

    pick = (
        lax.broadcasted_iota(jnp.int32, (states, LANES), 0)
        == lax.broadcasted_iota(jnp.int32, (states, LANES), 1) + p.t * sw
    ) & (lax.broadcasted_iota(jnp.int32, (states, LANES), 1) < sw)
    pick_f = jnp.where(pick, 1.0, 0.0)
    steps = s.step_w[...].astype(F32)
    steps = jnp.concatenate([steps, jnp.zeros((LANES - heads, rows), F32)], axis=0).T
    steps = pltpu.roll(steps, sw, 1)
    s.ws[...] = (dot(s.state_w[...], pick_f.astype(BF16)) + steps).astype(BF16)
    res = s.res[...]
    inv = lax.rsqrt(jnp.mean(res * res, axis=1, keepdims=True) + epsilon)
    s.a_own[...] = (res * inv * s.norm_gain[...]).astype(BF16)

    def gather(kind, name, src):
        sems = [getattr(s, name + b) for b in ("_x", "_u", "_d", "_r")]
        return kind(p, src, getattr(s, name), sems, 0, 1)

    gS = gather(Gather, "gS", s.ws)
    gV = gather(Chain, "gV", s.value_w)
    gG = gather(Chain, "gG", s.gate_w)
    gO = gather(Chain, "gO", s.out_w)
    queue = [gS, gV, gG, gO]

    def ahead(i):
        if i < len(queue):
            queue[i].open()

    def follow(i):
        loop(1, min(2, line), queue[i].step)
        ahead(i + 2)

    def rest(i):
        loop(min(2, line), line, queue[i].step)

    ga = Spread(p, s.a_own, s.ga, (s.ga_s, s.ga_s2, s.ga_r))
    gc = Spread(p, s.c_own, s.gc, (s.gc_s, s.gc_s2, s.gc_r))
    bc = Swap(p, s.bc_own, s.bc_got, (s.bc_s, s.bc_r), False)
    sm = Swap(p, s.sm_own, s.sm_got, (s.sm_s, s.sm_r), False)
    sn = Swap(p, s.sn_own, s.sn_got, (s.sn_s, s.sn_r), False)
    db = Swap(p, s.db_own, s.db_got, (s.db_s, s.db_r), True)
    sl = Swap(p, s.gc, s.l_got, (s.l_s, s.l_r), True)
    sg = Halve(
        p, (s.g_out, s.g_in, s.g_out2, s.g_in2, s.g_mine), (s.g_st, s.g_qt, s.g_sy, s.g_qy)
    )
    tn = Swap(p, s.tn_own, s.tn_got, (s.tn_s, s.tn_r), False)
    ts = Swap(p, s.ts_own, s.ts_got, (s.ts_s, s.ts_r), False)
    en = Everyone(p, s.en_own, s.en_got, (s.en_s, s.en_r))
    ed = Everyone(p, s.ed_own, s.ed_got, (s.ed_s, s.ed_r))

    def reducer(name, w):
        bufs = [getattr(s, name + b) for b in ("_rx", "_buf", "_got")]
        sems = [getattr(s, name + b) for b in ("_sx", "_qx", "_ss", "_qs")]
        return [Reduce(p, w, bufs, sems, i, c.pieces) for i in range(c.pieces)]

    rO = reducer("rO", s.wO)
    rG = reducer("rG", s.wG)
    rV = reducer("rV", s.gO)
    rS = reducer("rS", s.wS)

    pl.semaphore_wait(barrier, n + t_size - 2)
    ahead(0)
    ga.open()
    ahead(1)
    s.gS[p.d] = s.ws[...]
    s.gV[p.d] = s.value_w[...]
    s.gG[p.d] = s.gate_w[...]
    s.gO[p.d] = s.out_w[...]
    s.ga[p.t] = s.a_own[...]
    s.c_own[...] = s.cot[...].astype(BF16)
    s.gc[p.t] = s.c_own[...]

    seg_row = s.seg[...].astype(F32)
    seg_col = jnp.broadcast_to(seg_row, (LANES, tokens)).T
    position = lax.broadcasted_iota(jnp.int32, (tokens, LANES), 0)
    for k in range(1, taps):
        same = (pltpu.roll(seg_col, k, 0) == seg_col) & (position >= k)
        s.masks[k - 1, :tokens, :] = jnp.where(same, 1.0, 0.0)
        s.masks[k - 1, tokens:, :] = jnp.zeros((8, LANES), F32)
    row_at = lax.broadcasted_iota(jnp.int32, (LANES, LANES), 0)
    col_at = lax.broadcasted_iota(jnp.int32, (LANES, LANES), 1)
    for r in range(blocks):
        for q in range(blocks):
            later = col_at + q * LANES <= row_at + r * LANES
            s.tri[cut(r), cut(q)] = jnp.where(later, 1.0, 0.0).astype(BF16)
            after = col_at + q * LANES >= row_at + r * LANES
            s.upper[cut(r), cut(q)] = jnp.where(after, 1.0, 0.0).astype(BF16)
            if q in range(*band(r)):
                allowed = (seg_col[cut(r)] == seg_row[:, cut(q)]) & later
                s.mask[cut(r), cut(q)] = jnp.where(allowed, 0.0, -1e30)

    def place(ref):
        out = jnp.zeros((1, LANES), F32)
        for h in range(heads):
            out = jnp.where(wide == sw + h, ref[:, h : h + 1], out)
        return out

    is_step = (wide >= sw) & (wide < sw + heads)
    s.ks_own[...] = dot(s.ks[...], pick_f, precision=precise)
    s.bs_own[...] = dot(s.bs[...], pick_f, precision=precise)
    rate = jnp.where(is_step, -jnp.exp(place(s.log_decay)), 0.0)
    step_bias = place(s.step_bias)
    for b in range(tiles):
        out = jnp.zeros((1, LANES), F32)
        for i in range(per):
            out = jnp.where(wide // hw == i, s.skip[:, b * per + i : b * per + i + 1], out)
        s.skips[b] = jnp.broadcast_to(out, (8, LANES))

    follow(0)
    rest(0)
    ga.pass_on()
    follow(1)
    rest(1)
    gS.finish()
    ga.finish()

    def full():
        return s.ga[...].reshape(tokens, model)

    s.pS[...] = dot(full(), s.gS[...].reshape(model, LANES))
    s.rawS[:8, :] = jnp.zeros((8, LANES), F32)
    s.rawS[8:, :] = s.pS[...]
    conv_forward(
        s.rawS, s.ks_own, s.bs_own, s.masks, tokens, lambda base, j, x, dx: set_state(s, base, x, dx)
    )
    pieces = s.xS[...]
    fold_rows = tokens // halves
    packed = jnp.zeros((fold_rows, LANES), F32)
    for i in range(halves):
        piece = pieces[i * fold_rows : (i + 1) * fold_rows]
        if i:
            piece = pltpu.roll(piece, i * sw, 1)
        packed = jnp.where(wide // sw == i, piece, packed)
    s.bc_own[...] = packed.astype(BF16)
    bc.open()
    s.bc_got[p.t] = s.bc_own[...]
    gc.open()

    step_in = s.pS[...] + step_bias
    u = jnp.exp(-jnp.abs(step_in))
    w = 1.0 + u
    soft = jnp.where(w == 1.0, u, jnp.log(w) * u / jnp.where(w == 1.0, 1.0, w - 1.0))
    step_size = jnp.where(is_step, jnp.maximum(step_in, 0.0) + soft, 0.0)
    s.step[...] = step_size
    s.sig_step[...] = jax.nn.sigmoid(step_in)
    keep = rate * step_size
    s.keep[...] = keep
    cum = dot(s.tri[...], jnp.concatenate(three(keep), axis=1))
    cum = (cum[:, :LANES] + cum[:, LANES : 2 * LANES] + cum[:, 2 * LANES :]) * LOG2E
    cum_t = cum.T
    for h in range(heads):
        s.cumr[h] = jnp.broadcast_to(cum_t[sw + h : sw + h + 1], (8, tokens))
        s.cumb[h] = jnp.broadcast_to(cum[:, sw + h : sw + h + 1], (tokens, LANES))
    for b in range(tiles):
        out = jnp.zeros((tokens, LANES), F32)
        for i in range(per):
            h = sw + b * per + i
            out = jnp.where(wide // hw == i, step_size[:, h : h + 1], out)
        s.stepb[b] = out

    gV.finish()
    s.rawV[:8, :] = jnp.zeros((8, width), F32)
    follow(2)
    s.rawV[8:, :] = dot(full(), s.gV[...].reshape(model, width))
    conv_forward(
        s.rawV, s.kv, s.bv, s.masks, tokens, lambda base, j, x, dx: set_value(s, base, j, x, dx)
    )

    rest(2)
    bc.wait()

    def unpack(rank, ref, col):
        got = s.bc_got[rank].astype(F32)
        for i in range(halves):
            shift = (col - i * sw) % LANES
            piece = pltpu.roll(got, shift, 1) if shift else got
            here = slice(i * fold_rows, (i + 1) * fold_rows)
            ref[here, :] = jnp.where((wide >= col) & (wide < col + sw), piece, ref[here, :])

    s.bvec[...] = jnp.zeros_like(s.bvec)
    s.cvec[...] = jnp.zeros_like(s.cvec)
    for rank in range(t_size):
        unpack(rank, s.bvec if rank * sw < part else s.cvec, rank * sw % part)
    s.bh[...] = s.bvec[...].astype(BF16)
    s.ch[...] = s.cvec[...].astype(BF16)
    for r in range(blocks):
        c0, c1 = band(r)
        s.scores[cut(r), c0 * LANES : c1 * LANES] = dot(
            s.ch[cut(r), :], s.bh[c0 * LANES : c1 * LANES, :], 1, 1
        )

    def serve(first, last, b, events):
        count = last - first
        loop(first + count * b // tiles, first + count * (b + 1) // tiles, events)

    def forward(b):
        fed = (s.x[b] * s.stepb[b]).astype(BF16)
        s.fed[b] = fed
        mine = [jnp.where(wide // hw == i, fed, jnp.zeros_like(fed)) for i in range(per)]
        for r in range(blocks):
            c0, c1 = band(r)
            cols = slice(c0 * LANES, c1 * LANES)
            y = jnp.zeros((LANES, LANES), F32)
            for i in range(per):
                h = b * per + i
                col = s.cumb[h, cut(r), :]
                for q in range(c0, c1):
                    row = s.cumr[h, 0:1, cut(q)]
                    decay = jnp.exp2((col - row) + s.mask[cut(r), cut(q)])
                    s.decay[h, r, :, cut(q - c0)] = decay
                    s.mix[h, cut(r), cut(q)] = (s.scores[cut(r), cut(q)] * decay).astype(BF16)
                y = y + dot(s.mix[h, cut(r), cols], mine[i][cols])
            s.core[b, cut(r), :] = y
            s.y[b, cut(r), :] = y + s.skips[b, 0:1, :] * s.x[b, cut(r), :]
        serve(1, min(3, line), b, gO.step)

    loop(0, tiles, forward)
    gG.finish()
    s.gate[:tokens, :] = dot(full(), s.gG[...].reshape(model, width))
    loop(min(3, line), line, gO.step)
    gc.pass_on()

    def squares(i):
        base = pl.multiple_of(i * CHUNK, CHUNK)
        at = pl.ds(base, CHUNK)
        square = jnp.zeros((CHUNK, LANES), F32)
        for j in range(tiles):
            gate = s.gate[at, cut(j)]
            gated = s.y[j, at, :] * (gate * jax.nn.sigmoid(gate))
            s.gated[at, cut(j)] = gated
            square += gated * gated
        s.sums[at, :] = jnp.broadcast_to(jnp.sum(square, axis=1, keepdims=True), square.shape)

    loop(0, chunks, squares)
    s.sm_own[...] = s.sums[...].T[:8]
    ga.drain()
    sm.open()
    s.aT[...] = s.ga[...].reshape(tokens, model).astype(F32).T.astype(BF16)
    gc.finish()
    s.cT[...] = s.gc[...].reshape(tokens, model).astype(F32).T.astype(BF16)

    def columns(total):
        return jnp.broadcast_to(total[0:1], (LANES, tokens)).T

    s.inv_rms[...] = lax.rsqrt(columns(sm.total()) / inner + epsilon)

    def norm(i):
        base = pl.multiple_of(i * CHUNK, CHUNK)
        at = pl.ds(base, CHUNK)
        inv_rms = s.inv_rms[at, :]
        for j in range(tiles):
            unit = s.gated[at, cut(j)] * inv_rms
            s.gn[at, cut(j)] = (unit * s.gate_gain[:, cut(j)]).astype(BF16)

    loop(0, chunks, norm)

    def turns(group, begin, end):
        for r in group:
            loop(begin, end, r.turn)

    def weight_grad(left, right, ref):
        size = max(rows, 256)
        for i in range(model // size):
            out = dot(left[i * size : (i + 1) * size, :], right)
            ref[i * size // rows : (i + 1) * size // rows] = out.astype(BF16).reshape(
                size // rows, rows, out.shape[1]
            )

    weight_grad(s.cT, s.gn[...], s.wO)
    for r in rO:
        r.open()
    gO.finish()
    s.ggn[...] = dot(s.gc[...].reshape(tokens, model), s.gO[...].reshape(model, width))

    def inners(i):
        base = pl.multiple_of(i * CHUNK, CHUNK)
        at = pl.ds(base, CHUNK)
        inner_dot = jnp.zeros((CHUNK, LANES), F32)
        for j in range(tiles):
            scaled = s.ggn[at, cut(j)] * s.gate_gain[:, cut(j)]
            inner_dot += scaled * s.gated[at, cut(j)]
        s.sums[at, :] = jnp.broadcast_to(
            jnp.sum(inner_dot, axis=1, keepdims=True), inner_dot.shape
        )

    loop(0, chunks, inners)
    s.sn_own[...] = s.sums[...].T[:8]
    gc.drain()
    sn.open()
    s.gg_sum[...] = jnp.zeros_like(s.gg_sum)
    for r in range(t_size):
        s.gc[r] = dot(
            s.gn[r * own_rows : (r + 1) * own_rows, :], s.gO[...].reshape(model, width), 1, 1
        ).astype(BF16)
    s.sums[...] = columns(sn.total())
    sl.open()

    def gated_norm(i):
        base = pl.multiple_of(i * CHUNK, CHUNK)
        at = pl.ds(base, CHUNK)
        inv_rms = s.inv_rms[at, :]
        coef = inv_rms * inv_rms * inv_rms * (s.sums[at, :] / inner)
        for j in range(tiles):
            gate = s.gate[at, cut(j)]
            sig = jax.nn.sigmoid(gate)
            act = gate * sig
            gated = s.gated[at, cut(j)]
            grad = s.ggn[at, cut(j)]
            s.gg_sum[:, cut(j)] += fold(grad * (gated * inv_rms))
            d_gated = inv_rms * (grad * s.gate_gain[:, cut(j)]) - gated * coef
            mixed = s.y[j, at, :]
            s.y[j, at, :] = d_gated * act
            s.gpG[at, cut(j)] = (d_gated * mixed * (sig + act * (1.0 - sig))).astype(BF16)

    turns(rO, 1, 2)
    loop(0, chunks, gated_norm)

    weight_grad(s.aT, s.gpG[...], s.wG)
    for r in rG:
        r.open()
    turns(rO, 2, min(3, line))

    s.dS[...] = jnp.zeros_like(s.dS)
    s.dskip[...] = jnp.zeros_like(s.dskip)

    def o_turn(j):
        for r in rO:
            r.turn(j)

    def backward(b):
        fed = s.fed[b]
        half = s.y[b].astype(BF16)
        mine = [jnp.where(wide // hw == i, half, jnp.zeros_like(half)) for i in range(per)]
        for r in range(blocks):
            c0, c1 = band(r)
            cols = slice(c0 * LANES, c1 * LANES)
            acc = s.dS[cut(r), cols]
            for i in range(per):
                h = b * per + i
                d_mix = dot(mine[i][cut(r)], fed[cols], 1, 1)
                acc = acc + d_mix * s.decay[h, r, :, : (c1 - c0) * LANES]
            s.dS[cut(r), cols] = acc
        for q in range(blocks):
            r1 = min(blocks, q + reach + 1)
            down = slice(q * LANES, r1 * LANES)
            d_fed = jnp.zeros((LANES, LANES), F32)
            for i in range(per):
                d_fed = d_fed + dot(s.mix[b * per + i, down, cut(q)], mine[i][down], 0, 0)
            x = s.x[b, cut(q), :]
            dy = s.y[b, cut(q), :]
            s.core[b, cut(q), :] = (
                half[cut(q)].astype(F32) * s.core[b, cut(q), :] - fed[cut(q)].astype(F32) * d_fed
            )
            s.dskip[b] += fold(dy * x)
            d_x = d_fed * s.stepb[b, cut(q), :] + s.skips[b, 0:1, :] * dy
            s.x[b, cut(q), :] = d_fed * x
            lanes = pl.ds(pl.multiple_of(b * LANES, LANES), LANES)
            s.gate[cut(q), lanes] = d_x * s.dsil[b, cut(q), :]
        serve(min(3, line), line, b, o_turn)

    loop(0, tiles, backward)

    grad_scores = s.dS[...].astype(BF16)
    for r in range(blocks):
        c0, c1 = band(r)
        cols = slice(c0 * LANES, c1 * LANES)
        s.cvec[cut(r), :] = dot(grad_scores[cut(r), cols], s.bh[cols, :])
        r1 = min(blocks, r + reach + 1)
        down = slice(r * LANES, r1 * LANES)
        s.bvec[cut(r), :] = dot(grad_scores[down, cut(r)], s.ch[down, :], 0, 0)
    for rank in range(t_size):
        ref = s.bvec if rank * sw < part else s.cvec
        col = rank * sw % part
        packed = jnp.zeros((fold_rows, LANES), F32)
        for i in range(halves):
            piece = ref[i * fold_rows : (i + 1) * fold_rows, :]
            shift = (i * sw - col) % LANES
            if shift:
                piece = pltpu.roll(piece, shift, 1)
            packed = jnp.where(wide // sw == i, piece, packed)
        s.db_own[rank] = packed.astype(BF16)
    db.open()

    s.gate[tokens:, :] = jnp.zeros((8, width), F32)

    def put_value(base, j, grad):
        s.gpV[pl.ds(base, CHUNK), cut(j)] = grad.astype(BF16)

    conv_backward(s.gate, s.rawV, s.kv, s.masks, s.sumV, tokens, put_value)
    gO.drain()
    weight_grad(s.aT, s.gpV[...], s.gO)
    for r in rV:
        r.open()
    turns(rG, 1, line)

    head_sum = jnp.zeros((2 * tokens, LANES), F32)
    lane_in = lax.broadcasted_iota(jnp.int32, (LANES, LANES), 0)
    lane_out = lax.broadcasted_iota(jnp.int32, (LANES, LANES), 1)
    skip_sum = jnp.zeros((8, LANES), F32)
    for b in range(tiles):
        to_head = jnp.where(lane_out == sw + b * per + lane_in // hw, 1.0, 0.0)
        both = jnp.concatenate([s.core[b], s.x[b]], axis=0)
        head_sum = head_sum + dot(both, to_head, precision=precise)
        skip_sum = skip_sum + dot(s.dskip[b], to_head, precision=precise)
    d_keep = dot(s.upper[...], jnp.concatenate(three(head_sum[:tokens]), axis=1))
    d_keep = d_keep[:, :LANES] + d_keep[:, LANES : 2 * LANES] + d_keep[:, 2 * LANES :]
    grad_step = (head_sum[tokens:] + d_keep * rate) * s.sig_step[...]
    grad_step = jnp.where(is_step, grad_step, 0.0)
    s.ed_own[taps + 2 : taps + 3, 0:LANES] = jnp.sum(grad_step, axis=0, keepdims=True)
    s.ed_own[taps + 2 : taps + 3, LANES : 2 * LANES] = jnp.sum(
        d_keep * s.keep[...], axis=0, keepdims=True
    )
    s.ed_own[taps + 2 : taps + 3, 2 * LANES : 3 * LANES] = jnp.sum(
        skip_sum, axis=0, keepdims=True
    )

    got = db.total()
    s.dpreS[tokens:, :] = jnp.zeros((8, LANES), F32)
    for i in range(halves):
        piece = pltpu.roll(got, (LANES - i * sw) % LANES, 1) if i else got
        here = slice(i * fold_rows, (i + 1) * fold_rows)
        s.dpreS[here, :] = jnp.where(wide < sw, piece * s.dsilS[here, :], 0.0)

    def put_state(base, j, grad):
        s.gradS[pl.ds(base, CHUNK), :] = grad

    conv_backward(s.dpreS, s.rawS, s.ks_own, s.masks, s.sumS, tokens, put_state)
    s.gpS[...] = jnp.where(wide < sw, s.gradS[...], grad_step).astype(BF16)
    weight_grad(s.aT, s.gpS[...], s.wS)
    for r in rS:
        r.open()

    s.o_layer[...] = s.res[...] + sl.total()
    s.norm_sum[...] = jnp.zeros_like(s.norm_sum)
    for k in [*range(1, p.chips), 0]:
        chip = lax.rem(p.y + k, p.chips)
        here = pl.ds(pl.multiple_of(chip * 2 * own_rows, 2 * own_rows), 2 * own_rows)
        out = dot(s.gpG[here, :], s.gG[...].reshape(model, width), 1, 1)
        out = out + dot(s.gpV[here, :], s.gV[...].reshape(model, width), 1, 1)
        out = out + dot(s.gpS[here, :], s.gS[...].reshape(model, LANES), 1, 1)
        sg.put(k, out)
        rows_in = s.ga[pl.ds(chip * 2, 2)].reshape(2 * own_rows, model).astype(F32)
        s.norm_sum[...] += fold(out * rows_in)
    sg.pass_on()
    s.en_own[...] = jnp.sum(s.norm_sum[...], axis=0, keepdims=True) / s.norm_gain[...]
    en.open()

    for k in range(taps):
        s.ed_own[k : k + 1, :] = jnp.sum(s.sumV[k], axis=0, keepdims=True)
        s.ed_own[taps + 3 : taps + 4, cut(k)] = jnp.sum(s.sumS[k], axis=0, keepdims=True)
    s.ed_own[taps : taps + 1, :] = jnp.sum(s.sumV[taps], axis=0, keepdims=True)
    s.ed_own[taps + 1 : taps + 2, :] = jnp.sum(s.gg_sum[...], axis=0, keepdims=True)
    s.ed_own[taps + 2 : taps + 3, 3 * LANES : 4 * LANES] = jnp.sum(
        s.sumS[taps], axis=0, keepdims=True
    )
    ed.open()

    turns(rV, 1, line)
    turns(rS, 1, line)
    s.tn_own[...] = en.total()
    tn.open()
    small = ed.total()
    s.o_small[...] = small
    for k in range(taps):
        s.ts_own[k : k + 1, :] = small[taps + 3 : taps + 4, cut(k)]
    s.ts_own[taps : taps + 1, :] = small[taps + 2 : taps + 3, 3 * LANES : 4 * LANES]
    s.ts_own[taps + 1 :, :] = jnp.zeros((8 - taps - 1, LANES), F32)
    ts.open()
    for r in rO:
        r.settle(s.o_proj)
    for r in rG:
        r.settle(s.o_gate)

    g_sum = sg.total()
    res = s.res[...]
    inv = lax.rsqrt(jnp.mean(res * res, axis=1, keepdims=True) + epsilon)
    unit = res * inv
    scaled = g_sum * s.norm_gain[...]
    mean = jnp.mean(scaled * unit, axis=1, keepdims=True)
    s.o_input[...] = s.cot[...] + inv * (scaled - unit * mean)

    ts.wait()
    s.ts_got[p.t] = s.ts_own[...]
    for rank in range(t_size):
        piece = s.ts_got[rank]
        whole_at = rank * sw // LANES * LANES
        shift = rank * sw % LANES
        if shift:
            piece = pltpu.roll(piece, shift, 1)
        at = slice(whole_at, whole_at + LANES)
        inside = (wide >= shift) & (wide < shift + sw)
        base = jnp.zeros_like(piece) if shift == 0 else s.o_taps[:, at]
        s.o_taps[:, at] = jnp.where(inside, piece, base)
    s.o_norm[...] = tn.total()
    for r in rV:
        r.settle(s.o_value)
    for r in rS:
        r.settle(s.o_state)

    sg.drain()
    for thing in [gS, gV, gG] + rO + rG + rV + rS:
        thing.drain()


def set_state(s, base, x, dx):
    s.xS[pl.ds(base, CHUNK), :] = x
    s.dsilS[pl.ds(base, CHUNK), :] = dx


def set_value(s, base, j, x, dx):
    s.x[j, pl.ds(base, CHUNK), :] = x
    s.dsil[j, pl.ds(base, CHUNK), :] = dx


def finish_kernel(
    sw,
    heads,
    taps,
    layer,
    inp,
    norm,
    gate,
    value,
    state,
    proj,
    small,
    state_taps,
    layer_out,
    input_out,
    norm_out,
    gate_out,
    value_out,
    step_out,
    state_out,
    kv_out,
    bv_out,
    ks_out,
    bs_out,
    sb_out,
    ld_out,
    sk_out,
    gg_out,
    proj_out,
):
    layer_out[...] = layer[...]
    input_out[...] = inp[...]
    norm_out[...] = norm[...]
    gate_out[...] = gate[...]
    value_out[...] = value[...]
    proj_out[...] = proj[...]
    turned = state[...].T
    state_out[...] = turned[:sw]
    step_out[...] = turned[sw : sw + heads]
    kv_out[...] = small[:taps]
    bv_out[...] = small[taps : taps + 1]
    gg_out[...] = small[taps + 1 : taps + 2]
    for i, ref in enumerate((sb_out, ld_out, sk_out)):
        row = small[taps + 2 : taps + 3, i * LANES : (i + 1) * LANES]
        ref[...] = row[:, sw : sw + heads]
    ks_out[...] = state_taps[:taps]
    bs_out[...] = state_taps[taps : taps + 1]


def local(
    n,
    t_size,
    residual,
    segments,
    norm_gain,
    in_gate,
    in_value,
    in_step,
    in_state,
    kernel_value,
    bias_value,
    kernel_state,
    bias_state,
    step_bias,
    log_decay,
    skip_gain,
    gate_gain,
    out_proj,
    cotangent,
):
    tokens = segments.shape[1]
    model = residual.shape[1]
    width = in_gate.shape[1]
    heads = in_step.shape[1]
    states = in_state.shape[1]
    rows = in_gate.shape[0]
    taps = kernel_value.shape[0]
    own_rows = residual.shape[0]
    sw = states // t_size
    hw = width // heads
    tiles = width // LANES
    line = n // 2
    halves = LANES // sw
    vm = pltpu.VMEM
    dma = pltpu.SemaphoreType.DMA
    struct = jax.ShapeDtypeStruct

    args = dict(
        res=residual,
        seg=segments,
        norm_gain=norm_gain[None],
        gate_w=in_gate,
        value_w=in_value,
        step_w=in_step.T,
        state_w=in_state,
        kv=kernel_value,
        bv=bias_value[None],
        ks=kernel_state,
        bs=bias_state[None],
        step_bias=step_bias[None],
        log_decay=log_decay[None],
        skip=skip_gain[None],
        gate_gain=gate_gain[None],
        out_w=out_proj,
        cot=cotangent,
    )
    outs = dict(
        o_layer=struct(residual.shape, F32),
        o_input=struct(residual.shape, F32),
        o_norm=struct((1, model), F32),
        o_gate=struct((rows, width), F32),
        o_value=struct((rows, width), F32),
        o_state=struct((rows, LANES), F32),
        o_proj=struct((rows, width), F32),
        o_small=struct((8, width), F32),
        o_taps=struct((8, states), F32),
    )
    tok_cols = {
        "ggn": width,
        "pS": LANES,
        "xS": LANES,
        "dsilS": LANES,
        "step": LANES,
        "sig_step": LANES,
        "keep": LANES,
        "bvec": LANES,
        "cvec": LANES,
        "sums": LANES,
        "gradS": LANES,
        "scores": tokens,
        "mask": tokens,
        "dS": tokens,
    }
    half_cols = {
        "bh": LANES,
        "ch": LANES,
        "tri": tokens,
        "upper": tokens,
        "gn": width,
        "gpG": width,
        "gpV": width,
        "gpS": LANES,
    }
    scratch = {k: vm((tokens, cols), F32) for k, cols in tok_cols.items()}
    scratch |= {k: vm((tokens, cols), BF16) for k, cols in half_cols.items()}
    scratch |= {
        k: vm((tiles, tokens, LANES), F32)
        for k in ("x", "dsil", "y", "core", "stepb")
    }
    small_rows = 8
    pieces = 1
    scratch |= dict(
        fed=vm((tiles, tokens, LANES), BF16),
        cumb=vm((heads, tokens, LANES), F32),
        cumr=vm((heads, 8, tokens), F32),
        decay=vm((heads, tokens // LANES, LANES, (-(-(LONGEST - 1) // LANES) + 1) * LANES), F32),
        mix=vm((heads, tokens, tokens), BF16),
        ws=vm((rows, LANES), BF16),
        a_own=vm((own_rows, model), BF16),
        c_own=vm((own_rows, model), BF16),
        ga=vm((t_size, own_rows, model), BF16),
        gc=vm((t_size, own_rows, model), BF16),
        aT=vm((model, tokens), BF16),
        cT=vm((model, tokens), BF16),
        gS=vm((n, rows, LANES), BF16),
        gV=vm((n, rows, width), BF16),
        gG=vm((n, rows, width), BF16),
        gO=vm((n, rows, width), BF16),
        wS=vm((n, rows, LANES), BF16),
        wG=vm((n, rows, width), BF16),
        wO=vm((n, rows, width), BF16),
        masks=vm((taps - 1, tokens + 8, LANES), F32),
        ks_own=vm((taps, LANES), F32),
        bs_own=vm((1, LANES), F32),
        skips=vm((tiles, 8, LANES), F32),
        dskip=vm((tiles, 8, LANES), F32),
        rawS=vm((tokens + 8, LANES), F32),
        rawV=vm((tokens + 8, width), F32),
        gate=vm((tokens + 8, width), F32),
        dpreS=vm((tokens + 8, LANES), F32),
        sumV=vm((taps + 1, 8, width), F32),
        sumS=vm((taps + 1, 8, LANES), F32),
        gg_sum=vm((8, width), F32),
        bc_own=vm((tokens // halves, LANES), BF16),
        bc_got=vm((t_size, tokens // halves, LANES), BF16),
        db_own=vm((t_size, tokens // halves, LANES), BF16),
        db_got=vm((t_size, tokens // halves, LANES), BF16),
        gated=vm((tokens, width), F32),
        inv_rms=vm((tokens, LANES), F32),
        sn_own=vm((8, tokens), F32),
        sn_got=vm((t_size, 8, tokens), F32),
        sm_own=vm((8, tokens), F32),
        sm_got=vm((t_size, 8, tokens), F32),
        l_got=vm((t_size, own_rows, model), BF16),
        norm_sum=vm((8, model), F32),
        g_out=vm((t_size // 2, own_rows, model), BF16),
        g_in=vm((t_size // 2, own_rows, model), BF16),
        g_out2=vm((t_size // 2, own_rows, model), BF16),
        g_in2=vm((t_size // 2, own_rows, model), BF16),
        g_mine=vm((t_size // 2, own_rows, model), F32),
        tn_own=vm((1, model), F32),
        tn_got=vm((t_size, 1, model), F32),
        ts_own=vm((8, LANES), F32),
        ts_got=vm((t_size, 8, LANES), F32),
        en_own=vm((1, model), F32),
        en_got=vm((n, 1, model), F32),
        ed_own=vm((small_rows, width), F32),
        ed_got=vm((n, small_rows, width), F32),
    )
    for g in ("gS", "gV", "gG", "gO"):
        for k in "xudr":
            scratch[g + "_" + k] = dma((1, n))
    for g in ("ga", "gc"):
        for k in ("s", "s2", "r"):
            scratch[g + "_" + k] = dma((t_size,))
    for g in ("bc", "sm", "sn", "db", "l", "tn", "ts"):
        for k in "sr":
            scratch[g + "_" + k] = dma((t_size,))
    for k in ("g_st", "g_qt", "g_sy", "g_qy"):
        scratch[k] = dma((t_size // 2,))
    for g in ("en", "ed"):
        for k in "sr":
            scratch[g + "_" + k] = dma((n,))
    for g in ("rO", "rG", "rV", "rS"):
        cols = LANES if g == "rS" else width
        for k in ("_rx", "_buf", "_got"):
            scratch[g + k] = vm((line, rows, cols), BF16)
        for k in ("_sx", "_qx", "_ss", "_qs"):
            scratch[g + k] = dma((pieces, line))

    names = list(args) + list(outs) + list(scratch)
    conf = SimpleNamespace(
        names=names,
        n=n,
        t_size=t_size,
        tokens=tokens,
        model=model,
        width=width,
        heads=heads,
        states=states,
        rows=rows,
        sw=sw,
        hw=hw,
        pieces=pieces,
    )
    results = pl.pallas_call(
        partial(kernel, conf),
        out_shape=tuple(outs.values()),
        in_specs=[VM] * len(args),
        out_specs=(VM,) * len(outs),
        scratch_shapes=list(scratch.values()),
        compiler_params=pltpu.CompilerParams(
            collective_id=0, has_side_effects=True, vmem_limit_bytes=VMEM_BYTES
        ),
    )(*args.values())
    finals = (
        struct(residual.shape, F32),
        struct(residual.shape, F32),
        struct((1, model), F32),
        struct((rows, width), F32),
        struct((rows, width), F32),
        struct((heads, rows), F32),
        struct((sw, rows), F32),
        struct((taps, width), F32),
        struct((1, width), F32),
        struct((taps, states), F32),
        struct((1, states), F32),
        struct((1, heads), F32),
        struct((1, heads), F32),
        struct((1, heads), F32),
        struct((1, width), F32),
        struct((rows, width), F32),
    )
    out = pl.pallas_call(
        partial(finish_kernel, sw, heads, taps),
        out_shape=finals,
        in_specs=[VM] * len(results),
        out_specs=(VM,) * len(finals),
    )(*results)
    out = list(out)
    out[5], out[6] = out[5].T, out[6].T
    for i in (2, 8, 10, 11, 12, 13, 14):
        out[i] = out[i][0]
    return tuple(out)


def solution(mesh):
    in_specs = (
        P(("dp", "tensor"), None),
        P("dp", None),
        P(),
        P("dp", "tensor"),
        P("dp", "tensor"),
        P("dp", "tensor"),
        P("dp", None),
        P(None, "tensor"),
        P("tensor"),
        P(),
        P(),
        P("tensor"),
        P("tensor"),
        P("tensor"),
        P("tensor"),
        P("dp", "tensor"),
        P(("dp", "tensor"), None),
    )
    out_specs = (
        P(("dp", "tensor"), None),
        P(("dp", "tensor"), None),
        P(),
        P("dp", "tensor"),
        P("dp", "tensor"),
        P("dp", "tensor"),
        P("dp", "tensor"),
        P(None, "tensor"),
        P("tensor"),
        P(),
        P(),
        P("tensor"),
        P("tensor"),
        P("tensor"),
        P("tensor"),
        P("dp", "tensor"),
    )
    body = partial(local, mesh.shape["dp"], mesh.shape["tensor"])
    return jax.shard_map(body, mesh=mesh, in_specs=in_specs, out_specs=out_specs, check_vma=False)
```
